128 devices in a mesh: sensor: 8 (over x, z_lo), chan: 16 (over z_hi, y, core).
Axes of the slice: x: 4, y: 4, z: 4 (z_hi: 2, z_lo: 2; z = z_hi * 2 + z_lo), core: 2. Of those that a mesh axis runs over, the one named last changes fastest.
Arguments:
- samples: float32 [2, 128, 512, 128], P(None, 'sensor', 'chan'), may hold values from -6 to 6
- bins: int32 [64], replicated, may hold values from 1 to 511
- offsets: int32 [64], replicated, may hold values from 0 to 7
Outputs:
- gram: float32 [64, 2, 128, 128], P('chan', None, 'sensor')
The draws below stay inside these ranges and needn't reach their ends.
All inputs are finite; a program needn't handle non-finite values.
Results may differ from the reference program's by a relative error of at most 0.00009.
Values sent between devices are 32-bit elements; how exact they have to be, the bound alone decides.
A program may use at most 64 MiB of HBM per device.

```python
import math
import jax
import jax.numpy as jnp
from jax import lax

SENSORS = 128
CHANNELS = 128
BLOCKS = 512
ALPHAS = 64
CH_DEV = 8


def plant(values, key, smallest, top_value):
    shape = values.shape
    place = [jax.random.randint(jax.random.fold_in(key, axis), (), 0, shape[axis]) for axis in range(len(shape))]
    values = values.at[tuple(place)].set(smallest)
    longest = shape.index(max(shape))
    place[longest] = (place[longest] + 1) % shape[longest]
    return values.at[tuple(place)].set(top_value)


def shard_levels(rng, dims, split, smallest, largest):
    gain, own = 1.0, jax.random.fold_in(rng, 6)
    for position, blocks in split:
        heights = jnp.exp(jax.random.uniform(jax.random.fold_in(own, position), (blocks,), jnp.float32, smallest / len(split), largest / len(split)))
        gain = gain * jnp.repeat(heights, dims[position] // blocks).reshape([-1 if axis == position else 1 for axis in range(len(dims))])
    return gain


def scatter_about(own_key, shape, deviation, limit, shards=(), kind=jnp.bfloat16):
    level = shard_levels(own_key, shape, shards, -0.22, 0.18) if shards else 1.0
    array = jax.random.normal(own_key, shape, jnp.float32) * deviation * level
    return jnp.minimum(jnp.maximum(array, -limit), limit).astype(kind)


def setup_inputs(seed: int = 0) -> dict:
    seeds = jax.random.split(jax.random.key(seed), 4)
    return {
        "samples": scatter_about(seeds[0], (2, SENSORS, BLOCKS, CHANNELS), 1.0, 6.0, ((1, 8), (2, 16)), jnp.float32),
        "bins": plant(jax.random.randint(seeds[1], (ALPHAS,), 1, BLOCKS), jax.random.fold_in(seeds[1], 1), 1, BLOCKS - 1).astype(jnp.int32),
        "offsets": plant(jax.random.randint(seeds[2], (ALPHAS,), 0, CH_DEV), jax.random.fold_in(seeds[2], 1), 0, CH_DEV - 1).astype(jnp.int32),
    }


power_floor = 0.1

def reference(samples, bins, offsets):
    channel_count = samples.shape[3]
    length = samples.shape[2]
    positions = jnp.arange(channel_count, dtype=jnp.float32)
    window = 0.5 - 0.5 * jnp.cos(positions * (2.0 * math.pi / channel_count))
    signal = samples[0] * window + 1j * (samples[1] * window)
    demodulates = jnp.fft.fft(signal, axis=2) / math.sqrt(channel_count)
    spectra = jnp.fft.fft(demodulates, axis=1) / math.sqrt(length)
    power = jnp.real(spectra) * jnp.real(spectra) + jnp.imag(spectra) * jnp.imag(spectra)
    spectra = spectra / jnp.sqrt(power + power_floor)
    spectra = jnp.transpose(spectra, (0, 2, 1))
    sensors_all = spectra.shape[0]
    flattened = spectra.reshape(sensors_all, -1)
    factor = 1.0 / math.sqrt(channel_count * length)

    def one_alpha(inputs_pair):
        cycle_bin, offset = inputs_pair
        shifted = jnp.roll(spectra, (offset, -cycle_bin), axis=(1, 2)).reshape(sensors_all, -1)
        product = jnp.matmul(shifted, jnp.conj(flattened).T, precision=lax.Precision.HIGHEST) * factor
        return jnp.stack([jnp.real(product), jnp.imag(product)])
    return lax.map(one_alpha, (bins, offsets))
```

```python
import math

import jax
import jax.numpy as jnp
import ml_dtypes
import numpy as np
from jax import lax
from jax.experimental import pallas as pl
from jax.experimental.pallas import tpu as pltpu
from jax.sharding import Mesh
from jax.sharding import PartitionSpec as P

CHANNELS = 128
BLOCKS = 512
ALPHAS = 64
SHIFTS = 8
FLOOR = 0.1
F32 = jnp.float32
BF16 = jnp.bfloat16
VMEM = pl.BlockSpec(memory_space=pltpu.VMEM)
LIMIT = pltpu.CompilerParams(vmem_limit_bytes=48 * 2**20)


def halves(table):
    high = table.astype(ml_dtypes.bfloat16)
    low = (table - high.astype(np.float64)).astype(ml_dtypes.bfloat16)
    return high, low


def channel_table():
    n = np.arange(CHANNELS)
    window = 0.5 - 0.5 * np.cos(2 * np.pi * n / CHANNELS)
    angle = 2 * np.pi * (n[:, None] * n[None, :] % CHANNELS) / CHANNELS
    cosine = window[:, None] * np.cos(angle) / math.sqrt(CHANNELS)
    sine = window[:, None] * np.sin(angle) / math.sqrt(CHANNELS)
    return np.block([[cosine, -sine], [sine, cosine]])


def block_table():
    n = np.arange(BLOCKS)
    angle = 2 * np.pi * (n[:, None] * n[None, :] % BLOCKS) / BLOCKS
    return np.concatenate([np.cos(angle), np.sin(angle)], 0) / math.sqrt(BLOCKS)


def split(x):
    high = x.astype(BF16)
    return high, (x - high.astype(F32)).astype(BF16)


def dot3(a, b, dims):
    def one(u, v):
        return lax.dot_general(u, v, (dims, ((), ())), preferred_element_type=F32)

    return one(a[0], b[0]) + (one(a[0], b[1]) + one(a[1], b[0]))


def lane_block(shape, width):
    return lax.broadcasted_iota(jnp.int32, shape, len(shape) - 1) // width % 2


def swap_blocks(tiles):
    tiles = list(tiles)
    for bit in (1, 2, 4, 8):
        width = 8 * bit
        upper = lane_block(tiles[0].shape, width) == 1
        for i in range(16):
            if i & bit:
                continue
            a, b = tiles[i], tiles[i | bit]
            axis = a.ndim - 1
            tiles[i] = jnp.where(upper, pltpu.roll(b, width, axis), a)
            tiles[i | bit] = jnp.where(upper, b, pltpu.roll(a, 128 - width, axis))
    return tiles


def demod_kernel(x_ref, high_ref, low_ref, out_ref, mid_ref):
    sensors, blocks = x_ref.shape[1], x_ref.shape[2]
    rows = sensors * blocks
    x = jnp.concatenate([x_ref[0].reshape(rows, 128), x_ref[1].reshape(rows, 128)], 1)
    mid_ref[...] = dot3(split(x), (high_ref[...], low_ref[...]), ((1,), (0,)))
    for part in range(2):
        for m in range(0, blocks, 8):
            tiles = [
                mid_ref[s * blocks + m : s * blocks + m + 8, part * 128 : part * 128 + 128]
                for s in range(sensors)
            ]
            for dest, tile in enumerate(swap_blocks(tiles)):
                out_ref[dest, part, m : m + 8, :] = tile


def white_kernel(d_ref, high_ref, low_ref, out_ref):
    parts = [d_ref[:, part].reshape(BLOCKS, 128) for part in range(2)]
    table = (high_ref[...], low_ref[...])
    u = dot3(table, split(jnp.concatenate(parts, 1)), ((1,), (0,)))
    real = u[:BLOCKS, :128] + u[BLOCKS:, 128:]
    imag = u[:BLOCKS, 128:] - u[BLOCKS:, :128]
    scale = 1.0 / jnp.sqrt(real * real + imag * imag + FLOOR)
    u = dot3(table, split(jnp.concatenate([real * scale, imag * scale], 1)), ((1,), (0,)))
    out_ref[:, 0] = (u[:BLOCKS, :128] - u[BLOCKS:, 128:]).reshape(16, 32, 128)
    out_ref[:, 1] = (u[:BLOCKS, 128:] + u[BLOCKS:, :128]).reshape(16, 32, 128)


def turn_kernel(r_ref, out_ref):
    for part in range(2):
        for m in range(0, 32, 8):
            tiles = [r_ref[i, part, m : m + 8, :] for i in range(16)]
            for s, tile in enumerate(swap_blocks(tiles)):
                out_ref[s, part, m : m + 8, :] = tile


def gram_kernel(a_ref, b_ref, ehigh_ref, elow_ref, out_ref, p_ref):
    def one_block(m, carry):
        left = []
        for part in range(2):
            rows = []
            for a in range(32):
                row = a_ref[pl.ds(a * 64 + part * 32 + m, 1), :]
                tile = jnp.broadcast_to(row, (8, 128))
                rows.append(pltpu.roll(tile, 0, 1, stride=1, stride_axis=0))
            left.append(jnp.concatenate(rows, 0))
        left = split(jnp.concatenate(left, 1))
        real = b_ref[pl.ds(m, 64, stride=64), :]
        imag = b_ref[pl.ds(32 + m, 64, stride=64), :]
        upper = jnp.concatenate([real, imag], 1)
        under = jnp.concatenate([-imag, real], 1)
        rows = []
        for x in range(4):
            rows += [upper[x * 16 : x * 16 + 16], under[x * 16 : x * 16 + 16]]
        right = split(jnp.concatenate(rows, 0))
        product = dot3(left, right, ((1,), (1,)))
        p_ref[:, pl.ds(pl.multiple_of(m * 8, 8), 8), :] = product.reshape(32, 8, 128)
        return carry

    lax.fori_loop(0, 32, one_block, 0)
    table = (ehigh_ref[...], elow_ref[...])

    def one_sensor(a, carry):
        t = dot3(table, split(p_ref[a]), ((1,), (0,)))
        cosine, sine = t[:64], t[64:]
        odd = lane_block(sine.shape, 16) == 1
        g = cosine + jnp.where(odd, -pltpu.roll(sine, 16, 1), pltpu.roll(sine, 112, 1))
        for dest in range(16):
            out_ref[dest, a] = g[dest * 4 : dest * 4 + 4]
        return carry

    lax.fori_loop(0, 32, one_sensor, 0)


def call(kernel, out_shape, scratch=()):
    return pl.pallas_call(
        kernel,
        out_shape=jax.ShapeDtypeStruct(out_shape, F32),
        out_specs=VMEM,
        scratch_shapes=list(scratch),
        compiler_params=LIMIT,
    )


def phases(bins, offsets, first):
    m = first + jnp.arange(32, dtype=jnp.int32)
    angle = (bins[:, None] * m[None, :] % BLOCKS).astype(F32) * (2.0 * math.pi / BLOCKS)
    both = jnp.stack([jnp.cos(angle), jnp.sin(angle)]) * (1.0 / 256.0)
    chosen = offsets[:, None] == jnp.arange(SHIFTS, dtype=jnp.int32)[None, :]
    table = jnp.where(chosen[None, :, None, :], both[:, :, :, None], 0.0)
    table = table.reshape(2 * ALPHAS, 32 * SHIFTS)
    high = lax.reduce_precision(table, 8, 7)
    return high.astype(BF16), (table - high).astype(BF16)


def on_device(samples, bins, offsets):
    chan = lax.axis_index("chan")
    wide = lax.axis_index("z")
    e_high, e_low = phases(bins, offsets, chan * 32)
    chunk = (16, 2, 32, 128)
    demod = call(demod_kernel, chunk, [pltpu.VMEM((512, 256), F32)])(
        samples, *halves(channel_table())
    )
    received = lax.all_to_all(demod, "chan", 0, 0, tiled=True)
    white = call(white_kernel, chunk)(received, *halves(block_table()))
    received = lax.all_to_all(white, "chan", 0, 0, tiled=True)
    own = call(turn_kernel, chunk)(received)
    other = lax.ppermute(own, "z", [(0, 1), (1, 0)])
    first = wide == 0
    left = jnp.concatenate([jnp.where(first, own, other), jnp.where(first, other, own)], 0)
    right = lax.all_gather(own, "x", axis=0, tiled=True)
    part = call(gram_kernel, (16, 32, 4, 128), [pltpu.VMEM((32, 256, 128), F32)])(
        left.reshape(-1, 128), right.reshape(-1, 128), e_high, e_low
    )
    part = jnp.sum(lax.all_to_all(part[:, None], "chan", 0, 0, tiled=True), axis=0)
    part = part.reshape(2, 16, 4, 128)
    mine = jnp.where(first, part[0], part[1])
    theirs = lax.ppermute(jnp.where(first, part[1], part[0]), "z", [(0, 1), (1, 0)])
    low = jnp.where(first, mine, theirs).reshape(16, 4, 4, 2, 16)
    high = jnp.where(first, theirs, mine).reshape(16, 4, 4, 2, 16)
    both = jnp.stack([low, high], 4)
    return jnp.transpose(both, (1, 3, 0, 2, 4, 5)).reshape(4, 2, 16, 128)


def solution(mesh):
    finer = Mesh(mesh.devices.reshape(4, 2, mesh.shape["chan"]), ("x", "z", "chan"))
    sensor = ("x", "z")
    return jax.shard_map(
        on_device,
        mesh=finer,
        in_specs=(P(None, sensor, "chan", None), P(), P()),
        out_specs=P("chan", None, sensor, None),
        check_vma=False,
    )
```

```python
import math

import jax
import jax.numpy as jnp
import ml_dtypes
import numpy as np
from jax import lax
from jax.experimental import pallas as pl
from jax.experimental.pallas import tpu as pltpu
from jax.sharding import Mesh
from jax.sharding import PartitionSpec as P

CHANNELS = 128
BLOCKS = 512
ALPHAS = 64
SHIFTS = 8
FLOOR = 0.1
F32 = jnp.float32
BF16 = jnp.bfloat16
VMEM = pl.BlockSpec(memory_space=pltpu.VMEM)


def halves(table):
    high = table.astype(ml_dtypes.bfloat16)
    low = (table - high.astype(np.float64)).astype(ml_dtypes.bfloat16)
    return high, low


def channel_table():
    n = np.arange(CHANNELS)
    window = 0.5 - 0.5 * np.cos(2 * np.pi * n / CHANNELS)
    angle = 2 * np.pi * (n[:, None] * n[None, :] % CHANNELS) / CHANNELS
    cosine = window[:, None] * np.cos(angle) / math.sqrt(CHANNELS)
    sine = window[:, None] * np.sin(angle) / math.sqrt(CHANNELS)
    return np.block([[cosine, -sine], [sine, cosine]])


def block_table():
    n = np.arange(BLOCKS).reshape(16, 4, 8).transpose(1, 0, 2).reshape(-1)
    angle = 2 * np.pi * (n[:, None] * n[None, :] % BLOCKS) / BLOCKS
    return np.concatenate([np.cos(angle), np.sin(angle)], 0) / math.sqrt(BLOCKS)


def split(x):
    high = x.astype(BF16)
    return high, (x - high.astype(F32)).astype(BF16)


def dot3(a, b, dims):
    def one(u, v):
        return lax.dot_general(u, v, (dims, ((), ())), preferred_element_type=F32)

    return one(a[0], b[0]) + (one(a[0], b[1]) + one(a[1], b[0]))


def lane_block(shape, width):
    return lax.broadcasted_iota(jnp.int32, shape, len(shape) - 1) // width % 2


def swap_blocks(tiles):
    tiles = list(tiles)
    for bit in (1, 2, 4, 8):
        width = 8 * bit
        upper = lane_block(tiles[0].shape, width) == 1
        for i in range(16):
            if i & bit:
                continue
            a, b = tiles[i], tiles[i | bit]
            axis = a.ndim - 1
            tiles[i] = jnp.where(upper, pltpu.roll(b, width, axis), a)
            tiles[i | bit] = jnp.where(upper, b, pltpu.roll(a, 128 - width, axis))
    return tiles


def fill(copies, start=True):
    for copy in copies:
        copy.start() if start else copy.wait()


def remote(src, dst, send, recv, **where):
    return pltpu.make_async_remote_copy(
        src_ref=src,
        dst_ref=dst,
        send_sem=send,
        recv_sem=recv,
        device_id=where,
        device_id_type=pl.DeviceIdType.MESH,
    )


def greet(peers):
    barrier = pltpu.get_barrier_semaphore()
    for where in peers:
        pl.semaphore_signal(barrier, device_id=where, device_id_type=pl.DeviceIdType.MESH)
    return lambda: pl.semaphore_wait(barrier, len(peers))


def front_kernel(
    x_ref, chigh_ref, clow_ref, thigh_hbm, tlow_hbm, right_ref, other_ref,
    mid_ref, made_ref, got_ref, back_ref, land_ref, thigh_ref, tlow_ref,
    table_sem, send1, recv1, send2, recv2, sendx, recvx, sendf, recvf, sendz, recvz,
):
    chan, x, z = lax.axis_index("chan"), lax.axis_index("x"), lax.axis_index("z")
    after, before = lax.rem(x + 1, 4), lax.rem(x + 3, 4)
    peers = [lax.rem(chan + o, 16) for o in range(1, 16)]
    arrived = greet(
        [{"chan": c} for c in peers] + [{"x": after}, {"x": before}, {"z": 1 - z}]
    )
    tables = [
        pltpu.make_async_copy(thigh_hbm, thigh_ref, table_sem.at[0]),
        pltpu.make_async_copy(tlow_hbm, tlow_ref, table_sem.at[1]),
    ]
    fill(tables)
    part = jnp.concatenate([x_ref[0].reshape(512, 128), x_ref[1].reshape(512, 128)], 1)
    mid_ref[...] = dot3(split(part), (chigh_ref[...], clow_ref[...]), ((1,), (0,)))
    for c in range(2):
        for mc in range(4):
            tiles = [
                mid_ref[s * 32 + mc * 8 : s * 32 + mc * 8 + 8, c * 128 : c * 128 + 128]
                for s in range(16)
            ]
            for dest, tile in enumerate(swap_blocks(tiles)):
                made_ref[dest, mc, c] = tile
    arrived()

    def first_out(o):
        peer = lax.rem(chan + o, 16)
        return remote(made_ref.at[peer], got_ref.at[chan], send1.at[o], recv1.at[chan], chan=peer)

    def first_in(o):
        peer = lax.rem(chan + o, 16)
        return remote(made_ref.at[peer], got_ref.at[peer], send1.at[o], recv1.at[peer], chan=peer)

    @pl.loop(1, 16)
    def _(o):
        first_out(o).start()

    got_ref[chan] = made_ref[chan]
    fill(tables, False)

    @pl.loop(1, 16)
    def _(o):
        first_in(o).wait_recv()

    def gathered(c):
        return jnp.concatenate([got_ref[:, mc, c].reshape(128, 128) for mc in range(4)], 0)

    u = dot3(
        (thigh_ref[...], tlow_ref[...]),
        split(jnp.concatenate([gathered(0), gathered(1)], 1)),
        ((1,), (0,)),
    )
    real = u[:BLOCKS, :128] + u[BLOCKS:, 128:]
    imag = u[:BLOCKS, 128:] - u[BLOCKS:, :128]
    scale = 1.0 / jnp.sqrt(real * real + imag * imag + FLOOR)
    white = split(jnp.concatenate([real * scale, imag * scale], 1))

    def second_out(o, mc):
        peer = lax.rem(chan + o, 16)
        return remote(
            back_ref.at[peer, mc], land_ref.at[chan, mc], send2.at[mc, o], recv2.at[mc, chan], chan=peer
        )

    def second_in(o, mc):
        peer = lax.rem(chan + o, 16)
        return remote(
            back_ref.at[peer, mc], land_ref.at[peer, mc], send2.at[mc, o], recv2.at[mc, peer], chan=peer
        )

    for mc in range(4):
        ups = []
        for row in (mc * 128, BLOCKS + mc * 128):
            table = (thigh_ref[row : row + 128, :], tlow_ref[row : row + 128, :])
            ups.append(dot3(table, white, ((1,), (0,))))
        cosine, sine = ups
        back_ref[:, mc, 0] = (cosine[:, :128] - sine[:, 128:]).reshape(16, 8, 128)
        back_ref[:, mc, 1] = (cosine[:, 128:] + sine[:, :128]).reshape(16, 8, 128)

        @pl.loop(1, 16)
        def _(o, mc=mc):
            second_out(o, mc).start()

        land_ref[chan, mc] = back_ref[chan, mc]

    def to_x(mc, way):
        peer = after if way == 0 else before
        return remote(
            right_ref.at[x, mc], right_ref.at[x, mc], sendx.at[way, mc], recvx.at[way, mc], x=peer
        )

    def from_x(mc, way):
        peer = before if way == 0 else after
        return remote(
            right_ref.at[peer, mc], right_ref.at[peer, mc], sendx.at[way, mc], recvx.at[way, mc], x=peer
        )

    def passed(mc):
        source, peer = (before, after) if mc % 2 == 0 else (after, before)
        return remote(
            right_ref.at[source, mc], right_ref.at[source, mc], sendf.at[mc], recvf.at[mc], x=peer
        )

    def passed_in(mc):
        far = lax.rem(x + 2, 4)
        return remote(right_ref.at[far, mc], right_ref.at[far, mc], sendf.at[mc], recvf.at[mc], x=after)

    def to_z(mc):
        return remote(right_ref.at[x, mc], other_ref.at[mc], sendz.at[mc], recvz.at[mc], z=1 - z)

    for mc in range(4):

        @pl.loop(1, 16)
        def _(o, mc=mc):
            second_in(o, mc).wait_recv()

        for c in range(2):
            tiles = [land_ref[i, mc, c] for i in range(16)]
            for s, tile in enumerate(swap_blocks(tiles)):
                right_ref[x, mc, s, c] = tile
        to_x(mc, 0).start()
        to_x(mc, 1).start()
        to_z(mc).start()
    for mc in range(4):
        from_x(mc, mc % 2).wait_recv()
        passed(mc).start()
    for mc in range(4):
        from_x(mc, 1 - mc % 2).wait_recv()
        to_z(mc).wait_recv()
        passed_in(mc).wait_recv()

    @pl.loop(1, 16)
    def _(o):
        first_out(o).wait_send()
        for mc in range(4):
            second_out(o, mc).wait_send()

    for mc in range(4):
        to_x(mc, 0).wait_send()
        to_x(mc, 1).wait_send()
        to_z(mc).wait_send()
        passed(mc).wait_send()


def gram_kernel(right_ref, other_ref, ehigh_ref, elow_ref, out_ref, p_ref):
    own = lax.axis_index("x") * 1024

    def one_block(m, carry):
        at = m // 8 * 256 + m % 8
        left = []
        for part in range(2):
            rows = []
            for a in range(32):
                start = at + a % 16 * 16 + part * 8
                ref, start = (right_ref, start + own) if a < 16 else (other_ref, start)
                tile = jnp.broadcast_to(ref[pl.ds(start, 1), :], (8, 128))
                rows.append(pltpu.roll(tile, 0, 1, stride=1, stride_axis=0))
            left.append(jnp.concatenate(rows, 0))
        left = split(jnp.concatenate(left, 1))
        rows = []
        for x in range(4):
            real = right_ref[pl.ds(at + x * 1024, 16, stride=16), :]
            imag = right_ref[pl.ds(at + x * 1024 + 8, 16, stride=16), :]
            rows.append(jnp.concatenate([real, imag], 1))
            rows.append(jnp.concatenate([-imag, real], 1))
        right = split(jnp.concatenate(rows, 0))
        product = dot3(left, right, ((1,), (1,)))
        p_ref[:, pl.ds(pl.multiple_of(m * 8, 8), 8), :] = product.reshape(32, 8, 128)
        return carry

    lax.fori_loop(0, 32, one_block, 0, unroll=2)
    table = (ehigh_ref[...], elow_ref[...])
    low = lax.broadcasted_iota(jnp.int32, (8, 128), 0) < 4

    def one_pair(pair, carry):
        both = jnp.concatenate([p_ref[pair * 2], p_ref[pair * 2 + 1]], 1)
        t = dot3(table, split(both), ((1,), (0,)))
        gs = []
        for i in range(2):
            cosine, sine = t[:64, i * 128 : i * 128 + 128], t[64:, i * 128 : i * 128 + 128]
            odd = lane_block(sine.shape, 16) == 1
            gs.append(cosine + jnp.where(odd, -pltpu.roll(sine, 16, 1), pltpu.roll(sine, 112, 1)))
        row = pl.ds(pl.multiple_of(lax.rem(pair, 8) * 8, 8), 8)
        for t8 in range(8):
            a0, a1 = (g[t8 * 8 : t8 * 8 + 8] for g in gs)
            out_ref[0, pair // 8, t8, row, :] = jnp.where(low, a0, pltpu.roll(a1, 4, 0))
            out_ref[1, pair // 8, t8, row, :] = jnp.where(low, pltpu.roll(a0, 4, 0), a1)
        return carry

    lax.fori_loop(0, 16, one_pair, 0)


def back_kernel(g_ref, out_ref, pair_ref, sum_ref, all_ref, res_ref, sendp, recvp, sends, recvs):
    chan, z = lax.axis_index("chan"), lax.axis_index("z")
    core, place = lax.rem(chan, 2), chan // 2
    mate = chan + 1 - 2 * core
    peers = [{"chan": mate}]
    for o in range(1, 16):
        peers.append({"z": lax.rem(z + o // 8, 2), "chan": lax.rem(place + o, 8) * 2 + core})
    greet(peers)()

    def to_mate(h):
        return remote(g_ref.at[1 - core, h], pair_ref.at[h], sendp.at[h], recvp.at[h], chan=mate)

    def spread(o):
        to_z, to = lax.rem(z + o // 8, 2), lax.rem(place + lax.rem(o, 8), 8)
        return to_z, to

    def out(o):
        to_z, to = spread(o)
        return remote(
            sum_ref.at[o // 8, to], all_ref.at[z, place], sends.at[o], recvs.at[z, place],
            z=to_z, chan=to * 2 + core,
        )

    def into(o):
        from_z, at = spread(o)
        return remote(
            sum_ref.at[o // 8, at], all_ref.at[from_z, at], sends.at[o], recvs.at[from_z, at],
            z=from_z, chan=at * 2 + core,
        )

    to_mate(1).start()
    to_mate(0).start()
    to_mate(1).wait_recv()
    sum_ref[1] = g_ref[core, 1] + pair_ref[1]

    @pl.loop(8, 16)
    def _(o):
        out(o).start()

    to_mate(0).wait_recv()
    sum_ref[0] = g_ref[core, 0] + pair_ref[0]

    @pl.loop(1, 8)
    def _(o):
        out(o).start()

    all_ref[z, place] = sum_ref[0, place]

    @pl.loop(1, 16)
    def _(o):
        into(o).wait_recv()

    lo, hi = (jnp.sum(all_ref[h], axis=0) for h in range(2))
    odd = lane_block(lo.shape, 16) == 1
    res_ref[0] = jnp.where(odd, pltpu.roll(hi, 16, 1), lo)
    res_ref[1] = jnp.where(odd, hi, pltpu.roll(lo, 112, 1))
    for j in range(4):
        for c in range(2):
            out_ref[j, c] = res_ref[c, pl.ds(j, 16, stride=4), :]

    @pl.loop(1, 16)
    def _(o):
        out(o).wait_send()

    to_mate(0).wait_send()
    to_mate(1).wait_send()


ANY = pl.BlockSpec(memory_space=pl.ANY)
DMA = pltpu.SemaphoreType.DMA


def phases(bins, offsets, first):
    m = first + jnp.arange(32, dtype=jnp.int32)
    angle = (bins[:, None] * m[None, :] % BLOCKS).astype(F32) * (2.0 * math.pi / BLOCKS)
    both = jnp.stack([jnp.cos(angle), jnp.sin(angle)]) * (1.0 / 256.0)
    chosen = offsets[:, None] == jnp.arange(SHIFTS, dtype=jnp.int32)[None, :]
    table = jnp.where(chosen[None, :, None, :], both[:, :, :, None], 0.0)
    table = table.reshape(2 * ALPHAS, 32 * SHIFTS)
    high = lax.reduce_precision(table, 8, 7)
    return high.astype(BF16), (table - high).astype(BF16)


def params(collective=None):
    return pltpu.CompilerParams(
        vmem_limit_bytes=48 * 2**20,
        collective_id=collective,
        has_side_effects=collective is not None,
    )


def on_device(samples, bins, offsets):
    e_high, e_low = phases(bins, offsets, lax.axis_index("chan") * 32)
    chunk = (16, 4, 2, 8, 128)
    right, other = pl.pallas_call(
        front_kernel,
        out_shape=[
            jax.ShapeDtypeStruct((4, 4, 16, 2, 8, 128), F32),
            jax.ShapeDtypeStruct((4, 16, 2, 8, 128), F32),
        ],
        in_specs=[VMEM, VMEM, VMEM, ANY, ANY],
        out_specs=[VMEM, VMEM],
        scratch_shapes=[pltpu.VMEM((512, 256), F32)]
        + [pltpu.VMEM(chunk, F32)] * 4
        + [pltpu.VMEM((2 * BLOCKS, BLOCKS), BF16)] * 2
        + [DMA((2,)), DMA((16,)), DMA((16,)), DMA((4, 16)), DMA((4, 16))]
        + [DMA((2, 4)), DMA((2, 4)), DMA((4,)), DMA((4,)), DMA((4,)), DMA((4,))],
        compiler_params=params(0),
        name="front",
    )(samples, *halves(channel_table()), *halves(block_table()))
    part = pl.pallas_call(
        gram_kernel,
        out_shape=jax.ShapeDtypeStruct((2, 2, 8, 64, 128), F32),
        in_specs=[VMEM] * 4,
        out_specs=VMEM,
        scratch_shapes=[pltpu.VMEM((32, 256, 128), F32)],
        compiler_params=params(),
        name="gram",
    )(right.reshape(-1, 128), other.reshape(-1, 128), e_high, e_low)
    return pl.pallas_call(
        back_kernel,
        out_shape=jax.ShapeDtypeStruct((4, 2, 16, 128), F32),
        in_specs=[VMEM],
        out_specs=VMEM,
        scratch_shapes=[
            pltpu.VMEM((2, 8, 64, 128), F32),
            pltpu.VMEM((2, 8, 64, 128), F32),
            pltpu.VMEM((2, 8, 64, 128), F32),
            pltpu.VMEM((2, 64, 128), F32),
            DMA((2,)), DMA((2,)), DMA((16,)), DMA((2, 8)),
        ],
        compiler_params=params(1),
        name="back",
    )(part)


def solution(mesh):
    finer = Mesh(mesh.devices.reshape(4, 2, mesh.shape["chan"]), ("x", "z", "chan"))
    sensor = ("x", "z")
    return jax.shard_map(
        on_device,
        mesh=finer,
        in_specs=(P(None, sensor, "chan", None), P(), P()),
        out_specs=P("chan", None, sensor, None),
        check_vma=False,
    )
```

```python
import math

import jax
import jax.numpy as jnp
import ml_dtypes
import numpy as np
from jax import lax
from jax.experimental import pallas as pl
from jax.experimental.pallas import tpu as pltpu
from jax.sharding import Mesh
from jax.sharding import PartitionSpec as P

CHANNELS = 128
BLOCKS = 512
ALPHAS = 64
SHIFTS = 8
FLOOR = 0.1
F32 = jnp.float32
BF16 = jnp.bfloat16
VMEM = pl.BlockSpec(memory_space=pltpu.VMEM)


def halves(table):
    high = table.astype(ml_dtypes.bfloat16)
    low = (table - high.astype(np.float64)).astype(ml_dtypes.bfloat16)
    return np.stack([high, low])


def channel_table():
    n = np.arange(CHANNELS)
    window = 0.5 - 0.5 * np.cos(2 * np.pi * n / CHANNELS)
    angle = 2 * np.pi * (n[:, None] * n[None, :] % CHANNELS) / CHANNELS
    cosine = window[:, None] * np.cos(angle) / math.sqrt(CHANNELS)
    sine = window[:, None] * np.sin(angle) / math.sqrt(CHANNELS)
    return halves(np.block([[cosine, -sine], [sine, cosine]]))


def block_table():
    n = np.arange(BLOCKS).reshape(16, 4, 8).transpose(1, 0, 2).reshape(-1)
    angle = 2 * np.pi * (n[:, None] * n[None, :] % BLOCKS) / BLOCKS
    return halves(np.concatenate([np.cos(angle), np.sin(angle)], 0) / math.sqrt(BLOCKS))


def split(x):
    high = x.astype(BF16)
    return high, (x - high.astype(F32)).astype(BF16)


def dot3(a, b, dims):
    def one(u, v):
        return lax.dot_general(u, v, (dims, ((), ())), preferred_element_type=F32)

    rows = a[0].shape[0]
    top = one(jnp.concatenate(a, 0), b[0])
    return top[:rows] + (top[rows:] + one(a[0], b[1]))


def lane_block(shape, width):
    return lax.broadcasted_iota(jnp.int32, shape, len(shape) - 1) // width % 2


def swap_blocks(tiles):
    tiles = list(tiles)
    for bit in (1, 2, 4, 8):
        width = 8 * bit
        upper = lane_block(tiles[0].shape, width) == 1
        for i in range(16):
            if i & bit:
                continue
            a, b = tiles[i], tiles[i | bit]
            axis = a.ndim - 1
            tiles[i] = jnp.where(upper, pltpu.roll(b, width, axis), a)
            tiles[i | bit] = jnp.where(upper, b, pltpu.roll(a, 128 - width, axis))
    return tiles


def remote(src, dst, send, recv, **where):
    return pltpu.make_async_remote_copy(
        src_ref=src,
        dst_ref=dst,
        send_sem=send,
        recv_sem=recv,
        device_id=where,
        device_id_type=pl.DeviceIdType.MESH,
    )


def phase_rows(bins_ref, offsets_ref, first):
    row = lax.broadcasted_iota(jnp.int32, (ALPHAS, ALPHAS), 0)
    same = row == lax.broadcasted_iota(jnp.int32, (ALPHAS, ALPHAS), 1)

    def column(ref):
        return jnp.sum(jnp.where(same, ref[...].astype(F32), 0.0), 1, keepdims=True)

    lane = lax.broadcasted_iota(jnp.int32, (ALPHAS, 256), 1)
    turns = column(bins_ref).astype(jnp.int32) * (first + lane // 8) % BLOCKS
    angle = turns.astype(F32) * (2.0 * math.pi / BLOCKS)
    chosen = column(offsets_ref).astype(jnp.int32) == lane % 8
    both = [jnp.where(chosen, f(angle) * (1.0 / 256.0), 0.0) for f in (jnp.cos, jnp.sin)]
    return split(jnp.concatenate(both, 0))


def kernel(
    x_hbm, bins_ref, offsets_ref, ctable_hbm, table_hbm, out_ref,
    x_ref, ctable_ref, table_ref, mid_ref, made_ref, got_ref, back_ref, land_ref,
    right_ref, other_ref, phase_ref, high_ref, low_ref, part_ref, pair_ref, sum_ref, all_ref, res_ref,
    load_sem, send1, recv1, send2, recv2, sendx, recvx, sendf, recvf, sendz, recvz,
    sendp, recvp, sends, recvs,
):
    chan, x, z = lax.axis_index("chan"), lax.axis_index("x"), lax.axis_index("z")
    core, place = lax.rem(chan, 2), chan // 2
    mate = chan + 1 - 2 * core
    after, before = lax.rem(x + 1, 4), lax.rem(x + 3, 4)

    barrier = pltpu.get_barrier_semaphore()
    peers = [{"chan": lax.rem(chan + o, 16)} for o in range(1, 16)]
    peers += [{"x": after}, {"x": before}]
    peers += [{"z": 1 - z, "chan": lax.rem(place + o, 8) * 2 + core} for o in range(8)]
    for where in peers:
        pl.semaphore_signal(barrier, device_id=where, device_id_type=pl.DeviceIdType.MESH)
    loads = [
        pltpu.make_async_copy(src, dst, load_sem.at[i])
        for i, (src, dst) in enumerate(
            [(x_hbm, x_ref), (ctable_hbm, ctable_ref), (table_hbm, table_ref)]
        )
    ]
    for load in loads:
        load.start()

    loads[0].wait()
    loads[1].wait()
    both = jnp.concatenate([x_ref[0].reshape(512, 128), x_ref[1].reshape(512, 128)], 1)
    mid_ref[...] = dot3(split(both), (ctable_ref[0], ctable_ref[1]), ((1,), (0,)))
    for c in range(2):
        for mc in range(4):
            tiles = [
                mid_ref[s * 32 + mc * 8 : s * 32 + mc * 8 + 8, c * 128 : c * 128 + 128]
                for s in range(16)
            ]
            for dest, tile in enumerate(swap_blocks(tiles)):
                made_ref[dest, mc, c] = tile
    pl.semaphore_wait(barrier, len(peers))

    def first_way(o, incoming):
        peer = lax.rem(chan + o, 16)
        at = peer if incoming else chan
        return remote(made_ref.at[peer], got_ref.at[at], send1.at[o], recv1.at[at], chan=peer)

    @pl.loop(1, 16)
    def _(o):
        first_way(o, False).start()

    got_ref[chan] = made_ref[chan]
    phase_ref[0], phase_ref[1] = phase_rows(bins_ref, offsets_ref, chan * 32)
    loads[2].wait()

    @pl.loop(1, 16)
    def _(o):
        first_way(o, True).wait_recv()

    def gathered(c):
        return jnp.concatenate([got_ref[:, mc, c].reshape(128, 128) for mc in range(4)], 0)

    u = dot3(
        (table_ref[0], table_ref[1]),
        split(jnp.concatenate([gathered(0), gathered(1)], 1)),
        ((1,), (0,)),
    )
    real = u[:BLOCKS, :128] + u[BLOCKS:, 128:]
    imag = u[:BLOCKS, 128:] - u[BLOCKS:, :128]
    scale = 1.0 / jnp.sqrt(real * real + imag * imag + FLOOR)
    white = split(jnp.concatenate([real * scale, imag * scale], 1))

    def second_way(o, mc, incoming):
        peer = lax.rem(chan + o, 16)
        at = peer if incoming else chan
        return remote(
            back_ref.at[peer, mc], land_ref.at[at, mc], send2.at[mc, o], recv2.at[mc, at], chan=peer
        )

    for mc in range(4):
        rows = [
            jnp.concatenate([table_ref[i, at : at + 128, :] for at in (mc * 128, BLOCKS + mc * 128)], 0)
            for i in range(2)
        ]
        u = dot3(rows, white, ((1,), (0,)))
        back_ref[:, mc, 0] = (u[:128, :128] - u[128:, 128:]).reshape(16, 8, 128)
        back_ref[:, mc, 1] = (u[:128, 128:] + u[128:, :128]).reshape(16, 8, 128)

        @pl.loop(1, 16)
        def _(o, mc=mc):
            second_way(o, mc, False).start()

        land_ref[chan, mc] = back_ref[chan, mc]

    def to_x(mc, way, incoming=False):
        peer = (after, before)[way ^ incoming]
        at = peer if incoming else x
        return remote(
            right_ref.at[x, mc], right_ref.at[at, mc], sendx.at[way, mc], recvx.at[way, mc], x=peer
        )

    def passed(mc, incoming=False):
        source, peer = (before, after) if mc % 2 == 0 else (after, before)
        at = lax.rem(x + 2, 4) if incoming else source
        return remote(right_ref.at[source, mc], right_ref.at[at, mc], sendf.at[mc], recvf.at[mc], x=peer)

    def to_z(mc):
        return remote(right_ref.at[x, mc], other_ref.at[mc], sendz.at[mc], recvz.at[mc], z=1 - z)

    def turn(mc):
        @pl.loop(1, 16)
        def _(o):
            second_way(o, mc, True).wait_recv()

        for c in range(2):
            tiles = [land_ref[i, mc, c] for i in range(16)]
            for s, tile in enumerate(swap_blocks(tiles)):
                right_ref[x, mc, s, c] = tile
        to_x(mc, 0).start()
        to_x(mc, 1).start()
        to_z(mc).start()

    def forward(mc):
        to_x(mc, mc % 2, True).wait_recv()
        passed(mc).start()

    def product(mc, r):
        left = []
        for c in range(2):
            rows = []
            for a in range(32):
                if a < 16:
                    row = right_ref[x, mc, a, c, pl.ds(r, 1), :]
                else:
                    row = other_ref[mc, a - 16, c, pl.ds(r, 1), :]
                rows.append(pltpu.roll(jnp.broadcast_to(row, (8, 128)), 0, 1, stride=1, stride_axis=0))
            left.append(jnp.concatenate(rows, 0))
        left = split(jnp.concatenate(left, 1))
        rows = []
        for i in range(4):
            tall = right_ref.at[i, mc].reshape(256, 128)
            real, imag = (tall[pl.ds(r + c * 8, 16, stride=16), :] for c in range(2))
            rows.append(jnp.concatenate([real, imag], 1))
            rows.append(jnp.concatenate([-imag, real], 1))
        right = split(jnp.concatenate(rows, 0))
        return dot3(left, right, ((1,), (1,))).reshape(32, 8, 128)

    def products(mc):
        to_x(mc, 1 - mc % 2, True).wait_recv()
        to_z(mc).wait_recv()
        passed(mc, True).wait_recv()

        def step(i, carry):
            for half in range(2):
                r = i * 4 + half * 2
                tiles = jnp.concatenate([product(mc, r), product(mc, r + 1)], 1)
                rows = pl.ds(pl.multiple_of(mc * 64 + r * 8, 16), 16)
                high_ref[:, rows, :], low_ref[:, rows, :] = split(tiles)
            return carry

        lax.fori_loop(0, 2, step, 0)

    turn(0)
    turn(1)
    forward(0)
    turn(2)
    forward(1)
    turn(3)
    forward(2)
    products(0)
    forward(3)
    products(1)
    products(2)
    products(3)

    low = lax.broadcasted_iota(jnp.int32, (8, 128), 0) < 4

    def one_pair(half, pair):
        a = half * 16 + pair * 2
        both = tuple(jnp.concatenate([ref[a], ref[a + 1]], 1) for ref in (high_ref, low_ref))
        t = dot3((phase_ref[0], phase_ref[1]), both, ((1,), (0,)))
        gs = []
        for i in range(2):
            cosine, sine = t[:64, i * 128 : i * 128 + 128], t[64:, i * 128 : i * 128 + 128]
            odd = lane_block(sine.shape, 16) == 1
            gs.append(cosine + jnp.where(odd, -pltpu.roll(sine, 16, 1), pltpu.roll(sine, 112, 1)))
        row = pl.ds(pl.multiple_of(pair * 8, 8), 8)
        for t8 in range(8):
            a0, a1 = (g[t8 * 8 : t8 * 8 + 8] for g in gs)
            part_ref[0, half, t8, row, :] = jnp.where(low, a0, pltpu.roll(a1, 4, 0))
            part_ref[1, half, t8, row, :] = jnp.where(low, pltpu.roll(a0, 4, 0), a1)

    def to_mate(half, piece):
        rows = pl.ds(piece * 32, 32)
        at = half * 2 + piece
        return remote(
            part_ref.at[1 - core, half, :, rows], pair_ref.at[half, :, rows],
            sendp.at[at], recvp.at[at], chan=mate,
        )

    def spread(piece, o, incoming=False):
        peer_z, peer = lax.rem(z + o // 8, 2), lax.rem(place + lax.rem(o, 8), 8)
        rows = pl.ds(piece * 32, 32)
        at_z, at = (peer_z, peer) if incoming else (z, place)
        return remote(
            sum_ref.at[o // 8, peer, rows], all_ref.at[at_z, at, rows],
            sends.at[piece, o], recvs.at[piece, at_z, at],
            z=peer_z, chan=peer * 2 + core,
        )

    def add_and_send(half, piece):
        to_mate(half, piece).wait_recv()
        rows = pl.ds(piece * 32, 32)
        sum_ref[half, :, rows] = part_ref[core, half, :, rows] + pair_ref[half, :, rows]

        @pl.loop(8 if half else 1, 16 if half else 8)
        def _(o):
            spread(piece, o).start()

        if not half:
            all_ref[z, place, rows] = sum_ref[0, place, rows]

    order = [(1, 0), (1, 1), (0, 0), (0, 1)]
    for i, (half, piece) in enumerate(order):

        def step(p, carry, half=half, piece=piece):
            one_pair(half, piece * 4 + p * 2)
            one_pair(half, piece * 4 + p * 2 + 1)
            return carry

        lax.fori_loop(0, 2, step, 0)
        to_mate(half, piece).start()
        if i:
            add_and_send(*order[i - 1])
    add_and_send(*order[3])

    @pl.loop(1, 16)
    def _(o):
        for piece in range(2):
            spread(piece, o, True).wait_recv()

    lo, hi = (jnp.sum(all_ref[h], axis=0) for h in range(2))
    odd = lane_block(lo.shape, 16) == 1
    res_ref[0] = jnp.where(odd, pltpu.roll(hi, 16, 1), lo)
    res_ref[1] = jnp.where(odd, hi, pltpu.roll(lo, 112, 1))
    for j in range(4):
        for c in range(2):
            out_ref[j, c] = res_ref[c, pl.ds(j, 16, stride=4), :]

    @pl.loop(1, 16)
    def _(o):
        first_way(o, False).wait_send()
        for mc in range(4):
            second_way(o, mc, False).wait_send()
        for piece in range(2):
            spread(piece, o).wait_send()

    for mc in range(4):
        to_x(mc, 0).wait_send()
        to_x(mc, 1).wait_send()
        to_z(mc).wait_send()
        passed(mc).wait_send()
        to_mate(mc // 2, mc % 2).wait_send()


DMA = pltpu.SemaphoreType.DMA
HBM = pl.BlockSpec(memory_space=pltpu.HBM)


def on_device(samples, bins, offsets):
    chunk = pltpu.VMEM((16, 4, 2, 8, 128), F32)
    eighths = pltpu.VMEM((2, 8, 64, 128), F32)
    return pl.pallas_call(
        kernel,
        out_shape=jax.ShapeDtypeStruct((4, 2, 16, 128), F32),
        in_specs=[HBM, VMEM, VMEM, HBM, HBM],
        out_specs=VMEM,
        scratch_shapes=[
            pltpu.VMEM((2, 16, 32, 128), F32),
            pltpu.VMEM((2, 256, 256), BF16),
            pltpu.VMEM((2, 2 * BLOCKS, BLOCKS), BF16),
            pltpu.VMEM((512, 256), F32),
            chunk, chunk, chunk, chunk,
            pltpu.VMEM((4, 4, 16, 2, 8, 128), F32),
            pltpu.VMEM((4, 16, 2, 8, 128), F32),
            pltpu.VMEM((2, 128, 256), BF16),
            pltpu.VMEM((32, 256, 128), BF16),
            pltpu.VMEM((32, 256, 128), BF16),
            pltpu.VMEM((2, 2, 8, 64, 128), F32),
            eighths, eighths, eighths,
            pltpu.VMEM((2, 64, 128), F32),
            DMA((3,)), DMA((16,)), DMA((16,)), DMA((4, 16)), DMA((4, 16)),
            DMA((2, 4)), DMA((2, 4)), DMA((4,)), DMA((4,)), DMA((4,)), DMA((4,)),
            DMA((4,)), DMA((4,)), DMA((2, 16)), DMA((2, 2, 8)),
        ],
        compiler_params=pltpu.CompilerParams(
            vmem_limit_bytes=48 * 2**20, collective_id=0, has_side_effects=True
        ),
        name="coherence",
    )(samples, bins.reshape(1, -1), offsets.reshape(1, -1), channel_table(), block_table())


def solution(mesh):
    finer = Mesh(mesh.devices.reshape(4, 2, mesh.shape["chan"]), ("x", "z", "chan"))
    sensor = ("x", "z")
    return jax.shard_map(
        on_device,
        mesh=finer,
        in_specs=(P(None, sensor, "chan", None), P(), P()),
        out_specs=P("chan", None, sensor, None),
        check_vma=False,
    )
```

```python
import math

import jax
import jax.numpy as jnp
import ml_dtypes
import numpy as np
from jax import lax
from jax.experimental import pallas as pl
from jax.experimental.pallas import tpu as pltpu
from jax.sharding import Mesh
from jax.sharding import PartitionSpec as P

CHANNELS = 128
BLOCKS = 512
ALPHAS = 64
SHIFTS = 8
FLOOR = 0.1
F32 = jnp.float32
BF16 = jnp.bfloat16
VMEM = pl.BlockSpec(memory_space=pltpu.VMEM)
HBM = pl.BlockSpec(memory_space=pltpu.HBM)


def halves(table):
    high = table.astype(ml_dtypes.bfloat16)
    low = (table - high.astype(np.float64)).astype(ml_dtypes.bfloat16)
    return np.stack([high, low])


def channel_table():
    n = np.arange(CHANNELS)
    window = 0.5 - 0.5 * np.cos(2 * np.pi * n / CHANNELS)
    angle = 2 * np.pi * (n[:, None] * n[None, :] % CHANNELS) / CHANNELS
    cosine = window[:, None] * np.cos(angle) / math.sqrt(CHANNELS)
    sine = window[:, None] * np.sin(angle) / math.sqrt(CHANNELS)
    return halves(np.block([[cosine, -sine], [sine, cosine]]))


def block_table():
    n = np.arange(BLOCKS).reshape(16, 4, 8).transpose(1, 0, 2).reshape(-1)
    angle = 2 * np.pi * (n[:, None] * n[None, :] % BLOCKS) / BLOCKS
    return halves(np.concatenate([np.cos(angle), np.sin(angle)], 0) / math.sqrt(BLOCKS))


def split(x):
    high = x.astype(BF16)
    return high, (x - high.astype(F32)).astype(BF16)


def dot3(a, b, dims):
    def one(u, v):
        return lax.dot_general(u, v, (dims, ((), ())), preferred_element_type=F32)

    rows = a[0].shape[0]
    top = one(jnp.concatenate(a, 0), b[0])
    return top[:rows] + (top[rows:] + one(a[0], b[1]))


def lane_block(shape, width):
    return lax.broadcasted_iota(jnp.int32, shape, len(shape) - 1) // width % 2


def swap_blocks(tiles):
    tiles = list(tiles)
    for bit in (1, 2, 4, 8):
        width = 8 * bit
        upper = lane_block(tiles[0].shape, width) == 1
        for i in range(16):
            if i & bit:
                continue
            a, b = tiles[i], tiles[i | bit]
            axis = a.ndim - 1
            tiles[i] = jnp.where(upper, pltpu.roll(b, width, axis), a)
            tiles[i | bit] = jnp.where(upper, b, pltpu.roll(a, 128 - width, axis))
    return tiles


def remote(src, dst, send, recv, **where):
    return pltpu.make_async_remote_copy(
        src_ref=src,
        dst_ref=dst,
        send_sem=send,
        recv_sem=recv,
        device_id=where,
        device_id_type=pl.DeviceIdType.MESH,
    )


def phase_rows(bins_ref, offsets_ref, first):
    row = lax.broadcasted_iota(jnp.int32, (ALPHAS, ALPHAS), 0)
    same = row == lax.broadcasted_iota(jnp.int32, (ALPHAS, ALPHAS), 1)

    def column(ref):
        return jnp.sum(jnp.where(same, ref[...].astype(F32), 0.0), 1, keepdims=True)

    lane = lax.broadcasted_iota(jnp.int32, (ALPHAS, 256), 1)
    turns = column(bins_ref).astype(jnp.int32) * (first + lane // 8) % BLOCKS
    angle = turns.astype(F32) * (2.0 * math.pi / BLOCKS)
    chosen = column(offsets_ref).astype(jnp.int32) == lane % 8
    both = [jnp.where(chosen, f(angle) * (1.0 / 256.0), 0.0) for f in (jnp.cos, jnp.sin)]
    return split(jnp.concatenate(both, 0))


def kernel(
    x_hbm, bins_hbm, offsets_hbm, ctable_hbm, table_hbm, out_ref,
    bins_ref, offsets_ref, x_ref, ctable_ref, table_ref, mid_ref, made_ref, got_ref, back_ref, land_ref,
    right_ref, other_ref, phase_ref, high_ref, low_ref, part_ref, pair_ref, sum_ref, all_ref, res_ref,
    load_sem, send1, recv1, send2, recv2, sendx, recvx, sendf, recvf, sendz, recvz,
    sendp, recvp, sends, recvs,
):
    chan, x, z = lax.axis_index("chan"), lax.axis_index("x"), lax.axis_index("z")
    core, place = lax.rem(chan, 2), chan // 2
    mate = chan + 1 - 2 * core
    after, before = lax.rem(x + 1, 4), lax.rem(x + 3, 4)

    barrier = pltpu.get_barrier_semaphore()
    peers = [{"chan": lax.rem(chan + o, 16)} for o in range(1, 16)]
    peers += [{"x": after}, {"x": before}]
    peers += [{"z": 1 - z, "chan": lax.rem(place + o, 8) * 2 + core} for o in range(8)]
    for where in peers:
        pl.semaphore_signal(barrier, device_id=where, device_id_type=pl.DeviceIdType.MESH)
    loads = [
        pltpu.make_async_copy(src, dst, load_sem.at[i])
        for i, (src, dst) in enumerate(
            [
                (x_hbm, x_ref),
                (ctable_hbm, ctable_ref),
                (table_hbm, table_ref),
                (bins_hbm, bins_ref),
                (offsets_hbm, offsets_ref),
            ]
        )
    ]
    for load in loads:
        load.start()

    loads[0].wait()
    loads[1].wait()
    both = jnp.concatenate([x_ref[0].reshape(512, 128), x_ref[1].reshape(512, 128)], 1)
    mid_ref[...] = dot3(split(both), (ctable_ref[0], ctable_ref[1]), ((1,), (0,)))
    for c in range(2):
        for mc in range(4):
            tiles = [
                mid_ref[s * 32 + mc * 8 : s * 32 + mc * 8 + 8, c * 128 : c * 128 + 128]
                for s in range(16)
            ]
            for dest, tile in enumerate(swap_blocks(tiles)):
                made_ref[dest, mc, c] = tile
    pl.semaphore_wait(barrier, len(peers))

    def first_way(o, incoming):
        peer = lax.rem(chan + o, 16)
        at = peer if incoming else chan
        return remote(made_ref.at[peer], got_ref.at[at], send1.at[o], recv1.at[at], chan=peer)

    @pl.loop(1, 16)
    def _(o):
        first_way(o, False).start()

    got_ref[chan] = made_ref[chan]
    loads[3].wait()
    loads[4].wait()
    phase_ref[0], phase_ref[1] = phase_rows(bins_ref, offsets_ref, chan * 32)
    loads[2].wait()

    @pl.loop(1, 16)
    def _(o):
        first_way(o, True).wait_recv()

    def gathered(c):
        return jnp.concatenate([got_ref[:, mc, c].reshape(128, 128) for mc in range(4)], 0)

    u = dot3(
        (table_ref[0], table_ref[1]),
        split(jnp.concatenate([gathered(0), gathered(1)], 1)),
        ((1,), (0,)),
    )
    real = u[:BLOCKS, :128] + u[BLOCKS:, 128:]
    imag = u[:BLOCKS, 128:] - u[BLOCKS:, :128]
    scale = 1.0 / jnp.sqrt(real * real + imag * imag + FLOOR)
    white = split(jnp.concatenate([real * scale, imag * scale], 1))

    def second_way(o, mc, incoming):
        peer = lax.rem(chan + o, 16)
        at = peer if incoming else chan
        return remote(
            back_ref.at[peer, mc], land_ref.at[at, mc], send2.at[mc, o], recv2.at[mc, at], chan=peer
        )

    for mc in range(4):
        rows = [
            jnp.concatenate([table_ref[i, at : at + 128, :] for at in (mc * 128, BLOCKS + mc * 128)], 0)
            for i in range(2)
        ]
        u = dot3(rows, white, ((1,), (0,)))
        back_ref[:, mc, 0] = (u[:128, :128] - u[128:, 128:]).reshape(16, 8, 128)
        back_ref[:, mc, 1] = (u[:128, 128:] + u[128:, :128]).reshape(16, 8, 128)

        @pl.loop(1, 16)
        def _(o, mc=mc):
            second_way(o, mc, False).start()

        land_ref[chan, mc] = back_ref[chan, mc]

    def to_x(mc, way, incoming=False):
        peer = (after, before)[way ^ incoming]
        at = peer if incoming else x
        return remote(
            right_ref.at[x, mc], right_ref.at[at, mc], sendx.at[way, mc], recvx.at[way, mc], x=peer
        )

    def passed(mc, incoming=False):
        source, peer = (before, after) if mc % 2 == 0 else (after, before)
        at = lax.rem(x + 2, 4) if incoming else source
        return remote(right_ref.at[source, mc], right_ref.at[at, mc], sendf.at[mc], recvf.at[mc], x=peer)

    def to_z(mc):
        return remote(right_ref.at[x, mc], other_ref.at[mc], sendz.at[mc], recvz.at[mc], z=1 - z)

    def turn(mc):
        @pl.loop(1, 16)
        def _(o):
            second_way(o, mc, True).wait_recv()

        for c in range(2):
            tiles = [land_ref[i, mc, c] for i in range(16)]
            for s, tile in enumerate(swap_blocks(tiles)):
                right_ref[x, mc, s, c] = tile
        to_x(mc, 0).start()
        to_x(mc, 1).start()
        to_z(mc).start()

    def forward(mc):
        to_x(mc, mc % 2, True).wait_recv()
        passed(mc).start()

    def product(mc, r):
        left = []
        for c in range(2):
            rows = []
            for a in range(32):
                if a < 16:
                    row = right_ref[x, mc, a, c, pl.ds(r, 1), :]
                else:
                    row = other_ref[mc, a - 16, c, pl.ds(r, 1), :]
                rows.append(pltpu.roll(jnp.broadcast_to(row, (8, 128)), 0, 1, stride=1, stride_axis=0))
            left.append(jnp.concatenate(rows, 0))
        left = split(jnp.concatenate(left, 1))
        rows = []
        for i in range(4):
            tall = right_ref.at[i, mc].reshape(256, 128)
            real, imag = (tall[pl.ds(r + c * 8, 16, stride=16), :] for c in range(2))
            rows.append(jnp.concatenate([real, imag], 1))
            rows.append(jnp.concatenate([-imag, real], 1))
        right = split(jnp.concatenate(rows, 0))
        return dot3(left, right, ((1,), (1,))).reshape(32, 8, 128)

    def products(mc):
        to_x(mc, 1 - mc % 2, True).wait_recv()
        to_z(mc).wait_recv()
        passed(mc, True).wait_recv()

        def step(i, carry):
            for half in range(2):
                r = i * 4 + half * 2
                tiles = jnp.concatenate([product(mc, r), product(mc, r + 1)], 1)
                rows = pl.ds(pl.multiple_of(mc * 64 + r * 8, 16), 16)
                high_ref[:, rows, :], low_ref[:, rows, :] = split(tiles)
            return carry

        lax.fori_loop(0, 2, step, 0)

    turn(0)
    turn(1)
    forward(0)
    turn(2)
    forward(1)
    turn(3)
    forward(2)
    products(0)
    forward(3)
    products(1)
    products(2)
    products(3)

    low = lax.broadcasted_iota(jnp.int32, (8, 128), 0) < 4

    def one_pair(half, pair):
        a = half * 16 + pair * 2
        both = tuple(jnp.concatenate([ref[a], ref[a + 1]], 1) for ref in (high_ref, low_ref))
        t = dot3((phase_ref[0], phase_ref[1]), both, ((1,), (0,)))
        gs = []
        for i in range(2):
            cosine, sine = t[:64, i * 128 : i * 128 + 128], t[64:, i * 128 : i * 128 + 128]
            odd = lane_block(sine.shape, 16) == 1
            gs.append(cosine + jnp.where(odd, -pltpu.roll(sine, 16, 1), pltpu.roll(sine, 112, 1)))
        row = pl.ds(pl.multiple_of(pair * 8, 8), 8)
        for t8 in range(8):
            a0, a1 = (g[t8 * 8 : t8 * 8 + 8] for g in gs)
            part_ref[0, half, t8, row, :] = jnp.where(low, a0, pltpu.roll(a1, 4, 0))
            part_ref[1, half, t8, row, :] = jnp.where(low, pltpu.roll(a0, 4, 0), a1)

    def to_mate(half, piece):
        rows = pl.ds(piece * 32, 32)
        at = half * 2 + piece
        return remote(
            part_ref.at[1 - core, half, :, rows], pair_ref.at[half, :, rows],
            sendp.at[at], recvp.at[at], chan=mate,
        )

    def spread(piece, o, incoming=False):
        peer_z, peer = lax.rem(z + o // 8, 2), lax.rem(place + lax.rem(o, 8), 8)
        rows = pl.ds(piece * 32, 32)
        at_z, at = (peer_z, peer) if incoming else (z, place)
        return remote(
            sum_ref.at[o // 8, peer, rows], all_ref.at[at_z, at, rows],
            sends.at[piece, o], recvs.at[piece, at_z, at],
            z=peer_z, chan=peer * 2 + core,
        )

    def add_and_send(half, piece):
        to_mate(half, piece).wait_recv()
        rows = pl.ds(piece * 32, 32)
        sum_ref[half, :, rows] = part_ref[core, half, :, rows] + pair_ref[half, :, rows]

        @pl.loop(8 if half else 1, 16 if half else 8)
        def _(o):
            spread(piece, o).start()

        if not half:
            all_ref[z, place, rows] = sum_ref[0, place, rows]

    order = [(1, 0), (1, 1), (0, 0), (0, 1)]
    for i, (half, piece) in enumerate(order):

        def step(p, carry, half=half, piece=piece):
            one_pair(half, piece * 4 + p * 2)
            one_pair(half, piece * 4 + p * 2 + 1)
            return carry

        lax.fori_loop(0, 2, step, 0)
        to_mate(half, piece).start()
        if i:
            add_and_send(*order[i - 1])
    add_and_send(*order[3])

    @pl.loop(1, 16)
    def _(o):
        for piece in range(2):
            spread(piece, o, True).wait_recv()

    lo, hi = (jnp.sum(all_ref[h], axis=0) for h in range(2))
    odd = lane_block(lo.shape, 16) == 1
    res_ref[0] = jnp.where(odd, pltpu.roll(hi, 16, 1), lo)
    res_ref[1] = jnp.where(odd, hi, pltpu.roll(lo, 112, 1))
    for j in range(4):
        for c in range(2):
            out_ref[j, c] = res_ref[c, pl.ds(j, 16, stride=4), :]

    @pl.loop(1, 16)
    def _(o):
        first_way(o, False).wait_send()
        for mc in range(4):
            second_way(o, mc, False).wait_send()
        for piece in range(2):
            spread(piece, o).wait_send()

    for mc in range(4):
        to_x(mc, 0).wait_send()
        to_x(mc, 1).wait_send()
        to_z(mc).wait_send()
        passed(mc).wait_send()
        to_mate(mc // 2, mc % 2).wait_send()


DMA = pltpu.SemaphoreType.DMA


def on_device(samples, bins, offsets):
    chunk = pltpu.VMEM((16, 4, 2, 8, 128), F32)
    eighths = pltpu.VMEM((2, 8, 64, 128), F32)
    return pl.pallas_call(
        kernel,
        out_shape=jax.ShapeDtypeStruct((4, 2, 16, 128), F32),
        in_specs=[HBM] * 5,
        out_specs=VMEM,
        scratch_shapes=[
            pltpu.VMEM((1, ALPHAS), jnp.int32),
            pltpu.VMEM((1, ALPHAS), jnp.int32),
            pltpu.VMEM((2, 16, 32, 128), F32),
            pltpu.VMEM((2, 256, 256), BF16),
            pltpu.VMEM((2, 2 * BLOCKS, BLOCKS), BF16),
            pltpu.VMEM((512, 256), F32),
            chunk, chunk, chunk, chunk,
            pltpu.VMEM((4, 4, 16, 2, 8, 128), F32),
            pltpu.VMEM((4, 16, 2, 8, 128), F32),
            pltpu.VMEM((2, 128, 256), BF16),
            pltpu.VMEM((32, 256, 128), BF16),
            pltpu.VMEM((32, 256, 128), BF16),
            pltpu.VMEM((2, 2, 8, 64, 128), F32),
            eighths, eighths, eighths,
            pltpu.VMEM((2, 64, 128), F32),
            DMA((5,)), DMA((16,)), DMA((16,)), DMA((4, 16)), DMA((4, 16)),
            DMA((2, 4)), DMA((2, 4)), DMA((4,)), DMA((4,)), DMA((4,)), DMA((4,)),
            DMA((4,)), DMA((4,)), DMA((2, 16)), DMA((2, 2, 8)),
        ],
        compiler_params=pltpu.CompilerParams(
            vmem_limit_bytes=60 * 2**20, collective_id=0, has_side_effects=True
        ),
        name="coherence",
    )(samples, bins.reshape(1, -1), offsets.reshape(1, -1), channel_table(), block_table())


def solution(mesh):
    finer = Mesh(mesh.devices.reshape(4, 2, mesh.shape["chan"]), ("x", "z", "chan"))
    sensor = ("x", "z")
    return jax.shard_map(
        on_device,
        mesh=finer,
        in_specs=(P(None, sensor, "chan", None), P(), P()),
        out_specs=P("chan", None, sensor, None),
        check_vma=False,
    )
```

```python
import math

import jax
import jax.numpy as jnp
import ml_dtypes
import numpy as np
from jax import lax
from jax.experimental import pallas as pl
from jax.experimental.pallas import tpu as pltpu
from jax.sharding import Mesh
from jax.sharding import PartitionSpec as P

CHANNELS = 128
BLOCKS = 512
ALPHAS = 64
SHIFTS = 8
FLOOR = 0.1
F32 = jnp.float32
BF16 = jnp.bfloat16
VMEM = pl.BlockSpec(memory_space=pltpu.VMEM)
HBM = pl.BlockSpec(memory_space=pltpu.HBM)


def halves(table):
    high = table.astype(ml_dtypes.bfloat16)
    low = (table - high.astype(np.float64)).astype(ml_dtypes.bfloat16)
    return np.stack([high, low])


def channel_table():
    n = np.arange(CHANNELS)
    window = 0.5 - 0.5 * np.cos(2 * np.pi * n / CHANNELS)
    angle = 2 * np.pi * (n[:, None] * n[None, :] % CHANNELS) / CHANNELS
    cosine = window[:, None] * np.cos(angle) / math.sqrt(CHANNELS)
    sine = window[:, None] * np.sin(angle) / math.sqrt(CHANNELS)
    return halves(np.block([[cosine, -sine], [sine, cosine]]))


def block_table():
    n = np.arange(BLOCKS).reshape(16, 4, 8).transpose(1, 0, 2).reshape(-1)
    angle = 2 * np.pi * (n[:, None] * n[None, :] % BLOCKS) / BLOCKS
    return halves(np.concatenate([np.cos(angle), np.sin(angle)], 0) / math.sqrt(BLOCKS))


def split(x):
    high = x.astype(BF16)
    return high, (x - high.astype(F32)).astype(BF16)


def dot3(a, b, dims):
    def one(u, v):
        return lax.dot_general(u, v, (dims, ((), ())), preferred_element_type=F32)

    rows = a[0].shape[0]
    top = one(jnp.concatenate(a, 0), b[0])
    return top[:rows] + (top[rows:] + one(a[0], b[1]))


def lane_block(shape, width):
    return lax.broadcasted_iota(jnp.int32, shape, len(shape) - 1) // width % 2


def swap_blocks(tiles):
    tiles = list(tiles)
    for bit in (1, 2, 4, 8):
        width = 8 * bit
        upper = lane_block(tiles[0].shape, width) == 1
        for i in range(16):
            if i & bit:
                continue
            a, b = tiles[i], tiles[i | bit]
            axis = a.ndim - 1
            tiles[i] = jnp.where(upper, pltpu.roll(b, width, axis), a)
            tiles[i | bit] = jnp.where(upper, b, pltpu.roll(a, 128 - width, axis))
    return tiles


def remote(src, dst, send, recv, **where):
    return pltpu.make_async_remote_copy(
        src_ref=src,
        dst_ref=dst,
        send_sem=send,
        recv_sem=recv,
        device_id=where,
        device_id_type=pl.DeviceIdType.MESH,
    )


def phase_rows(bins_ref, offsets_ref, first):
    row = lax.broadcasted_iota(jnp.int32, (ALPHAS, ALPHAS), 0)
    same = row == lax.broadcasted_iota(jnp.int32, (ALPHAS, ALPHAS), 1)

    def column(ref):
        return jnp.sum(jnp.where(same, ref[...].astype(F32), 0.0), 1, keepdims=True)

    lane = lax.broadcasted_iota(jnp.int32, (ALPHAS, 256), 1)
    turns = column(bins_ref).astype(jnp.int32) * (first + lane // 8) % BLOCKS
    angle = turns.astype(F32) * (2.0 * math.pi / BLOCKS)
    chosen = column(offsets_ref).astype(jnp.int32) == lane % 8
    both = [jnp.where(chosen, f(angle) * (1.0 / 256.0), 0.0) for f in (jnp.cos, jnp.sin)]
    return split(jnp.concatenate(both, 0))


def kernel(
    x_hbm, bins_hbm, offsets_hbm, ctable_hbm, table_hbm, out_ref,
    bins_ref, offsets_ref, x_ref, ctable_ref, table_ref, mid_ref, made_ref, got_ref, back_ref, land_ref,
    right_ref, other_ref, phase_ref, high_ref, low_ref, part_ref, pair_ref, sum_ref, all_ref, res_ref,
    load_sem, send1, recv1, send2, recv2, sendx, recvx, sendf, recvf, sendz, recvz,
    sendp, recvp, sends, recvs,
):
    chan, x, z = lax.axis_index("chan"), lax.axis_index("x"), lax.axis_index("z")
    core, place = lax.rem(chan, 2), chan // 2
    mate = chan + 1 - 2 * core
    after, before = lax.rem(x + 1, 4), lax.rem(x + 3, 4)

    barrier = pltpu.get_barrier_semaphore()
    peers = [{"chan": lax.rem(chan + o, 16)} for o in range(1, 16)]
    peers += [{"x": after}, {"x": before}]
    peers += [{"z": 1 - z, "chan": lax.rem(place + o, 8) * 2 + core} for o in range(8)]
    for where in peers:
        pl.semaphore_signal(barrier, device_id=where, device_id_type=pl.DeviceIdType.MESH)
    loads = [
        pltpu.make_async_copy(src, dst, load_sem.at[i])
        for i, (src, dst) in enumerate(
            [
                (x_hbm, x_ref),
                (ctable_hbm, ctable_ref),
                (table_hbm, table_ref),
                (bins_hbm, bins_ref),
                (offsets_hbm, offsets_ref),
            ]
        )
    ]
    for load in loads:
        load.start()

    loads[0].wait()
    loads[1].wait()
    both = jnp.concatenate([x_ref[0].reshape(512, 128), x_ref[1].reshape(512, 128)], 1)
    mid_ref[...] = dot3(split(both), (ctable_ref[0], ctable_ref[1]), ((1,), (0,)))

    def tiles_of(h):
        for mc in range(4):
            tiles = [
                mid_ref[s * 32 + mc * 8 : s * 32 + mc * 8 + 8, c * 128 : c * 128 + 128]
                for c in range(2)
                for s in range(h * 8, h * 8 + 8)
            ]
            for dest, tile in enumerate(swap_blocks(tiles)):
                made_ref[h, dest, mc] = tile

    def exchange(src, dst, send, recv, h, o, incoming):
        peer = lax.rem(chan + o, 16)
        at = peer if incoming else chan
        return remote(src.at[h, peer], dst.at[h, at], send.at[h, o], recv.at[h, at], chan=peer)

    def first_way(h, o, incoming=False):
        return exchange(made_ref, got_ref, send1, recv1, h, o, incoming)

    def second_way(h, o, incoming=False):
        return exchange(back_ref, land_ref, send2, recv2, h, o, incoming)

    def send_all(way, h):
        @pl.loop(1, 16)
        def _(o):
            way(h, o).start()

    def wait_all(way, h):
        @pl.loop(1, 16)
        def _(o):
            way(h, o, True).wait_recv()

    tiles_of(0)
    pl.semaphore_wait(barrier, len(peers))
    send_all(first_way, 0)
    tiles_of(1)
    send_all(first_way, 1)
    for h in range(2):
        got_ref[h, chan] = made_ref[h, chan]
    loads[3].wait()
    loads[4].wait()
    phase_ref[0], phase_ref[1] = phase_rows(bins_ref, offsets_ref, chan * 32)
    loads[2].wait()

    for h in range(2):
        wait_all(first_way, h)
        table = (table_ref[0], table_ref[1])
        d = jnp.concatenate([got_ref[h, :, mc].reshape(128, 128) for mc in range(4)], 0)
        u = dot3(table, split(d), ((1,), (0,)))
        first_part = lax.broadcasted_iota(jnp.int32, (BLOCKS, 128), 1) < 64
        turned = pltpu.roll(u[BLOCKS:], 64, 1)
        spectra = u[:BLOCKS] + jnp.where(first_part, turned, -turned)
        power = spectra * spectra
        power = power + pltpu.roll(power, 64, 1)
        white = spectra / jnp.sqrt(power + FLOOR)
        u = dot3(table, split(white), ((1,), (0,)))
        turned = pltpu.roll(u[BLOCKS:], 64, 1)
        blocks = u[:BLOCKS] + jnp.where(first_part, -turned, turned)
        for mc in range(4):
            back_ref[h, :, mc] = blocks[mc * 128 : mc * 128 + 128].reshape(16, 8, 128)
        send_all(second_way, h)
        land_ref[h, chan] = back_ref[h, chan]

    def eight(i, mc, h):
        return right_ref.at[i, mc, pl.ds(h * 8, 8)]

    def to_x(h, mc, way, incoming=False):
        peer = (after, before)[way ^ incoming]
        at = peer if incoming else x
        return remote(
            eight(x, mc, h), eight(at, mc, h), sendx.at[way, h, mc], recvx.at[way, h, mc], x=peer
        )

    def passed(h, mc, way, incoming=False):
        source, peer = (before, after) if way == 0 else (after, before)
        at = lax.rem(x + 2, 4) if incoming else source
        four = pl.ds(h * 8 + way * 4, 4)
        return remote(
            right_ref.at[source, mc, four], right_ref.at[at, mc, four],
            sendf.at[way, h, mc], recvf.at[way, h, mc], x=peer,
        )

    def to_z(h, mc):
        return remote(
            eight(x, mc, h), other_ref.at[mc, pl.ds(h * 8, 8)], sendz.at[h, mc], recvz.at[h, mc], z=1 - z
        )

    def turn(h, mc):
        tiles = swap_blocks([land_ref[h, i, mc] for i in range(16)])
        for i, tile in enumerate(tiles):
            right_ref[x, mc, h * 8 + i % 8, i // 8] = tile
        to_x(h, mc, 0).start()
        to_x(h, mc, 1).start()
        to_z(h, mc).start()

    def forward(h, mc):
        for way in range(2):
            to_x(h, mc, way, True).wait_recv()
            passed(h, mc, way).start()

    def product(mc, r):
        left = []
        for c in range(2):
            rows = []
            for a in range(32):
                if a < 16:
                    row = right_ref[x, mc, a, c, pl.ds(r, 1), :]
                else:
                    row = other_ref[mc, a - 16, c, pl.ds(r, 1), :]
                rows.append(pltpu.roll(jnp.broadcast_to(row, (8, 128)), 0, 1, stride=1, stride_axis=0))
            left.append(jnp.concatenate(rows, 0))
        left = split(jnp.concatenate(left, 1))
        rows = []
        for i in range(4):
            tall = right_ref.at[i, mc].reshape(256, 128)
            real, imag = (tall[pl.ds(r + c * 8, 16, stride=16), :] for c in range(2))
            rows.append(jnp.concatenate([real, imag], 1))
            rows.append(jnp.concatenate([-imag, real], 1))
        right = split(jnp.concatenate(rows, 0))
        return dot3(left, right, ((1,), (1,))).reshape(32, 8, 128)

    def products(mc):
        for h in range(2):
            to_z(h, mc).wait_recv()
            for way in range(2):
                passed(h, mc, way, True).wait_recv()

        def step(i, carry):
            for half in range(2):
                r = i * 4 + half * 2
                tiles = jnp.concatenate([product(mc, r), product(mc, r + 1)], 1)
                rows = pl.ds(pl.multiple_of(mc * 64 + r * 8, 16), 16)
                high_ref[:, rows, :], low_ref[:, rows, :] = split(tiles)
            return carry

        lax.fori_loop(0, 2, step, 0)

    wait_all(second_way, 0)
    for mc in range(4):
        turn(0, mc)
    wait_all(second_way, 1)
    for mc in range(4):
        turn(1, mc)
        forward(0, mc)
    for mc in range(4):
        forward(1, mc)
    for mc in range(4):
        products(mc)

    low = lax.broadcasted_iota(jnp.int32, (8, 128), 0) < 4

    def one_pair(half, pair):
        a = half * 16 + pair * 2
        both = tuple(jnp.concatenate([ref[a], ref[a + 1]], 1) for ref in (high_ref, low_ref))
        t = dot3((phase_ref[0], phase_ref[1]), both, ((1,), (0,)))
        gs = []
        for i in range(2):
            cosine, sine = t[:64, i * 128 : i * 128 + 128], t[64:, i * 128 : i * 128 + 128]
            odd = lane_block(sine.shape, 16) == 1
            gs.append(cosine + jnp.where(odd, -pltpu.roll(sine, 16, 1), pltpu.roll(sine, 112, 1)))
        row = pl.ds(pair * 8, 8)
        for t8 in range(8):
            a0, a1 = (g[t8 * 8 : t8 * 8 + 8] for g in gs)
            part_ref[0, half, t8, row, :] = jnp.where(low, a0, pltpu.roll(a1, 4, 0))
            part_ref[1, half, t8, row, :] = jnp.where(low, pltpu.roll(a0, 4, 0), a1)

    def to_mate(half, piece):
        rows = pl.ds(piece * 32, 32)
        at = half * 2 + piece
        return remote(
            part_ref.at[1 - core, half, :, rows], pair_ref.at[half, :, rows],
            sendp.at[at], recvp.at[at], chan=mate,
        )

    def spread(piece, o, incoming=False):
        peer_z, peer = lax.rem(z + o // 8, 2), lax.rem(place + lax.rem(o, 8), 8)
        rows = pl.ds(piece * 32, 32)
        at_z, at = (peer_z, peer) if incoming else (z, place)
        return remote(
            sum_ref.at[o // 8, peer, rows], all_ref.at[at_z, at, rows],
            sends.at[piece, o], recvs.at[piece, at_z, at],
            z=peer_z, chan=peer * 2 + core,
        )

    def add_and_send(half, piece):
        to_mate(half, piece).wait_recv()
        rows = pl.ds(piece * 32, 32)
        sum_ref[half, :, rows] = part_ref[core, half, :, rows] + pair_ref[half, :, rows]

        @pl.loop(8 if half else 1, 16 if half else 8)
        def _(o):
            spread(piece, o).start()

        if not half:
            all_ref[z, place, rows] = sum_ref[0, place, rows]

    order = [(1, 0), (1, 1), (0, 0), (0, 1)]
    for i, (half, piece) in enumerate(order):

        for pair in range(piece * 4, piece * 4 + 4):
            one_pair(half, pair)
        to_mate(half, piece).start()
        if i:
            add_and_send(*order[i - 1])
    add_and_send(*order[3])

    @pl.loop(1, 16)
    def _(o):
        for piece in range(2):
            spread(piece, o, True).wait_recv()

    lo, hi = (jnp.sum(all_ref[h], axis=0) for h in range(2))
    odd = lane_block(lo.shape, 16) == 1
    res_ref[0] = jnp.where(odd, pltpu.roll(hi, 16, 1), lo)
    res_ref[1] = jnp.where(odd, hi, pltpu.roll(lo, 112, 1))
    for j in range(4):
        for c in range(2):
            out_ref[j, c] = res_ref[c, pl.ds(j, 16, stride=4), :]

    @pl.loop(1, 16)
    def _(o):
        for h in range(2):
            first_way(h, o).wait_send()
            second_way(h, o).wait_send()
        for piece in range(2):
            spread(piece, o).wait_send()

    for mc in range(4):
        for h in range(2):
            for way in range(2):
                to_x(h, mc, way).wait_send()
                passed(h, mc, way).wait_send()
            to_z(h, mc).wait_send()
        to_mate(mc // 2, mc % 2).wait_send()


DMA = pltpu.SemaphoreType.DMA


def on_device(samples, bins, offsets):
    chunk = pltpu.VMEM((2, 16, 4, 8, 128), F32)
    eighths = pltpu.VMEM((2, 8, 64, 128), F32)
    return pl.pallas_call(
        kernel,
        out_shape=jax.ShapeDtypeStruct((4, 2, 16, 128), F32),
        in_specs=[HBM] * 5,
        out_specs=VMEM,
        scratch_shapes=[
            pltpu.VMEM((1, ALPHAS), jnp.int32),
            pltpu.VMEM((1, ALPHAS), jnp.int32),
            pltpu.VMEM((2, 16, 32, 128), F32),
            pltpu.VMEM((2, 256, 256), BF16),
            pltpu.VMEM((2, 2 * BLOCKS, BLOCKS), BF16),
            pltpu.VMEM((512, 256), F32),
            chunk, chunk, chunk, chunk,
            pltpu.VMEM((4, 4, 16, 2, 8, 128), F32),
            pltpu.VMEM((4, 16, 2, 8, 128), F32),
            pltpu.VMEM((2, 128, 256), BF16),
            pltpu.VMEM((32, 256, 128), BF16),
            pltpu.VMEM((32, 256, 128), BF16),
            pltpu.VMEM((2, 2, 8, 64, 128), F32),
            eighths, eighths, eighths,
            pltpu.VMEM((2, 64, 128), F32),
            DMA((5,)), DMA((2, 16)), DMA((2, 16)), DMA((2, 16)), DMA((2, 16)),
            DMA((2, 2, 4)), DMA((2, 2, 4)), DMA((2, 2, 4)), DMA((2, 2, 4)), DMA((2, 4)), DMA((2, 4)),
            DMA((4,)), DMA((4,)), DMA((2, 16)), DMA((2, 2, 8)),
        ],
        compiler_params=pltpu.CompilerParams(
            vmem_limit_bytes=60 * 2**20, collective_id=0, has_side_effects=True
        ),
        name="coherence",
    )(samples, bins.reshape(1, -1), offsets.reshape(1, -1), channel_table(), block_table())


def solution(mesh):
    finer = Mesh(mesh.devices.reshape(4, 2, mesh.shape["chan"]), ("x", "z", "chan"))
    sensor = ("x", "z")
    return jax.shard_map(
        on_device,
        mesh=finer,
        in_specs=(P(None, sensor, "chan", None), P(), P()),
        out_specs=P("chan", None, sensor, None),
        check_vma=False,
    )
```

```python
import math

import jax
import jax.numpy as jnp
import ml_dtypes
import numpy as np
from jax import lax
from jax.experimental import pallas as pl
from jax.experimental.pallas import tpu as pltpu
from jax.sharding import Mesh
from jax.sharding import PartitionSpec as P

CHANNELS = 128
BLOCKS = 512
ALPHAS = 64
SHIFTS = 8
FLOOR = 0.1
F32 = jnp.float32
BF16 = jnp.bfloat16
VMEM = pl.BlockSpec(memory_space=pltpu.VMEM)
HBM = pl.BlockSpec(memory_space=pltpu.HBM)


def halves(table):
    high = table.astype(ml_dtypes.bfloat16)
    low = (table - high.astype(np.float64)).astype(ml_dtypes.bfloat16)
    return np.stack([high, low])


def channel_table():
    n = np.arange(CHANNELS)
    window = 0.5 - 0.5 * np.cos(2 * np.pi * n / CHANNELS)
    angle = 2 * np.pi * (n[:, None] * n[None, :] % CHANNELS) / CHANNELS
    cosine = window[:, None] * np.cos(angle) / math.sqrt(CHANNELS)
    sine = window[:, None] * np.sin(angle) / math.sqrt(CHANNELS)
    return halves(np.block([[cosine, -sine], [sine, cosine]]))


def block_table():
    n = np.arange(BLOCKS).reshape(16, 4, 8).transpose(1, 0, 2).reshape(-1)
    angle = 2 * np.pi * (n[:, None] * n[None, :] % BLOCKS) / BLOCKS
    return halves(np.concatenate([np.cos(angle), np.sin(angle)], 0) / math.sqrt(BLOCKS))


def split(x):
    high = x.astype(BF16)
    return high, (x - high.astype(F32)).astype(BF16)


def dot3(a, b, dims):
    def one(u, v):
        return lax.dot_general(u, v, (dims, ((), ())), preferred_element_type=F32)

    rows = a[0].shape[0]
    top = one(jnp.concatenate(a, 0), b[0])
    return top[:rows] + (top[rows:] + one(a[0], b[1]))


def lane_block(shape, width):
    return lax.broadcasted_iota(jnp.int32, shape, len(shape) - 1) // width % 2


def swap_blocks(tiles):
    tiles = list(tiles)
    for bit in (1, 2, 4, 8):
        width = 8 * bit
        upper = lane_block(tiles[0].shape, width) == 1
        for i in range(16):
            if i & bit:
                continue
            a, b = tiles[i], tiles[i | bit]
            axis = a.ndim - 1
            tiles[i] = jnp.where(upper, pltpu.roll(b, width, axis), a)
            tiles[i | bit] = jnp.where(upper, b, pltpu.roll(a, 128 - width, axis))
    return tiles


def remote(src, dst, send, recv, **where):
    return pltpu.make_async_remote_copy(
        src_ref=src,
        dst_ref=dst,
        send_sem=send,
        recv_sem=recv,
        device_id=where,
        device_id_type=pl.DeviceIdType.MESH,
    )


def phase_rows(bins_ref, offsets_ref, first):
    row = lax.broadcasted_iota(jnp.int32, (ALPHAS, ALPHAS), 0)
    same = row == lax.broadcasted_iota(jnp.int32, (ALPHAS, ALPHAS), 1)

    def column(ref):
        return jnp.sum(jnp.where(same, ref[...].astype(F32), 0.0), 1, keepdims=True)

    lane = lax.broadcasted_iota(jnp.int32, (ALPHAS, 256), 1)
    turns = column(bins_ref).astype(jnp.int32) * (first + lane // 8) % BLOCKS
    angle = turns.astype(F32) * (2.0 * math.pi / BLOCKS)
    chosen = column(offsets_ref).astype(jnp.int32) == lane % 8
    both = [jnp.where(chosen, f(angle) * (1.0 / 256.0), 0.0) for f in (jnp.cos, jnp.sin)]
    return split(jnp.concatenate(both, 0))


def kernel(
    x_hbm, bins_hbm, offsets_hbm, ctable_hbm, table_hbm, out_ref,
    bins_ref, offsets_ref, x_ref, ctable_ref, table_ref, mid_ref, made_ref, got_ref, back_ref, land_ref,
    right_ref, other_ref, phase_ref, high_ref, low_ref, part_ref, pair_ref, sum_ref, all_ref, res_ref,
    load_sem, send1, recv1, send2, recv2, sendx, recvx, sendf, recvf, sendz, recvz,
    sendp, recvp, sends, recvs,
):
    chan, x, z = lax.axis_index("chan"), lax.axis_index("x"), lax.axis_index("z")
    core, place = lax.rem(chan, 2), chan // 2
    mate = chan + 1 - 2 * core
    after, before = lax.rem(x + 1, 4), lax.rem(x + 3, 4)

    loads = [
        pltpu.make_async_copy(src, dst, load_sem.at[i])
        for i, (src, dst) in enumerate(
            [
                (x_hbm, x_ref),
                (ctable_hbm, ctable_ref),
                (table_hbm, table_ref),
                (bins_hbm, bins_ref),
                (offsets_hbm, offsets_ref),
            ]
        )
    ]
    for load in loads:
        load.start()

    barrier = pltpu.get_barrier_semaphore()
    peers = [{"chan": lax.rem(chan + o, 16)} for o in range(1, 16)]
    peers += [{"x": after}, {"x": before}]
    peers += [{"z": 1 - z, "chan": lax.rem(place + o, 8) * 2 + core} for o in range(8)]
    for where in peers:
        pl.semaphore_signal(barrier, device_id=where, device_id_type=pl.DeviceIdType.MESH)

    loads[0].wait()
    loads[1].wait()
    both = jnp.concatenate([x_ref[0].reshape(512, 128), x_ref[1].reshape(512, 128)], 1)
    mid_ref[...] = dot3(split(both), (ctable_ref[0], ctable_ref[1]), ((1,), (0,)))
    for c in range(2):
        for mc in range(4):
            tiles = [
                mid_ref[s * 32 + mc * 8 : s * 32 + mc * 8 + 8, c * 128 : c * 128 + 128]
                for s in range(16)
            ]
            for dest, tile in enumerate(swap_blocks(tiles)):
                made_ref[dest, mc, c] = tile
    pl.semaphore_wait(barrier, len(peers))

    def exchange(src, dst, send, recv, o):
        peer = lax.rem(chan + o, 16)
        return remote(src.at[peer], dst.at[chan], send, recv, chan=peer)

    def everyone(src, dst, send, recv):
        most = pl.ds(0, 15)
        return remote(src.at[most], dst.at[most], send, recv, chan=mate)

    first = (made_ref, got_ref, send1, recv1)

    @pl.loop(1, 16)
    def _(o):
        exchange(*first, o).start()

    got_ref[chan] = made_ref[chan]
    loads[3].wait()
    loads[4].wait()
    phase_ref[0], phase_ref[1] = phase_rows(bins_ref, offsets_ref, chan * 32)
    loads[2].wait()

    everyone(*first).wait_recv()

    def gathered(c):
        return jnp.concatenate([got_ref[:, mc, c].reshape(128, 128) for mc in range(4)], 0)

    u = dot3(
        (table_ref[0], table_ref[1]),
        split(jnp.concatenate([gathered(0), gathered(1)], 1)),
        ((1,), (0,)),
    )
    real = u[:BLOCKS, :128] + u[BLOCKS:, 128:]
    imag = u[:BLOCKS, 128:] - u[BLOCKS:, :128]
    scale = 1.0 / jnp.sqrt(real * real + imag * imag + FLOOR)
    white = split(jnp.concatenate([real * scale, imag * scale], 1))

    def second(mc):
        return back_ref.at[mc], land_ref.at[mc], send2.at[mc], recv2.at[mc]

    for mc in range(4):
        rows = [
            jnp.concatenate([table_ref[i, at : at + 128, :] for at in (mc * 128, BLOCKS + mc * 128)], 0)
            for i in range(2)
        ]
        u = dot3(rows, white, ((1,), (0,)))
        back_ref[mc, :, 0] = (u[:128, :128] - u[128:, 128:]).reshape(16, 8, 128)
        back_ref[mc, :, 1] = (u[:128, 128:] + u[128:, :128]).reshape(16, 8, 128)
        if mc:
            everyone(*second(mc - 1)).wait_send()

        @pl.loop(1, 16)
        def _(o, mc=mc):
            exchange(*second(mc), o).start()

        land_ref[mc, chan] = back_ref[mc, chan]

    def to_x(mc, way, incoming=False):
        peer = (after, before)[way ^ incoming]
        at = peer if incoming else x
        return remote(
            right_ref.at[x, mc], right_ref.at[at, mc], sendx.at[way, mc], recvx.at[way, mc], x=peer
        )

    def passed(mc, incoming=False):
        source, peer = (before, after) if mc % 2 == 0 else (after, before)
        at = lax.rem(x + 2, 4) if incoming else source
        return remote(right_ref.at[source, mc], right_ref.at[at, mc], sendf.at[mc], recvf.at[mc], x=peer)

    def to_z(mc):
        return remote(right_ref.at[x, mc], other_ref.at[mc], sendz.at[mc], recvz.at[mc], z=1 - z)

    def turn(mc):
        everyone(*second(mc)).wait_recv()
        for c in range(2):
            tiles = [land_ref[mc, i, c] for i in range(16)]
            for s, tile in enumerate(swap_blocks(tiles)):
                right_ref[x, mc, s, c] = tile
        to_x(mc, 0).start()
        to_x(mc, 1).start()
        to_z(mc).start()

    def forward(mc):
        to_x(mc, mc % 2, True).wait_recv()
        passed(mc).start()

    def product(mc, r):
        left = []
        for c in range(2):
            rows = []
            for a in range(32):
                if a < 16:
                    row = right_ref[x, mc, a, c, pl.ds(r, 1), :]
                else:
                    row = other_ref[mc, a - 16, c, pl.ds(r, 1), :]
                rows.append(pltpu.roll(jnp.broadcast_to(row, (8, 128)), 0, 1, stride=1, stride_axis=0))
            left.append(jnp.concatenate(rows, 0))
        left = split(jnp.concatenate(left, 1))
        rows = []
        for i in range(4):
            tall = right_ref.at[i, mc].reshape(256, 128)
            real, imag = (tall[pl.ds(r + c * 8, 16, stride=16), :] for c in range(2))
            rows.append(jnp.concatenate([real, imag], 1))
            rows.append(jnp.concatenate([-imag, real], 1))
        right = split(jnp.concatenate(rows, 0))
        return dot3(left, right, ((1,), (1,))).reshape(32, 8, 128)

    def products(mc):
        to_x(mc, 1 - mc % 2, True).wait_recv()
        to_z(mc).wait_recv()
        passed(mc, True).wait_recv()

        def step(i, carry):
            for half in range(2):
                r = i * 4 + half * 2
                tiles = jnp.concatenate([product(mc, r), product(mc, r + 1)], 1)
                rows = pl.ds(pl.multiple_of(mc * 64 + r * 8, 16), 16)
                high_ref[:, rows, :], low_ref[:, rows, :] = split(tiles)
            return carry

        lax.fori_loop(0, 2, step, 0)

    turn(0)
    turn(1)
    forward(0)
    turn(2)
    forward(1)
    turn(3)
    forward(2)
    products(0)
    forward(3)
    products(1)
    products(2)
    products(3)

    low = lax.broadcasted_iota(jnp.int32, (8, 128), 0) < 4

    def one_pair(half, pair):
        a = half * 16 + pair * 2
        both = tuple(jnp.concatenate([ref[a], ref[a + 1]], 1) for ref in (high_ref, low_ref))
        t = dot3((phase_ref[0], phase_ref[1]), both, ((1,), (0,)))
        gs = []
        for i in range(2):
            cosine, sine = t[:64, i * 128 : i * 128 + 128], t[64:, i * 128 : i * 128 + 128]
            odd = lane_block(sine.shape, 16) == 1
            gs.append(cosine + jnp.where(odd, -pltpu.roll(sine, 16, 1), pltpu.roll(sine, 112, 1)))
        row = pl.ds(pair * 8, 8)
        for t8 in range(8):
            a0, a1 = (g[t8 * 8 : t8 * 8 + 8] for g in gs)
            part_ref[0, half, t8, row, :] = jnp.where(low, a0, pltpu.roll(a1, 4, 0))
            part_ref[1, half, t8, row, :] = jnp.where(low, pltpu.roll(a0, 4, 0), a1)

    def to_mate(half, piece):
        rows = pl.ds(piece * 32, 32)
        at = half * 2 + piece
        return remote(
            part_ref.at[1 - core, half, :, rows], pair_ref.at[half, :, rows],
            sendp.at[at], recvp.at[at], chan=mate,
        )

    def spread(piece, o):
        peer_z, peer = lax.rem(z + o // 8, 2), lax.rem(place + lax.rem(o, 8), 8)
        rows = pl.ds(piece * 32, 32)
        return remote(
            sum_ref.at[o // 8 * 8 + peer, rows], all_ref.at[z * 8 + place, rows],
            sends, recvs, z=peer_z, chan=peer * 2 + core,
        )

    def add_and_send(half, piece):
        to_mate(half, piece).wait_recv()
        rows = pl.ds(piece * 32, 32)
        sum_ref[half * 8 : half * 8 + 8, rows] = part_ref[core, half, :, rows] + pair_ref[half, :, rows]

        @pl.loop(8 if half else 1, 16 if half else 8)
        def _(o):
            spread(piece, o).start()

        if not half:
            all_ref[z * 8 + place, rows] = sum_ref[place, rows]

    order = [(1, 0), (1, 1), (0, 0), (0, 1)]
    for i, (half, piece) in enumerate(order):

        for pair in range(piece * 4, piece * 4 + 4):
            one_pair(half, pair)
        to_mate(half, piece).start()
        if i:
            add_and_send(*order[i - 1])
    add_and_send(*order[3])

    last = (sum_ref, all_ref, sends, recvs)
    everyone(*last).wait_recv()
    lo, hi = (jnp.sum(all_ref[h * 8 : h * 8 + 8], axis=0) for h in range(2))
    odd = lane_block(lo.shape, 16) == 1
    res_ref[0] = jnp.where(odd, pltpu.roll(hi, 16, 1), lo)
    res_ref[1] = jnp.where(odd, hi, pltpu.roll(lo, 112, 1))
    for j in range(4):
        for c in range(2):
            out_ref[j, c] = res_ref[c, pl.ds(j, 16, stride=4), :]

    for group in (first, second(3), last):
        everyone(*group).wait_send()
    for mc in range(4):
        to_x(mc, 0).wait_send()
        to_x(mc, 1).wait_send()
        to_z(mc).wait_send()
        passed(mc).wait_send()
        to_mate(mc // 2, mc % 2).wait_send()


DMA = pltpu.SemaphoreType.DMA


def on_device(samples, bins, offsets):
    chunk = pltpu.VMEM((16, 4, 2, 8, 128), F32)
    quarters = pltpu.VMEM((4, 16, 2, 8, 128), F32)
    sixteen = pltpu.VMEM((16, 64, 128), F32)
    eighths = pltpu.VMEM((2, 8, 64, 128), F32)
    return pl.pallas_call(
        kernel,
        out_shape=jax.ShapeDtypeStruct((4, 2, 16, 128), F32),
        in_specs=[HBM] * 5,
        out_specs=VMEM,
        scratch_shapes=[
            pltpu.VMEM((1, ALPHAS), jnp.int32),
            pltpu.VMEM((1, ALPHAS), jnp.int32),
            pltpu.VMEM((2, 16, 32, 128), F32),
            pltpu.VMEM((2, 256, 256), BF16),
            pltpu.VMEM((2, 2 * BLOCKS, BLOCKS), BF16),
            pltpu.VMEM((512, 256), F32),
            chunk, chunk, quarters, quarters,
            pltpu.VMEM((4, 4, 16, 2, 8, 128), F32),
            pltpu.VMEM((4, 16, 2, 8, 128), F32),
            pltpu.VMEM((2, 128, 256), BF16),
            pltpu.VMEM((32, 256, 128), BF16),
            pltpu.VMEM((32, 256, 128), BF16),
            pltpu.VMEM((2, 2, 8, 64, 128), F32),
            eighths, sixteen, sixteen,
            pltpu.VMEM((2, 64, 128), F32),
            DMA((5,)), DMA, DMA, DMA((4,)), DMA((4,)),
            DMA((2, 4)), DMA((2, 4)), DMA((4,)), DMA((4,)), DMA((4,)), DMA((4,)),
            DMA((4,)), DMA((4,)), DMA, DMA,
        ],
        compiler_params=pltpu.CompilerParams(
            vmem_limit_bytes=60 * 2**20, collective_id=0, has_side_effects=True
        ),
        name="coherence",
    )(samples, bins.reshape(1, -1), offsets.reshape(1, -1), channel_table(), block_table())


def solution(mesh):
    finer = Mesh(mesh.devices.reshape(4, 2, mesh.shape["chan"]), ("x", "z", "chan"))
    sensor = ("x", "z")
    return jax.shard_map(
        on_device,
        mesh=finer,
        in_specs=(P(None, sensor, "chan", None), P(), P()),
        out_specs=P("chan", None, sensor, None),
        check_vma=False,
    )
```

```python
import math

import jax
import jax.numpy as jnp
import ml_dtypes
import numpy as np
from jax import lax
from jax.experimental import pallas as pl
from jax.experimental.pallas import tpu as pltpu
from jax.sharding import Mesh
from jax.sharding import PartitionSpec as P

CHANNELS = 128
BLOCKS = 512
ALPHAS = 64
SHIFTS = 8
FLOOR = 0.1
F32 = jnp.float32
BF16 = jnp.bfloat16
VMEM = pl.BlockSpec(memory_space=pltpu.VMEM)
HBM = pl.BlockSpec(memory_space=pltpu.HBM)


def halves(table):
    high = table.astype(ml_dtypes.bfloat16)
    low = (table - high.astype(np.float64)).astype(ml_dtypes.bfloat16)
    return np.stack([high, low])


def channel_table():
    n = np.arange(CHANNELS)
    window = 0.5 - 0.5 * np.cos(2 * np.pi * n / CHANNELS)
    angle = 2 * np.pi * (n[:, None] * n[None, :] % CHANNELS) / CHANNELS
    cosine = window[:, None] * np.cos(angle) / math.sqrt(CHANNELS)
    sine = window[:, None] * np.sin(angle) / math.sqrt(CHANNELS)
    return halves(np.block([[cosine, -sine], [sine, cosine]]))


def half_order():
    return np.arange(BLOCKS // 2).reshape(8, 4, 8).transpose(1, 0, 2).reshape(-1)


def block_table():
    n = half_order()
    angle = 4 * np.pi * (n[:, None] * n[None, :] % (BLOCKS // 2)) / BLOCKS
    return halves(np.concatenate([np.cos(angle), np.sin(angle)], 0) / math.sqrt(BLOCKS))


def twiddles():
    angle = 2 * np.pi * half_order()[:, None] / BLOCKS * np.ones((1, 128))
    sign = np.where(np.arange(128) < 64, 1.0, -1.0)
    return np.stack([np.cos(angle), np.sin(angle) * sign]).astype(np.float32)


def split(x):
    high = x.astype(BF16)
    return high, (x - high.astype(F32)).astype(BF16)


def dot3(a, b, dims):
    def one(u, v):
        return lax.dot_general(u, v, (dims, ((), ())), preferred_element_type=F32)

    rows = a[0].shape[0]
    top = one(jnp.concatenate(a, 0), b[0])
    return top[:rows] + (top[rows:] + one(a[0], b[1]))


def lane_block(shape, width):
    return lax.broadcasted_iota(jnp.int32, shape, len(shape) - 1) // width % 2


def swap_blocks(tiles):
    tiles = list(tiles)
    for bit in (1, 2, 4, 8):
        width = 8 * bit
        upper = lane_block(tiles[0].shape, width) == 1
        for i in range(16):
            if i & bit:
                continue
            a, b = tiles[i], tiles[i | bit]
            axis = a.ndim - 1
            tiles[i] = jnp.where(upper, pltpu.roll(b, width, axis), a)
            tiles[i | bit] = jnp.where(upper, b, pltpu.roll(a, 128 - width, axis))
    return tiles


def remote(src, dst, send, recv, **where):
    return pltpu.make_async_remote_copy(
        src_ref=src,
        dst_ref=dst,
        send_sem=send,
        recv_sem=recv,
        device_id=where,
        device_id_type=pl.DeviceIdType.MESH,
    )


def phase_rows(bins_ref, offsets_ref, first):
    row = lax.broadcasted_iota(jnp.int32, (ALPHAS, ALPHAS), 0)
    same = row == lax.broadcasted_iota(jnp.int32, (ALPHAS, ALPHAS), 1)

    def column(ref):
        return jnp.sum(jnp.where(same, ref[...].astype(F32), 0.0), 1, keepdims=True)

    lane = lax.broadcasted_iota(jnp.int32, (ALPHAS, 256), 1)
    turns = column(bins_ref).astype(jnp.int32) * (first + lane // 8) % BLOCKS
    angle = turns.astype(F32) * (2.0 * math.pi / BLOCKS)
    chosen = column(offsets_ref).astype(jnp.int32) == lane % 8
    both = [jnp.where(chosen, f(angle) * (1.0 / 256.0), 0.0) for f in (jnp.cos, jnp.sin)]
    return split(jnp.concatenate(both, 0))


def kernel(
    x_hbm, bins_hbm, offsets_hbm, ctable_hbm, table_hbm, twiddle_hbm, out_ref,
    bins_ref, offsets_ref, x_ref, ctable_ref, table_ref, twiddle_ref, mid_ref, made_ref, got_ref, back_ref, land_ref,
    right_ref, other_ref, phase_ref, high_ref, low_ref, high2_ref, low2_ref, left_ref,
    part_ref, pair_ref, sum_ref, all_ref, part2_ref, pair2_ref, sum2_ref, all2_ref, res_ref, late_ref,
    load_sem, send1, recv1, send2, recv2, sendx, recvx, sendf, recvf, sendz, recvz,
    sendp, recvp, sends, recvs,
):
    chan, x, z = lax.axis_index("chan"), lax.axis_index("x"), lax.axis_index("z")
    core, place = lax.rem(chan, 2), chan // 2
    mate = chan + 1 - 2 * core
    after, before = lax.rem(x + 1, 4), lax.rem(x + 3, 4)

    loads = [
        pltpu.make_async_copy(src, dst, load_sem.at[i])
        for i, (src, dst) in enumerate(
            [
                (x_hbm, x_ref),
                (ctable_hbm, ctable_ref),
                (table_hbm, table_ref),
                (bins_hbm, bins_ref),
                (offsets_hbm, offsets_ref),
                (twiddle_hbm, twiddle_ref),
            ]
        )
    ]
    for load in loads:
        load.start()

    barrier = pltpu.get_barrier_semaphore()
    peers = [{"chan": lax.rem(chan + o, 16)} for o in range(1, 16)]
    peers += [{"x": after}, {"x": before}]
    peers += [{"z": 1 - z, "chan": lax.rem(place + o, 8) * 2 + core} for o in range(8)]
    for where in peers:
        pl.semaphore_signal(barrier, device_id=where, device_id_type=pl.DeviceIdType.MESH)

    loads[0].wait()
    loads[1].wait()
    both = jnp.concatenate([x_ref[0].reshape(512, 128), x_ref[1].reshape(512, 128)], 1)
    mid_ref[...] = dot3(split(both), (ctable_ref[0], ctable_ref[1]), ((1,), (0,)))
    def tiles_of(h):
        for mc in range(4):
            tiles = [
                mid_ref[s * 32 + mc * 8 : s * 32 + mc * 8 + 8, c * 128 : c * 128 + 128]
                for c in range(2)
                for s in range(h * 8, h * 8 + 8)
            ]
            for dest, tile in enumerate(swap_blocks(tiles)):
                made_ref[h, dest, mc] = tile

    def exchange(src, dst, send, recv, o):
        peer = lax.rem(chan + o, 16)
        return remote(src.at[peer], dst.at[chan], send, recv, chan=peer)

    def everyone(src, dst, send, recv):
        most = pl.ds(0, 15)
        return remote(src.at[most], dst.at[most], send, recv, chan=mate)

    def first(h):
        return made_ref.at[h], got_ref.at[h], send1.at[h], recv1.at[h]

    def second(h):
        return back_ref.at[h], land_ref.at[h], send2.at[h], recv2.at[h]

    def send_all(group):
        @pl.loop(1, 16)
        def _(o):
            exchange(*group, o).start()

    tiles_of(0)
    pl.semaphore_wait(barrier, len(peers))
    send_all(first(0))
    tiles_of(1)
    everyone(*first(0)).wait_send()
    send_all(first(1))
    for h in range(2):
        got_ref[h, chan] = made_ref[h, chan]
    for load in loads[2:]:
        load.wait()
    phase_ref[0], phase_ref[1] = phase_rows(bins_ref, offsets_ref, chan * 32)

    first_part = lax.broadcasted_iota(jnp.int32, (BLOCKS // 2, 256), 1) % 128 < 64

    def turned(u):
        return jnp.concatenate([pltpu.roll(u[:, i : i + 128], 64, 1) for i in (0, 128)], 1)

    def transform(v):
        u = dot3((table_ref[0], table_ref[1]), split(v), ((1,), (0,)))
        return u[:256], turned(u[256:])

    for h in range(2):
        everyone(*first(h)).wait_recv()
        low, high = (
            jnp.concatenate([got_ref[h, i : i + 8, mc].reshape(64, 128) for mc in range(4)], 0)
            for i in (0, 8)
        )
        odd = low - high
        odd = odd * twiddle_ref[0] + pltpu.roll(odd, 64, 1) * twiddle_ref[1]
        cosine, sine = transform(jnp.concatenate([low + high, odd], 1))
        spectra = cosine + jnp.where(first_part, sine, -sine)
        power = spectra * spectra
        power = power + turned(power)
        cosine, sine = transform(spectra / jnp.sqrt(power + FLOOR))
        blocks = cosine - jnp.where(first_part, sine, -sine)
        even, odd = blocks[:, :128], blocks[:, 128:]
        odd = odd * twiddle_ref[0] - pltpu.roll(odd, 64, 1) * twiddle_ref[1]
        for i, half in ((0, even + odd), (8, even - odd)):
            for mc in range(4):
                back_ref[h, i : i + 8, mc] = half[mc * 64 : mc * 64 + 64].reshape(8, 8, 128)
        send_all(second(h))
        land_ref[h, chan] = back_ref[h, chan]

    def eight(i, mc, h):
        return right_ref.at[i, mc, pl.ds(h * 8, 8)]

    def to_x(h, mc, way, incoming=False):
        peer = (after, before)[way ^ incoming]
        at = peer if incoming else x
        return remote(
            eight(x, mc, h), eight(at, mc, h), sendx.at[way, h, mc], recvx.at[way, h, mc], x=peer
        )

    def passed(h, mc, way, incoming=False):
        source, peer = (before, after) if way == 0 else (after, before)
        at = lax.rem(x + 2, 4) if incoming else source
        four = pl.ds(h * 8 + way * 4, 4)
        return remote(
            right_ref.at[source, mc, four], right_ref.at[at, mc, four],
            sendf.at[way, h, mc], recvf.at[way, h, mc], x=peer,
        )

    def to_z(h, mc):
        return remote(
            eight(x, mc, h), other_ref.at[mc, pl.ds(h * 8, 8)], sendz.at[h, mc], recvz.at[h, mc], z=1 - z
        )

    def turn(h, mc):
        tiles = swap_blocks([land_ref[h, i, mc] for i in range(16)])
        for i, tile in enumerate(tiles):
            right_ref[x, mc, h * 8 + i % 8, i // 8] = tile
        to_x(h, mc, 0).start()
        to_x(h, mc, 1).start()
        to_z(h, mc).start()

    def forward(h, mc):
        for way in range(2):
            to_x(h, mc, way, True).wait_recv()
            passed(h, mc, way).start()

    far = lax.rem(x + 2, 4)

    def shifted(mc, r):
        left = []
        for c in range(2):
            rows = []
            for a in range(32):
                if a < 16:
                    row = right_ref[x, mc, a, c, pl.ds(r, 1), :]
                else:
                    row = other_ref[mc, a - 16, c, pl.ds(r, 1), :]
                rows.append(pltpu.roll(jnp.broadcast_to(row, (8, 128)), 0, 1, stride=1, stride_axis=0))
            left.append(jnp.concatenate(rows, 0))
        return split(jnp.concatenate(left, 1))

    def facing(i, mc, r):
        tall = right_ref.at[i, mc].reshape(256, 128)
        real, imag = (tall[pl.ds(r + c * 8, 16, stride=16), :] for c in range(2))
        return [jnp.concatenate([real, imag], 1), jnp.concatenate([-imag, real], 1)]

    def product(mc, r, part):
        m = mc * 8 + r
        if part == 0:
            left = shifted(mc, r)
            left_ref[0, m], left_ref[1, m] = left
            rows = []
            for i in range(4):
                rows += facing(jnp.where(far == i, x, i), mc, r)
        else:
            left = left_ref[0, m], left_ref[1, m]
            rows = facing(far, mc, r) * 4
        out = dot3(left, split(jnp.concatenate(rows, 0)), ((1,), (1,)))
        if part == 0:
            return out.reshape(32, 8, 128)
        out = out.reshape(8, 4, 8, 128)
        group = lax.broadcasted_iota(jnp.int32, (8, 8, 128), 2) // 32
        tiles = out[:, 3]
        for i in range(3):
            tiles = jnp.where(group == i, out[:, i], tiles)
        return tiles

    def products(mc, part, high_ref, low_ref):
        def step(i, carry):
            for half in range(2):
                r = i * 4 + half * 2
                tiles = jnp.concatenate([product(mc, r, part), product(mc, r + 1, part)], 1)
                rows = pl.ds(pl.multiple_of(mc * 64 + r * 8, 16), 16)
                high_ref[:, rows, :], low_ref[:, rows, :] = split(tiles)
            return carry

        lax.fori_loop(0, 2, step, 0)

    for h in range(2):
        everyone(*second(h)).wait_recv()
        for mc in range(4):
            turn(h, mc)
    for mc in range(4):
        for h in range(2):
            forward(h, mc)
            to_z(h, mc).wait_recv()
        products(mc, 0, high_ref, low_ref)

    low_rows = lax.broadcasted_iota(jnp.int32, (8, 128), 0) < 4

    def one_pair(refs, out_ref, half, pair):
        a = half * (refs[0].shape[0] // 2) + pair * 2
        both = tuple(jnp.concatenate([ref[a], ref[a + 1]], 1) for ref in refs)
        t = dot3((phase_ref[0], phase_ref[1]), both, ((1,), (0,)))
        gs = []
        for i in range(2):
            cosine, sine = t[:64, i * 128 : i * 128 + 128], t[64:, i * 128 : i * 128 + 128]
            odd = lane_block(sine.shape, 16) == 1
            gs.append(cosine + jnp.where(odd, -pltpu.roll(sine, 16, 1), pltpu.roll(sine, 112, 1)))
        row = pl.ds(pair * 8, 8)
        for t8 in range(8):
            a0, a1 = (g[t8 * 8 : t8 * 8 + 8] for g in gs)
            out_ref[0, half, t8, row, :] = jnp.where(low_rows, a0, pltpu.roll(a1, 4, 0))
            out_ref[1, half, t8, row, :] = jnp.where(low_rows, pltpu.roll(a0, 4, 0), a1)

    def to_mate(part, half):
        return remote(
            parts[part].at[1 - core, half], pairs[part].at[half],
            sendp.at[part, half], recvp.at[part, half], chan=mate,
        )

    def last(part):
        return sums[part], alls[part], sends.at[part], recvs.at[part]

    def spread(part, o):
        peer_z, peer = lax.rem(z + o // 8, 2), lax.rem(place + lax.rem(o, 8), 8)
        src, dst, send, recv = last(part)
        return remote(
            src.at[o // 8 * 8 + peer], dst.at[z * 8 + place], send, recv,
            z=peer_z, chan=peer * 2 + core,
        )

    def add_and_send(part, half):
        to_mate(part, half).wait_recv()
        sums[part][half * 8 : half * 8 + 8] = parts[part][core, half] + pairs[part][half]

        @pl.loop(8 if half else 1, 16 if half else 8)
        def _(o):
            spread(part, o).start()

        if not half:
            alls[part][z * 8 + place] = sums[part][place]

    parts, pairs = (part_ref, part2_ref), (pair_ref, pair2_ref)
    sums, alls = (sum_ref, sum2_ref), (all_ref, all2_ref)
    for half in (1, 0):
        for pair in range(8):
            one_pair((high_ref, low_ref), part_ref, half, pair)
        to_mate(0, half).start()
    for half in (1, 0):
        add_and_send(0, half)
    for mc in range(4):
        for h in range(2):
            for way in range(2):
                passed(h, mc, way, True).wait_recv()
        products(mc, 1, high2_ref, low2_ref)
    for half in (1, 0):
        for pair in range(2):
            one_pair((high2_ref, low2_ref), part2_ref, half, pair)
        to_mate(1, half).start()
    for half in (1, 0):
        add_and_send(1, half)

    everyone(*last(0)).wait_recv()
    for h in range(2):
        res_ref[h] = jnp.sum(all_ref[h * 8 : h * 8 + 8], axis=0)
    everyone(*last(1)).wait_recv()
    for h in range(2):
        late = jnp.sum(all2_ref[h * 8 : h * 8 + 8], axis=0)
        for i in range(4):
            there = pltpu.roll(late, lax.rem(far + 4 - i, 4) * 32, 1)
            for g in range(4):
                late_ref[h, g * 16 + i * 4 : g * 16 + i * 4 + 4] = there[g * 4 : g * 4 + 4]
    missing = lax.broadcasted_iota(jnp.int32, (64, 128), 1) // 32 == far
    lo, hi = (jnp.where(missing, late_ref[h], res_ref[h]) for h in range(2))
    odd = lane_block(lo.shape, 16) == 1
    res_ref[0] = jnp.where(odd, pltpu.roll(hi, 16, 1), lo)
    res_ref[1] = jnp.where(odd, hi, pltpu.roll(lo, 112, 1))
    for j in range(4):
        for c in range(2):
            out_ref[j, c] = res_ref[c, pl.ds(j, 16, stride=4), :]

    for group in (first(1), second(0), second(1), last(0), last(1)):
        everyone(*group).wait_send()
    for mc in range(4):
        for h in range(2):
            for way in range(2):
                to_x(h, mc, way).wait_send()
                passed(h, mc, way).wait_send()
            to_z(h, mc).wait_send()
        to_mate(mc // 2, mc % 2).wait_send()


DMA = pltpu.SemaphoreType.DMA


def summed(rows):
    shapes = [(2, 2, 8), (2, 8), (16,), (16,)]
    return [pltpu.VMEM((*shape, rows, 128), F32) for shape in shapes]


def on_device(samples, bins, offsets):
    chunk = pltpu.VMEM((2, 16, 4, 8, 128), F32)
    sixteen = pltpu.VMEM((16, 64, 128), F32)
    return pl.pallas_call(
        kernel,
        out_shape=jax.ShapeDtypeStruct((4, 2, 16, 128), F32),
        in_specs=[HBM] * 6,
        out_specs=VMEM,
        scratch_shapes=[
            pltpu.VMEM((1, ALPHAS), jnp.int32),
            pltpu.VMEM((1, ALPHAS), jnp.int32),
            pltpu.VMEM((2, 16, 32, 128), F32),
            pltpu.VMEM((2, 256, 256), BF16),
            pltpu.VMEM((2, BLOCKS, BLOCKS // 2), BF16),
            pltpu.VMEM((2, BLOCKS // 2, 128), F32),
            pltpu.VMEM((512, 256), F32),
            chunk, chunk, chunk, chunk,
            pltpu.VMEM((4, 4, 16, 2, 8, 128), F32),
            pltpu.VMEM((4, 16, 2, 8, 128), F32),
            pltpu.VMEM((2, 128, 256), BF16),
            pltpu.VMEM((32, 256, 128), BF16),
            pltpu.VMEM((32, 256, 128), BF16),
            pltpu.VMEM((8, 256, 128), BF16),
            pltpu.VMEM((8, 256, 128), BF16),
            pltpu.VMEM((2, 32, 256, 256), BF16),
            *summed(64),
            *summed(16),
            pltpu.VMEM((2, 64, 128), F32),
            pltpu.VMEM((2, 64, 128), F32),
            DMA((6,)), DMA((2,)), DMA((2,)), DMA((2,)), DMA((2,)),
            DMA((2, 2, 4)), DMA((2, 2, 4)), DMA((2, 2, 4)), DMA((2, 2, 4)), DMA((2, 4)), DMA((2, 4)),
            DMA((2, 2)), DMA((2, 2)), DMA((2,)), DMA((2,)),
        ],
        compiler_params=pltpu.CompilerParams(
            vmem_limit_bytes=60 * 2**20, collective_id=0, has_side_effects=True
        ),
        name="coherence",
    )(samples, bins.reshape(1, -1), offsets.reshape(1, -1), channel_table(), block_table(), twiddles())


def solution(mesh):
    finer = Mesh(mesh.devices.reshape(4, 2, mesh.shape["chan"]), ("x", "z", "chan"))
    sensor = ("x", "z")
    return jax.shard_map(
        on_device,
        mesh=finer,
        in_specs=(P(None, sensor, "chan", None), P(), P()),
        out_specs=P("chan", None, sensor, None),
        check_vma=False,
    )
```

```python
import math

import jax
import jax.numpy as jnp
import ml_dtypes
import numpy as np
from jax import lax
from jax.experimental import pallas as pl
from jax.experimental.pallas import tpu as pltpu
from jax.sharding import Mesh
from jax.sharding import PartitionSpec as P

CHANNELS = 128
BLOCKS = 512
ALPHAS = 64
SHIFTS = 8
FLOOR = 0.1
F32 = jnp.float32
BF16 = jnp.bfloat16
VMEM = pl.BlockSpec(memory_space=pltpu.VMEM)
HBM = pl.BlockSpec(memory_space=pltpu.HBM)


def halves(table):
    high = table.astype(ml_dtypes.bfloat16)
    low = (table - high.astype(np.float64)).astype(ml_dtypes.bfloat16)
    return np.stack([high, low])


def channel_table():
    n = np.arange(CHANNELS)
    window = 0.5 - 0.5 * np.cos(2 * np.pi * n / CHANNELS)
    angle = 2 * np.pi * (n[:, None] * n[None, :] % CHANNELS) / CHANNELS
    cosine = window[:, None] * np.cos(angle) / math.sqrt(CHANNELS)
    sine = window[:, None] * np.sin(angle) / math.sqrt(CHANNELS)
    return halves(np.block([[cosine, -sine], [sine, cosine]]))


def half_order():
    return np.arange(BLOCKS // 2).reshape(8, 4, 8).transpose(1, 0, 2).reshape(-1)


def block_table():
    n = half_order()
    angle = 4 * np.pi * (n[:, None] * n[None, :] % (BLOCKS // 2)) / BLOCKS
    return halves(np.concatenate([np.cos(angle), np.sin(angle)], 0) / math.sqrt(BLOCKS))


def twiddles():
    angle = 2 * np.pi * half_order()[:, None] / BLOCKS * np.ones((1, 128))
    sign = np.where(np.arange(128) < 64, 1.0, -1.0)
    return np.stack([np.cos(angle), np.sin(angle) * sign]).astype(np.float32)


def split(x):
    high = x.astype(BF16)
    return high, (x - high.astype(F32)).astype(BF16)


def dot3(a, b, dims):
    def one(u, v):
        return lax.dot_general(u, v, (dims, ((), ())), preferred_element_type=F32)

    rows = a[0].shape[0]
    top = one(jnp.concatenate(a, 0), b[0])
    return top[:rows] + (top[rows:] + one(a[0], b[1]))


def lane_block(shape, width):
    return lax.broadcasted_iota(jnp.int32, shape, len(shape) - 1) // width % 2


def swap_blocks(tiles):
    tiles = list(tiles)
    for bit in (1, 2, 4, 8):
        width = 8 * bit
        upper = lane_block(tiles[0].shape, width) == 1
        for i in range(16):
            if i & bit:
                continue
            a, b = tiles[i], tiles[i | bit]
            axis = a.ndim - 1
            tiles[i] = jnp.where(upper, pltpu.roll(b, width, axis), a)
            tiles[i | bit] = jnp.where(upper, b, pltpu.roll(a, 128 - width, axis))
    return tiles


def remote(src, dst, send, recv, **where):
    return pltpu.make_async_remote_copy(
        src_ref=src,
        dst_ref=dst,
        send_sem=send,
        recv_sem=recv,
        device_id=where,
        device_id_type=pl.DeviceIdType.MESH,
    )


def ring(d):
    return min(d, 4 - d)


OWNERS = sorted(
    ((d, y, c) for d in range(2) for y in range(4) for c in range(2) if d + y + c),
    key=lambda step: -(2 * step[0] + ring(step[1])),
)
PLANE = sorted(
    ((d, y, lo) for d in range(2) for y in range(4) for lo in range(2) if d + y + lo),
    key=lambda step: -(ring(2 * step[0] + step[2]) + ring(step[1])),
)


def phase_rows(bins_ref, offsets_ref, first):
    row = lax.broadcasted_iota(jnp.int32, (ALPHAS, ALPHAS), 0)
    same = row == lax.broadcasted_iota(jnp.int32, (ALPHAS, ALPHAS), 1)

    def column(ref):
        return jnp.sum(jnp.where(same, ref[...].astype(F32), 0.0), 1, keepdims=True)

    lane = lax.broadcasted_iota(jnp.int32, (ALPHAS, 256), 1)
    turns = column(bins_ref).astype(jnp.int32) * (first + lane // 8) % BLOCKS
    angle = turns.astype(F32) * (2.0 * math.pi / BLOCKS)
    chosen = column(offsets_ref).astype(jnp.int32) == lane % 8
    both = [jnp.where(chosen, f(angle) * (1.0 / 256.0), 0.0) for f in (jnp.cos, jnp.sin)]
    return split(jnp.concatenate(both, 0))


def kernel(
    x_hbm, bins_hbm, offsets_hbm, ctable_hbm, table_hbm, twiddle_hbm, out_ref,
    bins_ref, offsets_ref, x_ref, ctable_ref, table_ref, twiddle_ref, mid_ref, made_ref, got_ref, back_ref, land_ref,
    right_ref, other_ref, phase_ref, high_ref, low_ref, high2_ref, low2_ref, left_ref,
    part_ref, pair_ref, sum_ref, all_ref, part2_ref, pair2_ref, sum2_ref, all2_ref, res_ref, late_ref,
    load_sem, send1, recv1, send2, recv2, sendx, recvx, sendf, recvf, sendz, recvz,
    sendp, recvp, sends, recvs,
):
    chan, x, z = lax.axis_index("chan"), lax.axis_index("x"), lax.axis_index("z")
    core, place = lax.rem(chan, 2), chan // 2
    mate = chan + 1 - 2 * core
    after, before = lax.rem(x + 1, 4), lax.rem(x + 3, 4)

    loads = [
        pltpu.make_async_copy(src, dst, load_sem.at[i])
        for i, (src, dst) in enumerate(
            [
                (x_hbm, x_ref),
                (ctable_hbm, ctable_ref),
                (table_hbm, table_ref),
                (bins_hbm, bins_ref),
                (offsets_hbm, offsets_ref),
                (twiddle_hbm, twiddle_ref),
            ]
        )
    ]
    for load in loads:
        load.start()

    barrier = pltpu.get_barrier_semaphore()
    peers = [{"chan": lax.rem(chan + o, 16)} for o in range(1, 16)]
    peers += [{"x": after}, {"x": before}]
    peers += [{"z": 1 - z}]
    for where in peers:
        pl.semaphore_signal(barrier, device_id=where, device_id_type=pl.DeviceIdType.MESH)

    loads[0].wait()
    loads[1].wait()
    both = jnp.concatenate([x_ref[0].reshape(512, 128), x_ref[1].reshape(512, 128)], 1)
    mid_ref[...] = dot3(split(both), (ctable_ref[0], ctable_ref[1]), ((1,), (0,)))
    def tiles_of(h):
        for mc in range(4):
            tiles = [
                mid_ref[s * 32 + mc * 8 : s * 32 + mc * 8 + 8, c * 128 : c * 128 + 128]
                for c in range(2)
                for s in range(h * 8, h * 8 + 8)
            ]
            for dest, tile in enumerate(swap_blocks(tiles)):
                made_ref[h, dest, mc] = tile

    def owner(d, y, c):
        return lax.rem(place + d * 4, 8) // 4 * 8 + lax.rem(lax.rem(place, 4) + y, 4) * 2 + (core + c) % 2

    def exchange(src, dst, send, recv, step):
        peer = owner(*step)
        return remote(src.at[peer], dst.at[chan], send, recv, chan=peer)

    def everyone(src, dst, send, recv):
        most = pl.ds(0, 15)
        return remote(src.at[most], dst.at[most], send, recv, chan=mate)

    def first(h):
        return made_ref.at[h], got_ref.at[h], send1.at[h], recv1.at[h]

    def second(h):
        return back_ref.at[h], land_ref.at[h], send2.at[h], recv2.at[h]

    def send_all(group):
        for step in OWNERS:
            exchange(*group, step).start()

    tiles_of(0)
    pl.semaphore_wait(barrier, len(peers))
    send_all(first(0))
    tiles_of(1)
    everyone(*first(0)).wait_send()
    send_all(first(1))
    for h in range(2):
        got_ref[h, chan] = made_ref[h, chan]
    for load in loads[2:]:
        load.wait()
    phase_ref[0], phase_ref[1] = phase_rows(bins_ref, offsets_ref, chan * 32)

    first_part = lax.broadcasted_iota(jnp.int32, (BLOCKS // 2, 256), 1) % 128 < 64

    def turned(u):
        return jnp.concatenate([pltpu.roll(u[:, i : i + 128], 64, 1) for i in (0, 128)], 1)

    def transform(v):
        u = dot3((table_ref[0], table_ref[1]), split(v), ((1,), (0,)))
        return u[:256], turned(u[256:])

    for h in range(2):
        everyone(*first(h)).wait_recv()
        low, high = (
            jnp.concatenate([got_ref[h, i : i + 8, mc].reshape(64, 128) for mc in range(4)], 0)
            for i in (0, 8)
        )
        odd = low - high
        odd = odd * twiddle_ref[0] + pltpu.roll(odd, 64, 1) * twiddle_ref[1]
        cosine, sine = transform(jnp.concatenate([low + high, odd], 1))
        spectra = cosine + jnp.where(first_part, sine, -sine)
        power = spectra * spectra
        power = power + turned(power)
        cosine, sine = transform(spectra / jnp.sqrt(power + FLOOR))
        blocks = cosine - jnp.where(first_part, sine, -sine)
        even, odd = blocks[:, :128], blocks[:, 128:]
        odd = odd * twiddle_ref[0] - pltpu.roll(odd, 64, 1) * twiddle_ref[1]
        for i, half in ((0, even + odd), (8, even - odd)):
            for mc in range(4):
                back_ref[h, i : i + 8, mc] = half[mc * 64 : mc * 64 + 64].reshape(8, 8, 128)
        send_all(second(h))
        land_ref[h, chan] = back_ref[h, chan]

    def eight(i, mc, h):
        return right_ref.at[i, mc, pl.ds(h * 8, 8)]

    def to_x(h, mc, way, incoming=False):
        peer = (after, before)[way ^ incoming]
        at = peer if incoming else x
        return remote(
            eight(x, mc, h), eight(at, mc, h), sendx.at[way, h, mc], recvx.at[way, h, mc], x=peer
        )

    def passed(h, mc, way, incoming=False):
        source, peer = (before, after) if way == 0 else (after, before)
        at = lax.rem(x + 2, 4) if incoming else source
        four = pl.ds(h * 8 + way * 4, 4)
        return remote(
            right_ref.at[source, mc, four], right_ref.at[at, mc, four],
            sendf.at[way, h, mc], recvf.at[way, h, mc], x=peer,
        )

    def to_z(h, mc):
        return remote(
            eight(x, mc, h), other_ref.at[mc, pl.ds(h * 8, 8)], sendz.at[h, mc], recvz.at[h, mc], z=1 - z
        )

    def turn(h, mc):
        tiles = swap_blocks([land_ref[h, i, mc] for i in range(16)])
        for i, tile in enumerate(tiles):
            right_ref[x, mc, h * 8 + i % 8, i // 8] = tile
        to_x(h, mc, 0).start()
        to_x(h, mc, 1).start()
        to_z(h, mc).start()

    def forward(h, mc):
        for way in range(2):
            to_x(h, mc, way, True).wait_recv()
            passed(h, mc, way).start()

    far = lax.rem(x + 2, 4)

    def shifted(mc, r):
        left = []
        for c in range(2):
            rows = []
            for a in range(32):
                if a < 16:
                    row = right_ref[x, mc, a, c, pl.ds(r, 1), :]
                else:
                    row = other_ref[mc, a - 16, c, pl.ds(r, 1), :]
                rows.append(pltpu.roll(jnp.broadcast_to(row, (8, 128)), 0, 1, stride=1, stride_axis=0))
            left.append(jnp.concatenate(rows, 0))
        return split(jnp.concatenate(left, 1))

    def facing(i, mc, r):
        tall = right_ref.at[i, mc].reshape(256, 128)
        real, imag = (tall[pl.ds(r + c * 8, 16, stride=16), :] for c in range(2))
        return [jnp.concatenate([real, imag], 1), jnp.concatenate([-imag, real], 1)]

    def product(mc, r, part):
        m = mc * 8 + r
        if part == 0:
            left = shifted(mc, r)
            left_ref[0, m], left_ref[1, m] = left
            rows = []
            for i in range(4):
                rows += facing(jnp.where(far == i, x, i), mc, r)
        else:
            left = left_ref[0, m], left_ref[1, m]
            rows = facing(far, mc, r) * 4
        out = dot3(left, split(jnp.concatenate(rows, 0)), ((1,), (1,)))
        if part == 0:
            return out.reshape(32, 8, 128)
        out = out.reshape(8, 4, 8, 128)
        group = lax.broadcasted_iota(jnp.int32, (8, 8, 128), 2) // 32
        tiles = out[:, 3]
        for i in range(3):
            tiles = jnp.where(group == i, out[:, i], tiles)
        return tiles

    def products(mc, part, high_ref, low_ref):
        def step(i, carry):
            for half in range(2):
                r = i * 4 + half * 2
                tiles = jnp.concatenate([product(mc, r, part), product(mc, r + 1, part)], 1)
                rows = pl.ds(pl.multiple_of(mc * 64 + r * 8, 16), 16)
                high_ref[:, rows, :], low_ref[:, rows, :] = split(tiles)
            return carry

        lax.fori_loop(0, 2, step, 0)

    for h in range(2):
        everyone(*second(h)).wait_recv()
        for mc in range(4):
            turn(h, mc)
    @pl.loop(0, 4)
    def _(mc):
        for h in range(2):
            forward(h, mc)
            to_z(h, mc).wait_recv()
        products(mc, 0, high_ref, low_ref)

    low_rows = lax.broadcasted_iota(jnp.int32, (8, 128), 0) < 4

    def one_pair(refs, out_ref, half, pair):
        a = half * (refs[0].shape[0] // 2) + pair * 2
        both = tuple(jnp.concatenate([ref[a], ref[a + 1]], 1) for ref in refs)
        t = dot3((phase_ref[0], phase_ref[1]), both, ((1,), (0,)))
        gs = []
        for i in range(2):
            cosine, sine = t[:64, i * 128 : i * 128 + 128], t[64:, i * 128 : i * 128 + 128]
            odd = lane_block(sine.shape, 16) == 1
            gs.append(cosine + jnp.where(odd, -pltpu.roll(sine, 16, 1), pltpu.roll(sine, 112, 1)))
        row = pl.ds(pair * 8, 8)
        for t8 in range(8):
            a0, a1 = (g[t8 * 8 : t8 * 8 + 8] for g in gs)
            out_ref[0, half, t8, row, :] = jnp.where(low_rows, a0, pltpu.roll(a1, 4, 0))
            out_ref[1, half, t8, row, :] = jnp.where(low_rows, pltpu.roll(a0, 4, 0), a1)

    def to_mate(part, half):
        return remote(
            parts[part].at[1 - core, half], pairs[part].at[half],
            sendp.at[part, half], recvp.at[part, half], chan=mate,
        )

    def last(part):
        return sums[part], alls[part], sends.at[part], recvs.at[part]

    def spread(part, d, y, lo):
        peer_z, peer = (z + lo) % 2, owner(d, y, 0) // 2
        src, dst, send, recv = last(part)
        return remote(
            src.at[lo * 8 + peer], dst.at[z * 8 + place], send, recv,
            z=peer_z, chan=peer * 2 + core,
        )

    def add_and_send(part, half):
        to_mate(part, half).wait_recv()
        sums[part][half * 8 : half * 8 + 8] = parts[part][core, half] + pairs[part][half]

        for step in PLANE:
            if step[2] == half:
                spread(part, *step).start()

        if not half:
            alls[part][z * 8 + place] = sums[part][place]

    parts, pairs = (part_ref, part2_ref), (pair_ref, pair2_ref)
    sums, alls = (sum_ref, sum2_ref), (all_ref, all2_ref)
    for half in (1, 0):
        for pair in range(8):
            one_pair((high_ref, low_ref), part_ref, half, pair)
        to_mate(0, half).start()
    for half in (1, 0):
        add_and_send(0, half)
    @pl.loop(0, 4)
    def _(mc):
        for h in range(2):
            for way in range(2):
                passed(h, mc, way, True).wait_recv()
        products(mc, 1, high2_ref, low2_ref)
    for half in (1, 0):
        for pair in range(2):
            one_pair((high2_ref, low2_ref), part2_ref, half, pair)
        to_mate(1, half).start()
    for half in (1, 0):
        add_and_send(1, half)

    for group in (first(1), second(0), second(1), last(0)):
        everyone(*group).wait_send()
    for mc in range(4):
        for h in range(2):
            for way in range(2):
                to_x(h, mc, way).wait_send()
                passed(h, mc, way).wait_send()
            to_z(h, mc).wait_send()
        to_mate(mc // 2, mc % 2).wait_send()
    everyone(*last(0)).wait_recv()
    for h in range(2):
        res_ref[h] = jnp.sum(all_ref[h * 8 : h * 8 + 8], axis=0)
    everyone(*last(1)).wait_recv()
    for h in range(2):
        late = jnp.sum(all2_ref[h * 8 : h * 8 + 8], axis=0)
        for i in range(4):
            there = pltpu.roll(late, lax.rem(far + 4 - i, 4) * 32, 1)
            for g in range(4):
                late_ref[h, g * 16 + i * 4 : g * 16 + i * 4 + 4] = there[g * 4 : g * 4 + 4]
    missing = lax.broadcasted_iota(jnp.int32, (64, 128), 1) // 32 == far
    lo, hi = (jnp.where(missing, late_ref[h], res_ref[h]) for h in range(2))
    odd = lane_block(lo.shape, 16) == 1
    res_ref[0] = jnp.where(odd, pltpu.roll(hi, 16, 1), lo)
    res_ref[1] = jnp.where(odd, hi, pltpu.roll(lo, 112, 1))
    for j in range(4):
        for c in range(2):
            out_ref[j, c] = res_ref[c, pl.ds(j, 16, stride=4), :]

    everyone(*last(1)).wait_send()


DMA = pltpu.SemaphoreType.DMA


def summed(rows):
    shapes = [(2, 2, 8), (2, 8), (16,), (16,)]
    return [pltpu.VMEM((*shape, rows, 128), F32) for shape in shapes]


def on_device(samples, bins, offsets):
    chunk = pltpu.VMEM((2, 16, 4, 8, 128), F32)
    sixteen = pltpu.VMEM((16, 64, 128), F32)
    return pl.pallas_call(
        kernel,
        out_shape=jax.ShapeDtypeStruct((4, 2, 16, 128), F32),
        in_specs=[HBM] * 6,
        out_specs=VMEM,
        scratch_shapes=[
            pltpu.VMEM((1, ALPHAS), jnp.int32),
            pltpu.VMEM((1, ALPHAS), jnp.int32),
            pltpu.VMEM((2, 16, 32, 128), F32),
            pltpu.VMEM((2, 256, 256), BF16),
            pltpu.VMEM((2, BLOCKS, BLOCKS // 2), BF16),
            pltpu.VMEM((2, BLOCKS // 2, 128), F32),
            pltpu.VMEM((512, 256), F32),
            chunk, chunk, chunk, chunk,
            pltpu.VMEM((4, 4, 16, 2, 8, 128), F32),
            pltpu.VMEM((4, 16, 2, 8, 128), F32),
            pltpu.VMEM((2, 128, 256), BF16),
            pltpu.VMEM((32, 256, 128), BF16),
            pltpu.VMEM((32, 256, 128), BF16),
            pltpu.VMEM((8, 256, 128), BF16),
            pltpu.VMEM((8, 256, 128), BF16),
            pltpu.VMEM((2, 32, 256, 256), BF16),
            *summed(64),
            *summed(16),
            pltpu.VMEM((2, 64, 128), F32),
            pltpu.VMEM((2, 64, 128), F32),
            DMA((6,)), DMA((2,)), DMA((2,)), DMA((2,)), DMA((2,)),
            DMA((2, 2, 4)), DMA((2, 2, 4)), DMA((2, 2, 4)), DMA((2, 2, 4)), DMA((2, 4)), DMA((2, 4)),
            DMA((2, 2)), DMA((2, 2)), DMA((2,)), DMA((2,)),
        ],
        compiler_params=pltpu.CompilerParams(
            vmem_limit_bytes=60 * 2**20, collective_id=0, has_side_effects=True
        ),
        name="coherence",
    )(samples, bins.reshape(1, -1), offsets.reshape(1, -1), channel_table(), block_table(), twiddles())


def solution(mesh):
    finer = Mesh(mesh.devices.reshape(4, 2, mesh.shape["chan"]), ("x", "z", "chan"))
    sensor = ("x", "z")
    return jax.shard_map(
        on_device,
        mesh=finer,
        in_specs=(P(None, sensor, "chan", None), P(), P()),
        out_specs=P("chan", None, sensor, None),
        check_vma=False,
    )
```

```python
import math

import jax
import jax.numpy as jnp
import ml_dtypes
import numpy as np
from jax import lax
from jax.experimental import pallas as pl
from jax.experimental.pallas import tpu as pltpu
from jax.sharding import Mesh
from jax.sharding import PartitionSpec as P

CHANNELS = 128
BLOCKS = 512
ALPHAS = 64
SHIFTS = 8
FLOOR = 0.1
F32 = jnp.float32
BF16 = jnp.bfloat16
VMEM = pl.BlockSpec(memory_space=pltpu.VMEM)
HBM = pl.BlockSpec(memory_space=pltpu.HBM)


def halves(table):
    high = table.astype(ml_dtypes.bfloat16)
    low = (table - high.astype(np.float64)).astype(ml_dtypes.bfloat16)
    return np.stack([high, low])


def channel_table():
    n = np.arange(CHANNELS)
    window = 0.5 - 0.5 * np.cos(2 * np.pi * n / CHANNELS)
    angle = 2 * np.pi * (n[:, None] * n[None, :] % CHANNELS) / CHANNELS
    cosine = window[:, None] * np.cos(angle) / math.sqrt(CHANNELS)
    sine = window[:, None] * np.sin(angle) / math.sqrt(CHANNELS)
    return halves(np.block([[cosine, -sine], [sine, cosine]]))


def half_order():
    return np.arange(BLOCKS // 2).reshape(8, 4, 8).transpose(1, 0, 2).reshape(-1)


def block_table():
    n = half_order()
    angle = 4 * np.pi * (n[:, None] * n[None, :] % (BLOCKS // 2)) / BLOCKS
    return halves(np.concatenate([np.cos(angle), np.sin(angle)], 0) / math.sqrt(BLOCKS))


def twiddles():
    angle = 2 * np.pi * half_order()[:, None] / BLOCKS * np.ones((1, 128))
    sign = np.where(np.arange(128) < 64, 1.0, -1.0)
    return np.stack([np.cos(angle), np.sin(angle) * sign]).astype(np.float32)


def split(x):
    high = x.astype(BF16)
    return high, (x - high.astype(F32)).astype(BF16)


def dot3(a, b, dims):
    def one(u, v):
        return lax.dot_general(u, v, (dims, ((), ())), preferred_element_type=F32)

    rows = a[0].shape[0]
    top = one(jnp.concatenate(a, 0), b[0])
    return top[:rows] + (top[rows:] + one(a[0], b[1]))


def lane_block(shape, width):
    return lax.broadcasted_iota(jnp.int32, shape, len(shape) - 1) // width % 2


def swap_blocks(tiles):
    tiles = list(tiles)
    for bit in (1, 2, 4, 8):
        width = 8 * bit
        upper = lane_block(tiles[0].shape, width) == 1
        for i in range(16):
            if i & bit:
                continue
            a, b = tiles[i], tiles[i | bit]
            axis = a.ndim - 1
            tiles[i] = jnp.where(upper, pltpu.roll(b, width, axis), a)
            tiles[i | bit] = jnp.where(upper, b, pltpu.roll(a, 128 - width, axis))
    return tiles


def remote(src, dst, send, recv, **where):
    return pltpu.make_async_remote_copy(
        src_ref=src,
        dst_ref=dst,
        send_sem=send,
        recv_sem=recv,
        device_id=where,
        device_id_type=pl.DeviceIdType.MESH,
    )


def ring(d):
    return min(d, 4 - d)


OWNERS = sorted(
    ((d, y, c) for d in range(2) for y in range(4) for c in range(2) if d + y + c),
    key=lambda step: -(2 * step[0] + ring(step[1])),
)
PLANE = sorted(
    ((d, y, lo) for d in range(2) for y in range(4) for lo in range(2) if d + y + lo),
    key=lambda step: -(ring(2 * step[0] + step[2]) + ring(step[1])),
)


def phase_rows(bins_ref, offsets_ref, first):
    row = lax.broadcasted_iota(jnp.int32, (ALPHAS, ALPHAS), 0)
    same = row == lax.broadcasted_iota(jnp.int32, (ALPHAS, ALPHAS), 1)

    def column(ref):
        return jnp.sum(jnp.where(same, ref[...].astype(F32), 0.0), 1, keepdims=True)

    lane = lax.broadcasted_iota(jnp.int32, (ALPHAS, 256), 1)
    turns = column(bins_ref).astype(jnp.int32) * (first + lane // 8) % BLOCKS
    angle = turns.astype(F32) * (2.0 * math.pi / BLOCKS)
    chosen = column(offsets_ref).astype(jnp.int32) == lane % 8
    both = [jnp.where(chosen, f(angle) * (1.0 / 256.0), 0.0) for f in (jnp.cos, jnp.sin)]
    return split(jnp.concatenate(both, 0))


def kernel(
    x_hbm, bins_hbm, offsets_hbm, ctable_hbm, table_hbm, twiddle_hbm, out_ref,
    bins_ref, offsets_ref, x_ref, ctable_ref, table_ref, twiddle_ref, mid_ref, made_ref, got_ref, back_ref, land_ref,
    right_ref, other_ref, phase_ref, high_ref, low_ref, high2_ref, low2_ref, left_ref,
    part_ref, pair_ref, sum_ref, all_ref, part2_ref, pair2_ref, sum2_ref, all2_ref, res_ref, late_ref,
    load_sem, send1, recv1, send2, recv2, sendx, recvx, sendf, recvf, sendz, recvz,
    sendp, recvp, sends, recvs,
):
    chan, x, z = lax.axis_index("chan"), lax.axis_index("x"), lax.axis_index("z")
    core, place = lax.rem(chan, 2), chan // 2
    mate = chan + 1 - 2 * core
    after, before = lax.rem(x + 1, 4), lax.rem(x + 3, 4)

    loads = [
        pltpu.make_async_copy(src, dst, load_sem.at[i])
        for i, (src, dst) in enumerate(
            [
                (x_hbm, x_ref),
                (ctable_hbm, ctable_ref),
                (table_hbm, table_ref),
                (bins_hbm, bins_ref),
                (offsets_hbm, offsets_ref),
                (twiddle_hbm, twiddle_ref),
            ]
        )
    ]
    for load in loads:
        load.start()

    barrier = pltpu.get_barrier_semaphore()
    peers = [{"chan": lax.rem(chan + o, 16)} for o in range(1, 16)]
    peers += [{"x": after}, {"x": before}]
    peers += [{"z": 1 - z}]
    for where in peers:
        pl.semaphore_signal(barrier, device_id=where, device_id_type=pl.DeviceIdType.MESH)

    loads[0].wait()
    loads[1].wait()
    both = jnp.concatenate([x_ref[0].reshape(512, 128), x_ref[1].reshape(512, 128)], 1)
    mid_ref[...] = dot3(split(both), (ctable_ref[0], ctable_ref[1]), ((1,), (0,)))
    def tiles_of(h):
        for mc in range(4):
            tiles = [
                mid_ref[s * 32 + mc * 8 : s * 32 + mc * 8 + 8, c * 128 : c * 128 + 128]
                for c in range(2)
                for s in range(h * 8, h * 8 + 8)
            ]
            for dest, tile in enumerate(swap_blocks(tiles)):
                made_ref[h, dest, mc] = tile

    def owner(d, y, c):
        return lax.rem(place + d * 4, 8) // 4 * 8 + lax.rem(lax.rem(place, 4) + y, 4) * 2 + (core + c) % 2

    def exchange(src, dst, send, recv, step):
        peer = owner(*step)
        return remote(src.at[peer], dst.at[chan], send, recv, chan=peer)

    def everyone(src, dst, send, recv):
        most = pl.ds(0, 15)
        return remote(src.at[most], dst.at[most], send, recv, chan=mate)

    def first(h):
        return made_ref.at[h], got_ref.at[h], send1.at[h], recv1.at[h]

    def second(h, part):
        return back_ref.at[h, part], land_ref.at[h, part], send2.at[h, part], recv2.at[h, part]

    def send_all(group):
        for step in OWNERS:
            exchange(*group, step).start()

    tiles_of(0)
    pl.semaphore_wait(barrier, len(peers))
    send_all(first(0))
    tiles_of(1)
    everyone(*first(0)).wait_send()
    send_all(first(1))
    for h in range(2):
        got_ref[h, chan] = made_ref[h, chan]
    for load in loads[2:]:
        load.wait()
    phase_ref[0], phase_ref[1] = phase_rows(bins_ref, offsets_ref, chan * 32)

    first_part = lax.broadcasted_iota(jnp.int32, (BLOCKS // 2, 256), 1) % 128 < 64

    def turned(u):
        return jnp.concatenate([pltpu.roll(u[:, i : i + 128], 64, 1) for i in (0, 128)], 1)

    def transform(v):
        u = dot3((table_ref[0], table_ref[1]), split(v), ((1,), (0,)))
        return u[:256], turned(u[256:])

    for h in range(2):
        everyone(*first(h)).wait_recv()
        if h:
            everyone(*second(0, 0)).wait_send()
            send_all(second(0, 1))
        low, high = (
            jnp.concatenate([got_ref[h, i : i + 8, mc].reshape(64, 128) for mc in range(4)], 0)
            for i in (0, 8)
        )
        odd = low - high
        odd = odd * twiddle_ref[0] + pltpu.roll(odd, 64, 1) * twiddle_ref[1]
        cosine, sine = transform(jnp.concatenate([low + high, odd], 1))
        spectra = cosine + jnp.where(first_part, sine, -sine)
        power = spectra * spectra
        power = power + turned(power)
        cosine, sine = transform(spectra / jnp.sqrt(power + FLOOR))
        blocks = cosine - jnp.where(first_part, sine, -sine)
        even, odd = blocks[:, :128], blocks[:, 128:]
        odd = odd * twiddle_ref[0] - pltpu.roll(odd, 64, 1) * twiddle_ref[1]
        for i, half in ((0, even + odd), (8, even - odd)):
            for mc in range(4):
                rows = half[mc * 64 : mc * 64 + 64].reshape(8, 8, 128)
                back_ref[h, mc // 2, i : i + 8, mc % 2] = rows
        for part in range(2):
            land_ref[h, part, chan] = back_ref[h, part, chan]
        send_all(second(h, 0))
        if h:
            send_all(second(1, 1))

    def eight(i, mc, h):
        return right_ref.at[i, mc, pl.ds(h * 8, 8)]

    def to_x(h, mc, way, incoming=False):
        peer = (after, before)[way ^ incoming]
        at = peer if incoming else x
        return remote(
            eight(x, mc, h), eight(at, mc, h), sendx.at[way, h, mc], recvx.at[way, h, mc], x=peer
        )

    def passed(h, mc, way, incoming=False):
        source, peer = (before, after) if way == 0 else (after, before)
        at = lax.rem(x + 2, 4) if incoming else source
        four = pl.ds(h * 8 + way * 4, 4)
        return remote(
            right_ref.at[source, mc, four], right_ref.at[at, mc, four],
            sendf.at[way, h, mc], recvf.at[way, h, mc], x=peer,
        )

    def to_z(h, mc):
        return remote(
            eight(x, mc, h), other_ref.at[mc, pl.ds(h * 8, 8)], sendz.at[h, mc], recvz.at[h, mc], z=1 - z
        )

    def turn(h, mc):
        tiles = swap_blocks([land_ref[h, mc // 2, i, mc % 2] for i in range(16)])
        for i, tile in enumerate(tiles):
            right_ref[x, mc, h * 8 + i % 8, i // 8] = tile
        to_x(h, mc, 0).start()
        to_x(h, mc, 1).start()
        to_z(h, mc).start()

    def forward(h, mc):
        for way in range(2):
            to_x(h, mc, way, True).wait_recv()
            passed(h, mc, way).start()

    far = lax.rem(x + 2, 4)

    def shifted(mc, r):
        left = []
        for c in range(2):
            rows = []
            for a in range(32):
                if a < 16:
                    row = right_ref[x, mc, a, c, pl.ds(r, 1), :]
                else:
                    row = other_ref[mc, a - 16, c, pl.ds(r, 1), :]
                rows.append(pltpu.roll(jnp.broadcast_to(row, (8, 128)), 0, 1, stride=1, stride_axis=0))
            left.append(jnp.concatenate(rows, 0))
        return split(jnp.concatenate(left, 1))

    def facing(i, mc, r):
        tall = right_ref.at[i, mc].reshape(256, 128)
        real, imag = (tall[pl.ds(r + c * 8, 16, stride=16), :] for c in range(2))
        return [jnp.concatenate([real, imag], 1), jnp.concatenate([-imag, real], 1)]

    def product(mc, r, part):
        m = mc * 8 + r
        if part == 0:
            left = shifted(mc, r)
            left_ref[0, m], left_ref[1, m] = left
            rows = []
            for i in range(4):
                rows += facing(jnp.where(far == i, x, i), mc, r)
        else:
            left = left_ref[0, m], left_ref[1, m]
            rows = facing(far, mc, r)
        right = split(jnp.concatenate(rows, 0))
        if part:
            right = [jnp.concatenate([half] * 4, 0) for half in right]
        out = dot3(left, right, ((1,), (1,)))
        if part == 0:
            return out.reshape(32, 8, 128)
        out = out.reshape(8, 4, 8, 128)
        group = lax.broadcasted_iota(jnp.int32, (8, 8, 128), 2) // 32
        tiles = out[:, 3]
        for i in range(3):
            tiles = jnp.where(group == i, out[:, i], tiles)
        return tiles

    def products(mc, part, high_ref, low_ref):
        def step(i, carry):
            for half in range(2):
                r = i * 4 + half * 2
                tiles = jnp.concatenate([product(mc, r, part), product(mc, r + 1, part)], 1)
                rows = pl.ds(pl.multiple_of(mc * 64 + r * 8, 16), 16)
                high_ref[:, rows, :], low_ref[:, rows, :] = split(tiles)
            return carry

        lax.fori_loop(0, 2, step, 0)

    for h in range(2):
        for mc in range(4):
            if mc % 2 == 0:
                everyone(*second(h, mc // 2)).wait_recv()
            turn(h, mc)
    @pl.loop(0, 4)
    def _(mc):
        for h in range(2):
            forward(h, mc)
            to_z(h, mc).wait_recv()
        products(mc, 0, high_ref, low_ref)

    low_rows = lax.broadcasted_iota(jnp.int32, (8, 128), 0) < 4

    def one_pair(refs, out_ref, half, pair):
        a = half * (refs[0].shape[0] // 2) + pair * 2
        both = tuple(jnp.concatenate([ref[a], ref[a + 1]], 1) for ref in refs)
        t = dot3((phase_ref[0], phase_ref[1]), both, ((1,), (0,)))
        gs = []
        for i in range(2):
            cosine, sine = t[:64, i * 128 : i * 128 + 128], t[64:, i * 128 : i * 128 + 128]
            odd = lane_block(sine.shape, 16) == 1
            gs.append(cosine + jnp.where(odd, -pltpu.roll(sine, 16, 1), pltpu.roll(sine, 112, 1)))
        row = pl.ds(pair * 8, 8)
        for t8 in range(8):
            a0, a1 = (g[t8 * 8 : t8 * 8 + 8] for g in gs)
            out_ref[0, half, t8, row, :] = jnp.where(low_rows, a0, pltpu.roll(a1, 4, 0))
            out_ref[1, half, t8, row, :] = jnp.where(low_rows, pltpu.roll(a0, 4, 0), a1)

    def to_mate(part, half):
        return remote(
            parts[part].at[1 - core, half], pairs[part].at[half],
            sendp.at[part, half], recvp.at[part, half], chan=mate,
        )

    def last(part):
        return sums[part], alls[part], sends.at[part], recvs.at[part]

    def spread(part, d, y, lo):
        peer_z, peer = (z + lo) % 2, owner(d, y, 0) // 2
        src, dst, send, recv = last(part)
        return remote(
            src.at[lo * 8 + peer], dst.at[z * 8 + place], send, recv,
            z=peer_z, chan=peer * 2 + core,
        )

    def add_and_send(part, half):
        to_mate(part, half).wait_recv()
        sums[part][half * 8 : half * 8 + 8] = parts[part][core, half] + pairs[part][half]

        for step in PLANE:
            if step[2] == half:
                spread(part, *step).start()

        if not half:
            alls[part][z * 8 + place] = sums[part][place]

    parts, pairs = (part_ref, part2_ref), (pair_ref, pair2_ref)
    sums, alls = (sum_ref, sum2_ref), (all_ref, all2_ref)
    for half in (1, 0):
        for pair in range(8):
            one_pair((high_ref, low_ref), part_ref, half, pair)
        to_mate(0, half).start()
    def late_products(mc):
        for h in range(2):
            for way in range(2):
                passed(h, mc, way, True).wait_recv()
        products(mc, 1, high2_ref, low2_ref)

    @pl.loop(0, 1)
    def _(mc):
        late_products(mc)

    for half in (1, 0):
        add_and_send(0, half)

    @pl.loop(1, 4)
    def _(mc):
        late_products(mc)

    for half in (1, 0):
        for pair in range(2):
            one_pair((high2_ref, low2_ref), part2_ref, half, pair)
        to_mate(1, half).start()
    for half in (1, 0):
        add_and_send(1, half)

    for group in (first(1), second(0, 1), second(1, 0), second(1, 1), last(0)):
        everyone(*group).wait_send()
    for mc in range(4):
        for h in range(2):
            for way in range(2):
                to_x(h, mc, way).wait_send()
                passed(h, mc, way).wait_send()
            to_z(h, mc).wait_send()
        to_mate(mc // 2, mc % 2).wait_send()
    everyone(*last(0)).wait_recv()
    for h in range(2):
        res_ref[h] = jnp.sum(all_ref[h * 8 : h * 8 + 8], axis=0)
    everyone(*last(1)).wait_recv()
    for h in range(2):
        late = jnp.sum(all2_ref[h * 8 : h * 8 + 8], axis=0)
        for i in range(4):
            there = pltpu.roll(late, lax.rem(far + 4 - i, 4) * 32, 1)
            for g in range(4):
                late_ref[h, g * 16 + i * 4 : g * 16 + i * 4 + 4] = there[g * 4 : g * 4 + 4]
    missing = lax.broadcasted_iota(jnp.int32, (64, 128), 1) // 32 == far
    lo, hi = (jnp.where(missing, late_ref[h], res_ref[h]) for h in range(2))
    odd = lane_block(lo.shape, 16) == 1
    res_ref[0] = jnp.where(odd, pltpu.roll(hi, 16, 1), lo)
    res_ref[1] = jnp.where(odd, hi, pltpu.roll(lo, 112, 1))
    for j in range(4):
        for c in range(2):
            out_ref[j, c] = res_ref[c, pl.ds(j, 16, stride=4), :]

    everyone(*last(1)).wait_send()


DMA = pltpu.SemaphoreType.DMA


def summed(rows):
    shapes = [(2, 2, 8), (2, 8), (16,), (16,)]
    return [pltpu.VMEM((*shape, rows, 128), F32) for shape in shapes]


def on_device(samples, bins, offsets):
    chunk = pltpu.VMEM((2, 16, 4, 8, 128), F32)
    pieces = pltpu.VMEM((2, 2, 16, 2, 8, 128), F32)
    sixteen = pltpu.VMEM((16, 64, 128), F32)
    return pl.pallas_call(
        kernel,
        out_shape=jax.ShapeDtypeStruct((4, 2, 16, 128), F32),
        in_specs=[HBM] * 6,
        out_specs=VMEM,
        scratch_shapes=[
            pltpu.VMEM((1, ALPHAS), jnp.int32),
            pltpu.VMEM((1, ALPHAS), jnp.int32),
            pltpu.VMEM((2, 16, 32, 128), F32),
            pltpu.VMEM((2, 256, 256), BF16),
            pltpu.VMEM((2, BLOCKS, BLOCKS // 2), BF16),
            pltpu.VMEM((2, BLOCKS // 2, 128), F32),
            pltpu.VMEM((512, 256), F32),
            chunk, chunk, pieces, pieces,
            pltpu.VMEM((4, 4, 16, 2, 8, 128), F32),
            pltpu.VMEM((4, 16, 2, 8, 128), F32),
            pltpu.VMEM((2, 128, 256), BF16),
            pltpu.VMEM((32, 256, 128), BF16),
            pltpu.VMEM((32, 256, 128), BF16),
            pltpu.VMEM((8, 256, 128), BF16),
            pltpu.VMEM((8, 256, 128), BF16),
            pltpu.VMEM((2, 32, 256, 256), BF16),
            *summed(64),
            *summed(16),
            pltpu.VMEM((2, 64, 128), F32),
            pltpu.VMEM((2, 64, 128), F32),
            DMA((6,)), DMA((2,)), DMA((2,)), DMA((2, 2)), DMA((2, 2)),
            DMA((2, 2, 4)), DMA((2, 2, 4)), DMA((2, 2, 4)), DMA((2, 2, 4)), DMA((2, 4)), DMA((2, 4)),
            DMA((2, 2)), DMA((2, 2)), DMA((2,)), DMA((2,)),
        ],
        compiler_params=pltpu.CompilerParams(
            vmem_limit_bytes=60 * 2**20, collective_id=0, has_side_effects=True
        ),
        name="coherence",
    )(samples, bins.reshape(1, -1), offsets.reshape(1, -1), channel_table(), block_table(), twiddles())


def solution(mesh):
    finer = Mesh(mesh.devices.reshape(4, 2, mesh.shape["chan"]), ("x", "z", "chan"))
    sensor = ("x", "z")
    return jax.shard_map(
        on_device,
        mesh=finer,
        in_specs=(P(None, sensor, "chan", None), P(), P()),
        out_specs=P("chan", None, sensor, None),
        check_vma=False,
    )
```

```python
import math

import jax
import jax.numpy as jnp
import ml_dtypes
import numpy as np
from jax import lax
from jax.experimental import pallas as pl
from jax.experimental.pallas import tpu as pltpu
from jax.sharding import Mesh
from jax.sharding import PartitionSpec as P

CHANNELS = 128
BLOCKS = 512
ALPHAS = 64
SHIFTS = 8
FLOOR = 0.1
F32 = jnp.float32
BF16 = jnp.bfloat16
VMEM = pl.BlockSpec(memory_space=pltpu.VMEM)
HBM = pl.BlockSpec(memory_space=pltpu.HBM)


def halves(table):
    high = table.astype(ml_dtypes.bfloat16)
    low = (table - high.astype(np.float64)).astype(ml_dtypes.bfloat16)
    return np.stack([high, low])


def channel_table():
    n = np.arange(CHANNELS)
    window = 0.5 - 0.5 * np.cos(2 * np.pi * n / CHANNELS)
    angle = 2 * np.pi * (n[:, None] * n[None, :] % CHANNELS) / CHANNELS
    cosine = window[:, None] * np.cos(angle) / math.sqrt(CHANNELS)
    sine = window[:, None] * np.sin(angle) / math.sqrt(CHANNELS)
    return halves(np.block([[cosine, -sine], [sine, cosine]]))


def half_order():
    return np.arange(BLOCKS // 2).reshape(8, 4, 8).transpose(1, 0, 2).reshape(-1)


def block_table():
    n = half_order()
    angle = 4 * np.pi * (n[:, None] * n[None, :] % (BLOCKS // 2)) / BLOCKS
    return halves(np.concatenate([np.cos(angle), np.sin(angle)], 0) / math.sqrt(BLOCKS))


def twiddles():
    angle = 2 * np.pi * half_order()[:, None] / BLOCKS * np.ones((1, 128))
    sign = np.where(np.arange(128) < 64, 1.0, -1.0)
    return np.stack([np.cos(angle), np.sin(angle) * sign]).astype(np.float32)


def split(x):
    high = x.astype(BF16)
    return high, (x - high.astype(F32)).astype(BF16)


def dot3(a, b, dims):
    def one(u, v):
        return lax.dot_general(u, v, (dims, ((), ())), preferred_element_type=F32)

    rows = a[0].shape[0]
    top = one(jnp.concatenate(a, 0), b[0])
    return top[:rows] + (top[rows:] + one(a[0], b[1]))


def lane_block(shape, width):
    return lax.broadcasted_iota(jnp.int32, shape, len(shape) - 1) // width % 2


def swap_blocks(tiles):
    tiles = list(tiles)
    for bit in (1, 2, 4, 8):
        width = 8 * bit
        upper = lane_block(tiles[0].shape, width) == 1
        for i in range(16):
            if i & bit:
                continue
            a, b = tiles[i], tiles[i | bit]
            axis = a.ndim - 1
            tiles[i] = jnp.where(upper, pltpu.roll(b, width, axis), a)
            tiles[i | bit] = jnp.where(upper, b, pltpu.roll(a, 128 - width, axis))
    return tiles


def remote(src, dst, send, recv, **where):
    return pltpu.make_async_remote_copy(
        src_ref=src,
        dst_ref=dst,
        send_sem=send,
        recv_sem=recv,
        device_id=where,
        device_id_type=pl.DeviceIdType.MESH,
    )


def ring(d):
    return min(d, 4 - d)


OWNERS = sorted(
    ((d, y, c) for d in range(2) for y in range(4) for c in range(2) if d + y + c),
    key=lambda step: -(2 * step[0] + ring(step[1])),
)
PLANE = sorted(
    ((d, y, lo) for d in range(2) for y in range(4) for lo in range(2) if d + y + lo),
    key=lambda step: -(ring(2 * step[0] + step[2]) + ring(step[1])),
)


def phase_rows(bins_ref, offsets_ref, first):
    row = lax.broadcasted_iota(jnp.int32, (ALPHAS, ALPHAS), 0)
    same = row == lax.broadcasted_iota(jnp.int32, (ALPHAS, ALPHAS), 1)

    def column(ref):
        return jnp.sum(jnp.where(same, ref[...].astype(F32), 0.0), 1, keepdims=True)

    lane = lax.broadcasted_iota(jnp.int32, (ALPHAS, 256), 1)
    turns = column(bins_ref).astype(jnp.int32) * (first + lane // 8) % BLOCKS
    angle = turns.astype(F32) * (2.0 * math.pi / BLOCKS)
    chosen = column(offsets_ref).astype(jnp.int32) == lane % 8
    both = [jnp.where(chosen, f(angle) * (1.0 / 256.0), 0.0) for f in (jnp.cos, jnp.sin)]
    return split(jnp.concatenate(both, 0))


def kernel(
    x_hbm, bins_hbm, offsets_hbm, ctable_hbm, table_hbm, twiddle_hbm, out_ref,
    bins_ref, offsets_ref, x_ref, ctable_ref, table_ref, twiddle_ref, mid_ref, made_ref, got_ref, back_ref, land_ref,
    right_ref, other_ref, phase_ref, high_ref, low_ref, high2_ref, low2_ref, left_ref,
    part_ref, pair_ref, sum_ref, all_ref, part2_ref, pair2_ref, sum2_ref, all2_ref, res_ref, late_ref,
    load_sem, send1, recv1, send2, recv2, sendx, recvx, sendf, recvf, sendz, recvz,
    sendp, recvp, sends, recvs,
):
    chan, x, z = lax.axis_index("chan"), lax.axis_index("x"), lax.axis_index("z")
    core, place = lax.rem(chan, 2), chan // 2
    mate = chan + 1 - 2 * core
    after, before = lax.rem(x + 1, 4), lax.rem(x + 3, 4)

    loads = [
        pltpu.make_async_copy(src, dst, load_sem.at[i])
        for i, (src, dst) in enumerate(
            [
                (x_hbm, x_ref),
                (ctable_hbm, ctable_ref),
                (table_hbm, table_ref),
                (bins_hbm, bins_ref),
                (offsets_hbm, offsets_ref),
                (twiddle_hbm, twiddle_ref),
            ]
        )
    ]
    for load in loads:
        load.start()

    barrier = pltpu.get_barrier_semaphore()
    peers = [{"chan": lax.rem(chan + o, 16)} for o in range(1, 16)]
    peers += [{"x": after}, {"x": before}]
    peers += [{"z": 1 - z}]
    for where in peers:
        pl.semaphore_signal(barrier, device_id=where, device_id_type=pl.DeviceIdType.MESH)

    loads[0].wait()
    loads[1].wait()
    both = jnp.concatenate([x_ref[0].reshape(512, 128), x_ref[1].reshape(512, 128)], 1)
    mid_ref[...] = dot3(split(both), (ctable_ref[0], ctable_ref[1]), ((1,), (0,)))
    def tiles_of(h):
        for mc in range(4):
            tiles = [
                mid_ref[s * 32 + mc * 8 : s * 32 + mc * 8 + 8, c * 128 : c * 128 + 128]
                for c in range(2)
                for s in range(h * 8, h * 8 + 8)
            ]
            for dest, tile in enumerate(swap_blocks(tiles)):
                made_ref[h, dest, mc] = tile

    def owner(d, y, c):
        return lax.rem(place + d * 4, 8) // 4 * 8 + lax.rem(lax.rem(place, 4) + y, 4) * 2 + (core + c) % 2

    def exchange(src, dst, send, recv, step):
        peer = owner(*step)
        return remote(src.at[peer], dst.at[chan], send, recv, chan=peer)

    def everyone(src, dst, send, recv):
        most = pl.ds(0, 15)
        return remote(src.at[most], dst.at[most], send, recv, chan=mate)

    def first(h):
        return made_ref.at[h], got_ref.at[h], send1.at[h], recv1.at[h]

    def second(h, part):
        return back_ref.at[h, part], land_ref.at[h, part], send2.at[h, part], recv2.at[h, part]

    def send_all(group):
        for step in OWNERS:
            exchange(*group, step).start()

    tiles_of(0)
    pl.semaphore_wait(barrier, len(peers))
    send_all(first(0))
    tiles_of(1)
    everyone(*first(0)).wait_send()
    send_all(first(1))
    for h in range(2):
        got_ref[h, chan] = made_ref[h, chan]
    for load in loads[2:]:
        load.wait()
    phase_ref[0], phase_ref[1] = phase_rows(bins_ref, offsets_ref, chan * 32)

    first_part = lax.broadcasted_iota(jnp.int32, (BLOCKS // 2, 256), 1) % 128 < 64

    def turned(u):
        return jnp.concatenate([pltpu.roll(u[:, i : i + 128], 64, 1) for i in (0, 128)], 1)

    def transform(v):
        u = dot3((table_ref[0], table_ref[1]), split(v), ((1,), (0,)))
        return u[:256], turned(u[256:])

    for h in range(2):
        everyone(*first(h)).wait_recv()
        if h:
            everyone(*second(0, 0)).wait_send()
            send_all(second(0, 1))
        low, high = (
            jnp.concatenate([got_ref[h, i : i + 8, mc].reshape(64, 128) for mc in range(4)], 0)
            for i in (0, 8)
        )
        odd = low - high
        odd = odd * twiddle_ref[0] + pltpu.roll(odd, 64, 1) * twiddle_ref[1]
        cosine, sine = transform(jnp.concatenate([low + high, odd], 1))
        spectra = cosine + jnp.where(first_part, sine, -sine)
        power = spectra * spectra
        power = power + turned(power)
        cosine, sine = transform(spectra / jnp.sqrt(power + FLOOR))
        blocks = cosine - jnp.where(first_part, sine, -sine)
        even, odd = blocks[:, :128], blocks[:, 128:]
        odd = odd * twiddle_ref[0] - pltpu.roll(odd, 64, 1) * twiddle_ref[1]
        for i, half in ((0, even + odd), (8, even - odd)):
            for mc in range(4):
                rows = half[mc * 64 : mc * 64 + 64].reshape(8, 8, 128)
                back_ref[h, mc // 2, i : i + 8, mc % 2] = rows
        for part in range(2):
            land_ref[h, part, chan] = back_ref[h, part, chan]
        send_all(second(h, 0))
        if h:
            send_all(second(1, 1))

    def eight(i, mc, h):
        return right_ref.at[i, mc, pl.ds(h * 8, 8)]

    def to_x(h, mc, way, incoming=False):
        peer = (after, before)[way ^ incoming]
        at = peer if incoming else x
        return remote(
            eight(x, mc, h), eight(at, mc, h), sendx.at[way, h, mc], recvx.at[way, h, mc], x=peer
        )

    def passed(h, mc, way, incoming=False):
        source, peer = (before, after) if way == 0 else (after, before)
        at = lax.rem(x + 2, 4) if incoming else source
        four = pl.ds(h * 8 + way * 4, 4)
        return remote(
            right_ref.at[source, mc, four], right_ref.at[at, mc, four],
            sendf.at[way, h, mc], recvf.at[way, h, mc], x=peer,
        )

    def to_z(h, mc):
        return remote(
            eight(x, mc, h), other_ref.at[mc, pl.ds(h * 8, 8)], sendz.at[h, mc], recvz.at[h, mc], z=1 - z
        )

    def turn(h, mc):
        tiles = swap_blocks([land_ref[h, mc // 2, i, mc % 2] for i in range(16)])
        for i, tile in enumerate(tiles):
            right_ref[x, mc, h * 8 + i % 8, i // 8] = tile
        to_x(h, mc, 0).start()
        to_x(h, mc, 1).start()
        to_z(h, mc).start()

    def forward(h, mc):
        for way in range(2):
            to_x(h, mc, way, True).wait_recv()
            passed(h, mc, way).start()

    far = lax.rem(x + 2, 4)

    def shifted(mc, r):
        left = []
        for c in range(2):
            rows = []
            for a in range(32):
                if a < 16:
                    row = right_ref[x, mc, a, c, pl.ds(r, 1), :]
                else:
                    row = other_ref[mc, a - 16, c, pl.ds(r, 1), :]
                rows.append(pltpu.roll(jnp.broadcast_to(row, (8, 128)), 0, 1, stride=1, stride_axis=0))
            left.append(jnp.concatenate(rows, 0))
        return split(jnp.concatenate(left, 1))

    def facing(i, mc, r):
        tall = right_ref.at[i, mc].reshape(256, 128)
        real, imag = (tall[pl.ds(r + c * 8, 16, stride=16), :] for c in range(2))
        return [jnp.concatenate([real, imag], 1), jnp.concatenate([-imag, real], 1)]

    def product(mc, r, part):
        m = mc * 8 + r
        if part == 0:
            left = shifted(mc, r)
            left_ref[0, m], left_ref[1, m] = left
            rows = []
            for i in range(4):
                rows += facing(jnp.where(far == i, x, i), mc, r)
        else:
            left = left_ref[0, m], left_ref[1, m]
            rows = facing(far, mc, r)
        right = split(jnp.concatenate(rows, 0))
        if part:
            right = [jnp.concatenate([half] * 4, 0) for half in right]
        out = dot3(left, right, ((1,), (1,)))
        if part == 0:
            return out.reshape(32, 8, 128)
        out = out.reshape(8, 4, 8, 128)
        group = lax.broadcasted_iota(jnp.int32, (8, 8, 128), 2) // 32
        tiles = out[:, 3]
        for i in range(3):
            tiles = jnp.where(group == i, out[:, i], tiles)
        return tiles

    def products(mc, part, high_ref, low_ref):
        def step(i, carry):
            for half in range(2):
                r = i * 4 + half * 2
                tiles = jnp.concatenate([product(mc, r, part), product(mc, r + 1, part)], 1)
                rows = pl.ds(pl.multiple_of(mc * 64 + r * 8, 16), 16)
                high_ref[:, rows, :], low_ref[:, rows, :] = split(tiles)
            return carry

        lax.fori_loop(0, 2, step, 0)

    for h in range(2):
        for mc in range(4):
            if mc % 2 == 0:
                everyone(*second(h, mc // 2)).wait_recv()
            turn(h, mc)
    @pl.loop(0, 4)
    def _(mc):
        for h in range(2):
            forward(h, mc)
            to_z(h, mc).wait_recv()
        products(mc, 0, high_ref, low_ref)

    low_rows = lax.broadcasted_iota(jnp.int32, (8, 128), 0) < 4

    def one_pair(refs, out_ref, half, pair):
        a = half * (refs[0].shape[0] // 2) + pair * 2
        both = tuple(jnp.concatenate([ref[a], ref[a + 1]], 1) for ref in refs)
        t = dot3((phase_ref[0], phase_ref[1]), both, ((1,), (0,)))
        gs = []
        for i in range(2):
            cosine, sine = t[:64, i * 128 : i * 128 + 128], t[64:, i * 128 : i * 128 + 128]
            odd = lane_block(sine.shape, 16) == 1
            gs.append(cosine + jnp.where(odd, -pltpu.roll(sine, 16, 1), pltpu.roll(sine, 112, 1)))
        row = pl.ds(pair * 8, 8)
        for t8 in range(8):
            a0, a1 = (g[t8 * 8 : t8 * 8 + 8] for g in gs)
            out_ref[0, half, t8, row, :] = jnp.where(low_rows, a0, pltpu.roll(a1, 4, 0))
            out_ref[1, half, t8, row, :] = jnp.where(low_rows, pltpu.roll(a0, 4, 0), a1)

    def to_mate(part, half):
        return remote(
            parts[part].at[1 - core, half], pairs[part].at[half],
            sendp.at[part, half], recvp.at[part, half], chan=mate,
        )

    def last(part):
        return sums[part], alls[part], sends.at[part], recvs.at[part]

    def spread(part, d, y, lo):
        peer_z, peer = (z + lo) % 2, owner(d, y, 0) // 2
        src, dst, send, recv = last(part)
        return remote(
            src.at[lo * 8 + peer], dst.at[z * 8 + place], send, recv,
            z=peer_z, chan=peer * 2 + core,
        )

    def add_and_send(part, half):
        to_mate(part, half).wait_recv()
        sums[part][half * 8 : half * 8 + 8] = parts[part][core, half] + pairs[part][half]

        for step in PLANE:
            if step[2] == half:
                spread(part, *step).start()

        if not half:
            alls[part][z * 8 + place] = sums[part][place]

    parts, pairs = (part_ref, part2_ref), (pair_ref, pair2_ref)
    sums, alls = (sum_ref, sum2_ref), (all_ref, all2_ref)
    for half in (1, 0):
        for pair in range(8):
            one_pair((high_ref, low_ref), part_ref, half, pair)
        to_mate(0, half).start()
    def late_products(mc):
        for h in range(2):
            for way in range(2):
                passed(h, mc, way, True).wait_recv()
        products(mc, 1, high2_ref, low2_ref)

    @pl.loop(0, 1)
    def _(mc):
        late_products(mc)

    for half in (1, 0):
        add_and_send(0, half)

    @pl.loop(1, 4)
    def _(mc):
        late_products(mc)

    for half in (1, 0):
        for pair in range(2):
            one_pair((high2_ref, low2_ref), part2_ref, half, pair)
        to_mate(1, half).start()
    for half in (1, 0):
        add_and_send(1, half)

    for group in (first(1), second(0, 1), second(1, 0), second(1, 1), last(0)):
        everyone(*group).wait_send()
    for mc in range(4):
        for h in range(2):
            for way in range(2):
                to_x(h, mc, way).wait_send()
                passed(h, mc, way).wait_send()
            to_z(h, mc).wait_send()
        to_mate(mc // 2, mc % 2).wait_send()
    everyone(*last(0)).wait_recv()
    for h in range(2):
        res_ref[h] = jnp.sum(all_ref[h * 8 : h * 8 + 8], axis=0)
    everyone(*last(1)).wait_recv()
    for h in range(2):
        late = jnp.sum(all2_ref[h * 8 : h * 8 + 8], axis=0)
        for i in range(4):
            there = pltpu.roll(late, lax.rem(far + 4 - i, 4) * 32, 1)
            for g in range(4):
                late_ref[h, g * 16 + i * 4 : g * 16 + i * 4 + 4] = there[g * 4 : g * 4 + 4]
    missing = lax.broadcasted_iota(jnp.int32, (64, 128), 1) // 32 == far
    lo, hi = (jnp.where(missing, late_ref[h], res_ref[h]) for h in range(2))
    odd = lane_block(lo.shape, 16) == 1
    res_ref[0] = jnp.where(odd, pltpu.roll(hi, 16, 1), lo)
    res_ref[1] = jnp.where(odd, hi, pltpu.roll(lo, 112, 1))
    for j in range(4):
        for c in range(2):
            out_ref[j, c] = res_ref[c, pl.ds(j, 16, stride=4), :]

    everyone(*last(1)).wait_send()


DMA = pltpu.SemaphoreType.DMA


def summed(rows):
    shapes = [(2, 2, 8), (2, 8), (16,), (16,)]
    return [pltpu.VMEM((*shape, rows, 128), F32) for shape in shapes]


def on_device(samples, bins, offsets):
    chunk = pltpu.VMEM((2, 16, 4, 8, 128), F32)
    pieces = pltpu.VMEM((2, 2, 16, 2, 8, 128), F32)
    sixteen = pltpu.VMEM((16, 64, 128), F32)
    given = [
        samples, bins.reshape(1, -1), offsets.reshape(1, -1),
        jnp.asarray(channel_table()), jnp.asarray(block_table()), jnp.asarray(twiddles()),
    ]
    return pl.pallas_call(
        kernel,
        out_shape=jax.ShapeDtypeStruct((4, 2, 16, 128), F32),
        in_specs=[HBM] * 6,
        out_specs=VMEM,
        scratch_shapes=[
            pltpu.VMEM((1, ALPHAS), jnp.int32),
            pltpu.VMEM((1, ALPHAS), jnp.int32),
            pltpu.VMEM((2, 16, 32, 128), F32),
            pltpu.VMEM((2, 256, 256), BF16),
            pltpu.VMEM((2, BLOCKS, BLOCKS // 2), BF16),
            pltpu.VMEM((2, BLOCKS // 2, 128), F32),
            pltpu.VMEM((512, 256), F32),
            chunk, chunk, pieces, pieces,
            pltpu.VMEM((4, 4, 16, 2, 8, 128), F32),
            pltpu.VMEM((4, 16, 2, 8, 128), F32),
            pltpu.VMEM((2, 128, 256), BF16),
            pltpu.VMEM((32, 256, 128), BF16),
            pltpu.VMEM((32, 256, 128), BF16),
            pltpu.VMEM((8, 256, 128), BF16),
            pltpu.VMEM((8, 256, 128), BF16),
            pltpu.VMEM((2, 32, 256, 256), BF16),
            *summed(64),
            *summed(16),
            pltpu.VMEM((2, 64, 128), F32),
            pltpu.VMEM((2, 64, 128), F32),
            DMA((6,)), DMA((2,)), DMA((2,)), DMA((2, 2)), DMA((2, 2)),
            DMA((2, 2, 4)), DMA((2, 2, 4)), DMA((2, 2, 4)), DMA((2, 2, 4)), DMA((2, 4)), DMA((2, 4)),
            DMA((2, 2)), DMA((2, 2)), DMA((2,)), DMA((2,)),
        ],
        compiler_params=pltpu.CompilerParams(
            vmem_limit_bytes=40 * 2**20, collective_id=0, has_side_effects=True
        ),
        name="coherence",
    )(*(pltpu.with_memory_space_constraint(v, pltpu.HBM) for v in given))


def solution(mesh):
    finer = Mesh(mesh.devices.reshape(4, 2, mesh.shape["chan"]), ("x", "z", "chan"))
    sensor = ("x", "z")
    return jax.shard_map(
        on_device,
        mesh=finer,
        in_specs=(P(None, sensor, "chan", None), P(), P()),
        out_specs=P("chan", None, sensor, None),
        check_vma=False,
    )
```

```python
import math

import jax
import jax.numpy as jnp
import ml_dtypes
import numpy as np
from jax import lax
from jax.experimental import pallas as pl
from jax.experimental.pallas import tpu as pltpu
from jax.sharding import Mesh
from jax.sharding import PartitionSpec as P

CHANNELS = 128
BLOCKS = 512
ALPHAS = 64
SHIFTS = 8
FLOOR = 0.1
F32 = jnp.float32
BF16 = jnp.bfloat16
VMEM = pl.BlockSpec(memory_space=pltpu.VMEM)
HBM = pl.BlockSpec(memory_space=pltpu.HBM)


def halves(table):
    high = table.astype(ml_dtypes.bfloat16)
    low = (table - high.astype(np.float64)).astype(ml_dtypes.bfloat16)
    return np.stack([high, low])


def channel_table():
    n = np.arange(CHANNELS)
    window = 0.5 - 0.5 * np.cos(2 * np.pi * n / CHANNELS)
    angle = 2 * np.pi * (n[:, None] * n[None, :] % CHANNELS) / CHANNELS
    cosine = window[:, None] * np.cos(angle) / math.sqrt(CHANNELS)
    sine = window[:, None] * np.sin(angle) / math.sqrt(CHANNELS)
    return halves(np.block([[cosine, -sine], [sine, cosine]]))


def half_order():
    return np.arange(BLOCKS // 2).reshape(8, 4, 8).transpose(1, 0, 2).reshape(-1)


def block_table():
    n = half_order()
    angle = 4 * np.pi * (n[:, None] * n[None, :] % (BLOCKS // 2)) / BLOCKS
    return halves(np.concatenate([np.cos(angle), np.sin(angle)], 0) / math.sqrt(BLOCKS))


def twiddles():
    angle = 2 * np.pi * half_order()[:, None] / BLOCKS * np.ones((1, 128))
    sign = np.where(np.arange(128) < 64, 1.0, -1.0)
    return np.stack([np.cos(angle), np.sin(angle) * sign]).astype(np.float32)


def split(x):
    high = x.astype(BF16)
    return high, (x - high.astype(F32)).astype(BF16)


def dot3(a, b, dims):
    def one(u, v):
        return lax.dot_general(u, v, (dims, ((), ())), preferred_element_type=F32)

    rows = a[0].shape[0]
    top = one(jnp.concatenate(a, 0), b[0])
    return top[:rows] + (top[rows:] + one(a[0], b[1]))


def lane_block(shape, width):
    return lax.broadcasted_iota(jnp.int32, shape, len(shape) - 1) // width % 2


def swap_blocks(tiles):
    tiles = list(tiles)
    for bit in (1, 2, 4, 8):
        width = 8 * bit
        upper = lane_block(tiles[0].shape, width) == 1
        for i in range(16):
            if i & bit:
                continue
            a, b = tiles[i], tiles[i | bit]
            axis = a.ndim - 1
            tiles[i] = jnp.where(upper, pltpu.roll(b, width, axis), a)
            tiles[i | bit] = jnp.where(upper, b, pltpu.roll(a, 128 - width, axis))
    return tiles


def remote(src, dst, send, recv, **where):
    return pltpu.make_async_remote_copy(
        src_ref=src,
        dst_ref=dst,
        send_sem=send,
        recv_sem=recv,
        device_id=where,
        device_id_type=pl.DeviceIdType.MESH,
    )


def ring(d):
    return min(d, 4 - d)


OWNERS = sorted(
    ((d, y, c) for d in range(2) for y in range(4) for c in range(2) if d + y + c),
    key=lambda step: -(2 * step[0] + ring(step[1])),
)
PLANE = sorted(
    ((d, y, lo) for d in range(2) for y in range(4) for lo in range(2) if d + y + lo),
    key=lambda step: -(ring(2 * step[0] + step[2]) + ring(step[1])),
)


def phase_rows(bins_ref, offsets_ref, first):
    row = lax.broadcasted_iota(jnp.int32, (ALPHAS, ALPHAS), 0)
    same = row == lax.broadcasted_iota(jnp.int32, (ALPHAS, ALPHAS), 1)

    def column(ref):
        return jnp.sum(jnp.where(same, ref[...].astype(F32), 0.0), 1, keepdims=True)

    lane = lax.broadcasted_iota(jnp.int32, (ALPHAS, 256), 1)
    turns = column(bins_ref).astype(jnp.int32) * (first + lane // 8) % BLOCKS
    angle = turns.astype(F32) * (2.0 * math.pi / BLOCKS)
    chosen = column(offsets_ref).astype(jnp.int32) == lane % 8
    both = [jnp.where(chosen, f(angle) * (1.0 / 256.0), 0.0) for f in (jnp.cos, jnp.sin)]
    return split(jnp.concatenate(both, 0))


def kernel(
    x_hbm, bins_hbm, offsets_hbm, ctable_hbm, table_hbm, twiddle_hbm, out_ref,
    bins_ref, offsets_ref, x_ref, ctable_ref, table_ref, twiddle_ref, mid_ref, made_ref, got_ref, back_ref, land_ref,
    right_ref, other_ref, phase_ref, high_ref, low_ref, high2_ref, low2_ref, left_ref,
    part_ref, pair_ref, sum_ref, all_ref, part2_ref, pair2_ref, sum2_ref, all2_ref, res_ref, late_ref,
    load_sem, send1, recv1, send2, recv2, sendx, recvx, sendf, recvf, sendz, recvz,
    sendp, recvp, sends, recvs,
):
    chan, x, z = lax.axis_index("chan"), lax.axis_index("x"), lax.axis_index("z")
    core, place = lax.rem(chan, 2), chan // 2
    mate = chan + 1 - 2 * core
    after, before = lax.rem(x + 1, 4), lax.rem(x + 3, 4)

    loads = [
        pltpu.make_async_copy(src, dst, load_sem.at[i])
        for i, (src, dst) in enumerate(
            [
                (x_hbm, x_ref),
                (ctable_hbm, ctable_ref),
                (table_hbm, table_ref),
                (bins_hbm, bins_ref),
                (offsets_hbm, offsets_ref),
                (twiddle_hbm, twiddle_ref),
            ]
        )
    ]
    for load in loads:
        load.start()

    barrier = pltpu.get_barrier_semaphore()
    peers = [{"chan": lax.rem(chan + o, 16)} for o in range(1, 16)]
    peers += [{"x": after}, {"x": before}]
    peers += [{"z": 1 - z}]
    for where in peers:
        pl.semaphore_signal(barrier, device_id=where, device_id_type=pl.DeviceIdType.MESH)

    loads[0].wait()
    loads[1].wait()
    both = jnp.concatenate([x_ref[0].reshape(512, 128), x_ref[1].reshape(512, 128)], 1)
    mid_ref[...] = dot3(split(both), (ctable_ref[0], ctable_ref[1]), ((1,), (0,)))
    def tiles_of(h):
        for mc in range(4):
            tiles = [
                mid_ref[s * 32 + mc * 8 : s * 32 + mc * 8 + 8, c * 128 : c * 128 + 128]
                for c in range(2)
                for s in range(h * 8, h * 8 + 8)
            ]
            for dest, tile in enumerate(swap_blocks(tiles)):
                made_ref[h, dest, mc] = tile

    def owner(d, y, c):
        return lax.rem(place + d * 4, 8) // 4 * 8 + lax.rem(lax.rem(place, 4) + y, 4) * 2 + (core + c) % 2

    def exchange(src, dst, send, recv, step):
        peer = owner(*step)
        return remote(src.at[peer], dst.at[chan], send, recv, chan=peer)

    def everyone(src, dst, send, recv):
        most = pl.ds(0, 15)
        return remote(src.at[most], dst.at[most], send, recv, chan=mate)

    def first(h):
        return made_ref.at[h], got_ref.at[h], send1.at[h], recv1.at[h]

    def second(h, part):
        return back_ref.at[h, part], land_ref.at[h, part], send2.at[h, part], recv2.at[h, part]

    def send_all(group):
        for step in OWNERS:
            exchange(*group, step).start()

    tiles_of(0)
    pl.semaphore_wait(barrier, len(peers))
    send_all(first(0))
    tiles_of(1)
    everyone(*first(0)).wait_send()
    send_all(first(1))
    for h in range(2):
        got_ref[h, chan] = made_ref[h, chan]
    for load in loads[2:]:
        load.wait()
    phase_ref[0], phase_ref[1] = phase_rows(bins_ref, offsets_ref, chan * 32)

    first_part = lax.broadcasted_iota(jnp.int32, (BLOCKS // 2, 256), 1) % 128 < 64

    def turned(u):
        return jnp.concatenate([pltpu.roll(u[:, i : i + 128], 64, 1) for i in (0, 128)], 1)

    def transform(v):
        u = dot3((table_ref[0], table_ref[1]), split(v), ((1,), (0,)))
        return u[:256], turned(u[256:])

    for h in range(2):
        everyone(*first(h)).wait_recv()
        if h:
            everyone(*second(0, 0)).wait_send()
            send_all(second(0, 1))
        low, high = (
            jnp.concatenate([got_ref[h, i : i + 8, mc].reshape(64, 128) for mc in range(4)], 0)
            for i in (0, 8)
        )
        odd = low - high
        odd = odd * twiddle_ref[0] + pltpu.roll(odd, 64, 1) * twiddle_ref[1]
        cosine, sine = transform(jnp.concatenate([low + high, odd], 1))
        spectra = cosine + jnp.where(first_part, sine, -sine)
        power = spectra * spectra
        power = power + turned(power)
        cosine, sine = transform(spectra / jnp.sqrt(power + FLOOR))
        blocks = cosine - jnp.where(first_part, sine, -sine)
        even, odd = blocks[:, :128], blocks[:, 128:]
        odd = odd * twiddle_ref[0] - pltpu.roll(odd, 64, 1) * twiddle_ref[1]
        for i, half in ((0, even + odd), (8, even - odd)):
            for mc in range(4):
                rows = half[mc * 64 : mc * 64 + 64].reshape(8, 8, 128)
                back_ref[h, mc // 2, i : i + 8, mc % 2] = rows
        for part in range(2):
            land_ref[h, part, chan] = back_ref[h, part, chan]
        send_all(second(h, 0))
        if h:
            send_all(second(1, 1))

    def eight(i, mc, h):
        return right_ref.at[i, mc, pl.ds(h * 8, 8)]

    def to_x(h, mc, way):
        peer = (after, before)[way]
        return remote(
            eight(x, mc, h), eight(x, mc, h), sendx, recvx.at[h, mc], x=peer
        )

    def passed(h, mc, way):
        source, peer = (before, after) if way == 0 else (after, before)
        four = pl.ds(h * 8 + way * 4, 4)
        return remote(
            right_ref.at[source, mc, four], right_ref.at[source, mc, four],
            sendf, recvf.at[mc], x=peer,
        )

    def to_z(h, mc):
        return remote(
            eight(x, mc, h), other_ref.at[mc, pl.ds(h * 8, 8)], sendz, recvz.at[mc], z=1 - z
        )

    def turn(h, mc):
        tiles = swap_blocks([land_ref[h, mc // 2, i, mc % 2] for i in range(16)])
        for i, tile in enumerate(tiles):
            right_ref[x, mc, h * 8 + i % 8, i // 8] = tile
        to_x(h, mc, 0).start()
        to_x(h, mc, 1).start()
        to_z(h, mc).start()

    def whole(count, send, recv):
        some = right_ref.at[0, pl.ds(0, count)] if count <= 4 else right_ref.at[pl.ds(0, count // 4)]
        return remote(some, some, send, recv, x=after)

    def forward(h, mc):
        whole(1, sendx, recvx.at[h, mc]).wait_recv()
        for way in range(2):
            passed(h, mc, way).start()

    far = lax.rem(x + 2, 4)

    def shifted(mc, r):
        left = []
        for c in range(2):
            rows = []
            for a in range(32):
                if a < 16:
                    row = right_ref[x, mc, a, c, pl.ds(r, 1), :]
                else:
                    row = other_ref[mc, a - 16, c, pl.ds(r, 1), :]
                rows.append(pltpu.roll(jnp.broadcast_to(row, (8, 128)), 0, 1, stride=1, stride_axis=0))
            left.append(jnp.concatenate(rows, 0))
        return split(jnp.concatenate(left, 1))

    def facing(i, mc, r):
        tall = right_ref.at[i, mc].reshape(256, 128)
        real, imag = (tall[pl.ds(r + c * 8, 16, stride=16), :] for c in range(2))
        return [jnp.concatenate([real, imag], 1), jnp.concatenate([-imag, real], 1)]

    def product(mc, r, part):
        m = mc * 8 + r
        if part == 0:
            left = shifted(mc, r)
            left_ref[0, m], left_ref[1, m] = left
            rows = []
            for i in range(4):
                rows += facing(jnp.where(far == i, x, i), mc, r)
        else:
            left = left_ref[0, m], left_ref[1, m]
            rows = facing(far, mc, r)
        right = split(jnp.concatenate(rows, 0))
        if part:
            right = [jnp.concatenate([half] * 4, 0) for half in right]
        out = dot3(left, right, ((1,), (1,)))
        if part == 0:
            return out.reshape(32, 8, 128)
        out = out.reshape(8, 4, 8, 128)
        group = lax.broadcasted_iota(jnp.int32, (8, 8, 128), 2) // 32
        tiles = out[:, 3]
        for i in range(3):
            tiles = jnp.where(group == i, out[:, i], tiles)
        return tiles

    def products(mc, part, high_ref, low_ref):
        def step(i, carry):
            for half in range(2):
                r = i * 4 + half * 2
                tiles = jnp.concatenate([product(mc, r, part), product(mc, r + 1, part)], 1)
                rows = pl.ds(pl.multiple_of(mc * 64 + r * 8, 16), 16)
                high_ref[:, rows, :], low_ref[:, rows, :] = split(tiles)
            return carry

        lax.fori_loop(0, 2, step, 0)

    for h in range(2):
        for mc in range(4):
            if mc % 2 == 0:
                everyone(*second(h, mc // 2)).wait_recv()
            turn(h, mc)
    @pl.loop(0, 4)
    def _(mc):
        for h in range(2):
            forward(h, mc)
        whole(1, sendz, recvz.at[mc]).wait_recv()
        products(mc, 0, high_ref, low_ref)

    low_rows = lax.broadcasted_iota(jnp.int32, (8, 128), 0) < 4

    def one_pair(refs, out_ref, half, pair):
        a = half * (refs[0].shape[0] // 2) + pair * 2
        both = tuple(jnp.concatenate([ref[a], ref[a + 1]], 1) for ref in refs)
        t = dot3((phase_ref[0], phase_ref[1]), both, ((1,), (0,)))
        gs = []
        for i in range(2):
            cosine, sine = t[:64, i * 128 : i * 128 + 128], t[64:, i * 128 : i * 128 + 128]
            odd = lane_block(sine.shape, 16) == 1
            gs.append(cosine + jnp.where(odd, -pltpu.roll(sine, 16, 1), pltpu.roll(sine, 112, 1)))
        row = pl.ds(pair * 8, 8)
        for t8 in range(8):
            a0, a1 = (g[t8 * 8 : t8 * 8 + 8] for g in gs)
            out_ref[0, half, t8, row, :] = jnp.where(low_rows, a0, pltpu.roll(a1, 4, 0))
            out_ref[1, half, t8, row, :] = jnp.where(low_rows, pltpu.roll(a0, 4, 0), a1)

    def to_mate(part, half):
        return remote(
            parts[part].at[1 - core, half], pairs[part].at[half],
            sendp.at[part, half], recvp.at[part, half], chan=mate,
        )

    def last(part):
        return sums[part], alls[part], sends.at[part], recvs.at[part]

    def spread(part, d, y, lo):
        peer_z, peer = (z + lo) % 2, owner(d, y, 0) // 2
        src, dst, send, recv = last(part)
        return remote(
            src.at[lo * 8 + peer], dst.at[z * 8 + place], send, recv,
            z=peer_z, chan=peer * 2 + core,
        )

    def add_and_send(part, half):
        to_mate(part, half).wait_recv()
        sums[part][half * 8 : half * 8 + 8] = parts[part][core, half] + pairs[part][half]

        for step in PLANE:
            if step[2] == half:
                spread(part, *step).start()

        if not half:
            alls[part][z * 8 + place] = sums[part][place]

    parts, pairs = (part_ref, part2_ref), (pair_ref, pair2_ref)
    sums, alls = (sum_ref, sum2_ref), (all_ref, all2_ref)
    for half in (1, 0):
        for pair in range(8):
            one_pair((high_ref, low_ref), part_ref, half, pair)
        to_mate(0, half).start()
    def late_products(mc):
        whole(1, sendf, recvf.at[mc]).wait_recv()
        products(mc, 1, high2_ref, low2_ref)

    @pl.loop(0, 1)
    def _(mc):
        late_products(mc)

    for half in (1, 0):
        add_and_send(0, half)

    @pl.loop(1, 4)
    def _(mc):
        late_products(mc)

    for half in (1, 0):
        for pair in range(2):
            one_pair((high2_ref, low2_ref), part2_ref, half, pair)
        to_mate(1, half).start()
    for half in (1, 0):
        add_and_send(1, half)

    for group in (first(1), second(0, 1), second(1, 0), second(1, 1), last(0)):
        everyone(*group).wait_send()
    whole(8, sendx, recvx.at[0, 0]).wait_send()
    whole(4, sendf, recvf.at[0]).wait_send()
    whole(4, sendz, recvz.at[0]).wait_send()
    for part in range(2):
        for half in range(2):
            to_mate(part, half).wait_send()
    everyone(*last(0)).wait_recv()
    for h in range(2):
        res_ref[h] = jnp.sum(all_ref[h * 8 : h * 8 + 8], axis=0)
    everyone(*last(1)).wait_recv()
    for h in range(2):
        late = jnp.sum(all2_ref[h * 8 : h * 8 + 8], axis=0)
        for i in range(4):
            there = pltpu.roll(late, lax.rem(far + 4 - i, 4) * 32, 1)
            for g in range(4):
                late_ref[h, g * 16 + i * 4 : g * 16 + i * 4 + 4] = there[g * 4 : g * 4 + 4]
    missing = lax.broadcasted_iota(jnp.int32, (64, 128), 1) // 32 == far
    lo, hi = (jnp.where(missing, late_ref[h], res_ref[h]) for h in range(2))
    odd = lane_block(lo.shape, 16) == 1
    res_ref[0] = jnp.where(odd, pltpu.roll(hi, 16, 1), lo)
    res_ref[1] = jnp.where(odd, hi, pltpu.roll(lo, 112, 1))
    for j in range(4):
        for c in range(2):
            out_ref[j, c] = res_ref[c, pl.ds(j, 16, stride=4), :]

    everyone(*last(1)).wait_send()


DMA = pltpu.SemaphoreType.DMA


def summed(rows):
    shapes = [(2, 2, 8), (2, 8), (16,), (16,)]
    return [pltpu.VMEM((*shape, rows, 128), F32) for shape in shapes]


def on_device(samples, bins, offsets):
    chunk = pltpu.VMEM((2, 16, 4, 8, 128), F32)
    pieces = pltpu.VMEM((2, 2, 16, 2, 8, 128), F32)
    sixteen = pltpu.VMEM((16, 64, 128), F32)
    given = [
        samples, bins.reshape(1, -1), offsets.reshape(1, -1),
        jnp.asarray(channel_table()), jnp.asarray(block_table()), jnp.asarray(twiddles()),
    ]
    return pl.pallas_call(
        kernel,
        out_shape=jax.ShapeDtypeStruct((4, 2, 16, 128), F32),
        in_specs=[HBM] * 6,
        out_specs=VMEM,
        scratch_shapes=[
            pltpu.VMEM((1, ALPHAS), jnp.int32),
            pltpu.VMEM((1, ALPHAS), jnp.int32),
            pltpu.VMEM((2, 16, 32, 128), F32),
            pltpu.VMEM((2, 256, 256), BF16),
            pltpu.VMEM((2, BLOCKS, BLOCKS // 2), BF16),
            pltpu.VMEM((2, BLOCKS // 2, 128), F32),
            pltpu.VMEM((512, 256), F32),
            chunk, chunk, pieces, pieces,
            pltpu.VMEM((4, 4, 16, 2, 8, 128), F32),
            pltpu.VMEM((4, 16, 2, 8, 128), F32),
            pltpu.VMEM((2, 128, 256), BF16),
            pltpu.VMEM((32, 256, 128), BF16),
            pltpu.VMEM((32, 256, 128), BF16),
            pltpu.VMEM((8, 256, 128), BF16),
            pltpu.VMEM((8, 256, 128), BF16),
            pltpu.VMEM((2, 32, 256, 256), BF16),
            *summed(64),
            *summed(16),
            pltpu.VMEM((2, 64, 128), F32),
            pltpu.VMEM((2, 64, 128), F32),
            DMA((6,)), DMA((2,)), DMA((2,)), DMA((2, 2)), DMA((2, 2)),
            DMA, DMA((2, 4)), DMA, DMA((4,)), DMA, DMA((4,)),
            DMA((2, 2)), DMA((2, 2)), DMA((2,)), DMA((2,)),
        ],
        compiler_params=pltpu.CompilerParams(
            vmem_limit_bytes=40 * 2**20, collective_id=0, has_side_effects=True
        ),
        name="coherence",
    )(*(pltpu.with_memory_space_constraint(v, pltpu.HBM) for v in given))


def solution(mesh):
    finer = Mesh(mesh.devices.reshape(4, 2, mesh.shape["chan"]), ("x", "z", "chan"))
    sensor = ("x", "z")
    return jax.shard_map(
        on_device,
        mesh=finer,
        in_specs=(P(None, sensor, "chan", None), P(), P()),
        out_specs=P("chan", None, sensor, None),
        check_vma=False,
    )
```

```python
import math

import jax
import jax.numpy as jnp
import ml_dtypes
import numpy as np
from jax import lax
from jax.experimental import pallas as pl
from jax.experimental.pallas import tpu as pltpu
from jax.sharding import Mesh
from jax.sharding import PartitionSpec as P

CHANNELS = 128
BLOCKS = 512
ALPHAS = 64
SHIFTS = 8
FLOOR = 0.1
F32 = jnp.float32
BF16 = jnp.bfloat16
VMEM = pl.BlockSpec(memory_space=pltpu.VMEM)
HBM = pl.BlockSpec(memory_space=pltpu.HBM)


def halves(table):
    high = table.astype(ml_dtypes.bfloat16)
    low = (table - high.astype(np.float64)).astype(ml_dtypes.bfloat16)
    return np.stack([high, low])


def channel_table():
    n = np.arange(CHANNELS)
    window = 0.5 - 0.5 * np.cos(2 * np.pi * n / CHANNELS)
    angle = 2 * np.pi * (n[:, None] * n[None, :] % CHANNELS) / CHANNELS
    cosine = window[:, None] * np.cos(angle) / math.sqrt(CHANNELS)
    sine = window[:, None] * np.sin(angle) / math.sqrt(CHANNELS)
    return halves(np.block([[cosine, -sine], [sine, cosine]]))


def half_order():
    return np.arange(BLOCKS // 2).reshape(8, 4, 8).transpose(1, 0, 2).reshape(-1)


def block_table():
    n = half_order()
    angle = 4 * np.pi * (n[:, None] * n[None, :] % (BLOCKS // 2)) / BLOCKS
    return halves(np.concatenate([np.cos(angle), np.sin(angle)], 0) / math.sqrt(BLOCKS))


def twiddles():
    angle = 2 * np.pi * half_order()[:, None] / BLOCKS * np.ones((1, 128))
    sign = np.where(np.arange(128) < 64, 1.0, -1.0)
    return np.stack([np.cos(angle), np.sin(angle) * sign]).astype(np.float32)


def split(x):
    high = x.astype(BF16)
    return high, (x - high.astype(F32)).astype(BF16)


def dot3(a, b, dims):
    def one(u, v):
        return lax.dot_general(u, v, (dims, ((), ())), preferred_element_type=F32)

    rows = a[0].shape[0]
    top = one(jnp.concatenate(a, 0), b[0])
    return top[:rows] + (top[rows:] + one(a[0], b[1]))


def lane_block(shape, width):
    return lax.broadcasted_iota(jnp.int32, shape, len(shape) - 1) // width % 2


def swap_blocks(tiles):
    tiles = list(tiles)
    for bit in (1, 2, 4, 8):
        width = 8 * bit
        upper = lane_block(tiles[0].shape, width) == 1
        for i in range(16):
            if i & bit:
                continue
            a, b = tiles[i], tiles[i | bit]
            axis = a.ndim - 1
            tiles[i] = jnp.where(upper, pltpu.roll(b, width, axis), a)
            tiles[i | bit] = jnp.where(upper, b, pltpu.roll(a, 128 - width, axis))
    return tiles


def remote(src, dst, send, recv, **where):
    return pltpu.make_async_remote_copy(
        src_ref=src,
        dst_ref=dst,
        send_sem=send,
        recv_sem=recv,
        device_id=where,
        device_id_type=pl.DeviceIdType.MESH,
    )


def ring(d):
    return min(d, 4 - d)


OWNERS = sorted(
    ((d, y, c) for d in range(2) for y in range(4) for c in range(2) if d + y + c),
    key=lambda step: -(2 * step[0] + ring(step[1])),
)
PLANE = sorted(
    ((d, y, lo) for d in range(2) for y in range(4) for lo in range(2) if d + y + lo),
    key=lambda step: -(ring(2 * step[0] + step[2]) + ring(step[1])),
)


def phase_rows(bins_ref, offsets_ref, first):
    row = lax.broadcasted_iota(jnp.int32, (ALPHAS, ALPHAS), 0)
    same = row == lax.broadcasted_iota(jnp.int32, (ALPHAS, ALPHAS), 1)

    def column(ref):
        return jnp.sum(jnp.where(same, ref[...].astype(F32), 0.0), 1, keepdims=True)

    lane = lax.broadcasted_iota(jnp.int32, (ALPHAS, 256), 1)
    turns = column(bins_ref).astype(jnp.int32) * (first + lane // 8) % BLOCKS
    angle = turns.astype(F32) * (2.0 * math.pi / BLOCKS)
    chosen = column(offsets_ref).astype(jnp.int32) == lane % 8
    both = [jnp.where(chosen, f(angle) * (1.0 / 256.0), 0.0) for f in (jnp.cos, jnp.sin)]
    return split(jnp.concatenate(both, 0))


def kernel(
    x_hbm, bins_hbm, offsets_hbm, ctable_hbm, table_hbm, twiddle_hbm, out_ref,
    bins_ref, offsets_ref, x_ref, ctable_ref, table_ref, twiddle_ref, mid_ref, made_ref, got_ref, back_ref, land_ref,
    right_ref, other_ref, phase_ref, high_ref, low_ref, high2_ref, low2_ref, left_ref,
    part_ref, pair_ref, sum_ref, all_ref, part2_ref, pair2_ref, sum2_ref, all2_ref, res_ref, late_ref,
    load_sem, send1, recv1, send2, recv2, sendx, recvx, sendf, recvf, sendz, recvz,
    sendp, recvp, sends, recvs,
):
    chan, x, z = lax.axis_index("chan"), lax.axis_index("x"), lax.axis_index("z")
    core, place = lax.rem(chan, 2), chan // 2
    mate = chan + 1 - 2 * core
    after, before = lax.rem(x + 1, 4), lax.rem(x + 3, 4)

    loads = [
        pltpu.make_async_copy(src, dst, load_sem.at[i])
        for i, (src, dst) in enumerate(
            [
                (x_hbm, x_ref),
                (ctable_hbm, ctable_ref),
                (table_hbm, table_ref),
                (bins_hbm, bins_ref),
                (offsets_hbm, offsets_ref),
                (twiddle_hbm, twiddle_ref),
            ]
        )
    ]
    for load in loads:
        load.start()

    barrier = pltpu.get_barrier_semaphore()
    def owner(d, y, c):
        return lax.rem(place + d * 4, 8) // 4 * 8 + lax.rem(lax.rem(place, 4) + y, 4) * 2 + (core + c) % 2

    peers = [{"chan": owner(*step)} for step in OWNERS]
    peers += [{"x": after}, {"x": before}]
    peers += [{"z": 1 - z}]
    for where in peers:
        pl.semaphore_signal(barrier, device_id=where, device_id_type=pl.DeviceIdType.MESH)

    loads[0].wait()
    loads[1].wait()
    def demodulate(h):
        both = jnp.concatenate(
            [x_ref[c, h * 8 : h * 8 + 8].reshape(256, 128) for c in range(2)], 1
        )
        table = (ctable_ref[0], ctable_ref[1])
        mid_ref[h * 256 : h * 256 + 256] = dot3(split(both), table, ((1,), (0,)))

    def tiles_of(h):
        for mc in range(4):
            tiles = [
                mid_ref[s * 32 + mc * 8 : s * 32 + mc * 8 + 8, c * 128 : c * 128 + 128]
                for c in range(2)
                for s in range(h * 8, h * 8 + 8)
            ]
            for dest, tile in enumerate(swap_blocks(tiles)):
                made_ref[h, dest, mc] = tile

    def exchange(src, dst, send, recv, step):
        peer = owner(*step)
        return remote(src.at[peer], dst.at[chan], send, recv, chan=peer)

    def everyone(src, dst, send, recv):
        most = pl.ds(0, 15)
        return remote(src.at[most], dst.at[most], send, recv, chan=mate)

    def first(h):
        return made_ref.at[h], got_ref.at[h], send1.at[h], recv1.at[h]

    def second(h, part):
        return back_ref.at[h, part], land_ref.at[h, part], send2.at[h, part], recv2.at[h, part]

    def send_all(group):
        for step in OWNERS:
            exchange(*group, step).start()

    demodulate(0)
    tiles_of(0)
    pl.semaphore_wait(barrier, len(peers))
    send_all(first(0))
    demodulate(1)
    tiles_of(1)
    everyone(*first(0)).wait_send()
    send_all(first(1))
    for h in range(2):
        got_ref[h, chan] = made_ref[h, chan]
    for load in loads[2:]:
        load.wait()
    phase_ref[0], phase_ref[1] = phase_rows(bins_ref, offsets_ref, chan * 32)

    first_part = lax.broadcasted_iota(jnp.int32, (BLOCKS // 2, 256), 1) % 128 < 64

    def turned(u):
        return jnp.concatenate([pltpu.roll(u[:, i : i + 128], 64, 1) for i in (0, 128)], 1)

    def transform(v):
        u = dot3((table_ref[0], table_ref[1]), split(v), ((1,), (0,)))
        return u[:256], turned(u[256:])

    for h in range(2):
        everyone(*first(h)).wait_recv()
        if h:
            everyone(*second(0, 0)).wait_send()
            send_all(second(0, 1))
        low, high = (
            jnp.concatenate([got_ref[h, i : i + 8, mc].reshape(64, 128) for mc in range(4)], 0)
            for i in (0, 8)
        )
        odd = low - high
        odd = odd * twiddle_ref[0] + pltpu.roll(odd, 64, 1) * twiddle_ref[1]
        cosine, sine = transform(jnp.concatenate([low + high, odd], 1))
        spectra = cosine + jnp.where(first_part, sine, -sine)
        power = spectra * spectra
        power = power + turned(power)
        cosine, sine = transform(spectra / jnp.sqrt(power + FLOOR))
        blocks = cosine - jnp.where(first_part, sine, -sine)
        even, odd = blocks[:, :128], blocks[:, 128:]
        odd = odd * twiddle_ref[0] - pltpu.roll(odd, 64, 1) * twiddle_ref[1]
        for i, half in ((0, even + odd), (8, even - odd)):
            for mc in range(4):
                rows = half[mc * 64 : mc * 64 + 64].reshape(8, 8, 128)
                back_ref[h, mc // 2, i : i + 8, mc % 2] = rows
        for part in range(2):
            land_ref[h, part, chan] = back_ref[h, part, chan]
        send_all(second(h, 0))
        if h:
            send_all(second(1, 1))

    def eight(i, mc, h):
        return right_ref.at[i, mc, pl.ds(h * 8, 8)]

    def to_x(h, mc, way):
        peer = (after, before)[way]
        return remote(
            eight(x, mc, h), eight(x, mc, h), sendx, recvx.at[h, mc], x=peer
        )

    def passed(h, mc, way):
        source, peer = (before, after) if way == 0 else (after, before)
        four = pl.ds(h * 8 + way * 4, 4)
        return remote(
            right_ref.at[source, mc, four], right_ref.at[source, mc, four],
            sendf, recvf.at[mc], x=peer,
        )

    def to_z(h, mc):
        return remote(
            eight(x, mc, h), other_ref.at[mc, pl.ds(h * 8, 8)], sendz, recvz.at[mc], z=1 - z
        )

    def turn(h, mc):
        tiles = swap_blocks([land_ref[h, mc // 2, i, mc % 2] for i in range(16)])
        for i, tile in enumerate(tiles):
            right_ref[x, mc, h * 8 + i % 8, i // 8] = tile
        to_x(h, mc, 0).start()
        to_x(h, mc, 1).start()
        to_z(h, mc).start()

    def whole(count, send, recv):
        some = right_ref.at[0, pl.ds(0, count)] if count <= 4 else right_ref.at[pl.ds(0, count // 4)]
        return remote(some, some, send, recv, x=after)

    def forward(h, mc):
        whole(1, sendx, recvx.at[h, mc]).wait_recv()
        for way in range(2):
            passed(h, mc, way).start()

    far = lax.rem(x + 2, 4)

    def shifted(mc, r):
        left = []
        for c in range(2):
            rows = []
            for a in range(32):
                if a < 16:
                    row = right_ref[x, mc, a, c, pl.ds(r, 1), :]
                else:
                    row = other_ref[mc, a - 16, c, pl.ds(r, 1), :]
                rows.append(pltpu.roll(jnp.broadcast_to(row, (8, 128)), 0, 1, stride=1, stride_axis=0))
            left.append(jnp.concatenate(rows, 0))
        return split(jnp.concatenate(left, 1))

    def facing(i, mc, r):
        tall = right_ref.at[i, mc].reshape(256, 128)
        real, imag = (tall[pl.ds(r + c * 8, 16, stride=16), :] for c in range(2))
        return [jnp.concatenate([real, imag], 1), jnp.concatenate([-imag, real], 1)]

    def product(mc, r, part):
        m = mc * 8 + r
        if part == 0:
            left = shifted(mc, r)
            left_ref[0, m], left_ref[1, m] = left
            rows = []
            for i in range(4):
                rows += facing(jnp.where(far == i, x, i), mc, r)
        else:
            left = left_ref[0, m], left_ref[1, m]
            rows = facing(far, mc, r)
        right = split(jnp.concatenate(rows, 0))
        if part:
            right = [jnp.concatenate([half] * 4, 0) for half in right]
        out = dot3(left, right, ((1,), (1,)))
        if part == 0:
            return out.reshape(32, 8, 128)
        out = out.reshape(8, 4, 8, 128)
        group = lax.broadcasted_iota(jnp.int32, (8, 8, 128), 2) // 32
        tiles = out[:, 3]
        for i in range(3):
            tiles = jnp.where(group == i, out[:, i], tiles)
        return tiles

    def products(mc, part, high_ref, low_ref):
        def step(i, carry):
            for half in range(2):
                r = i * 4 + half * 2
                tiles = jnp.concatenate([product(mc, r, part), product(mc, r + 1, part)], 1)
                rows = pl.ds(pl.multiple_of(mc * 64 + r * 8, 16), 16)
                high_ref[:, rows, :], low_ref[:, rows, :] = split(tiles)
            return carry

        lax.fori_loop(0, 2, step, 0)

    for h in range(2):
        for mc in range(4):
            if mc % 2 == 0:
                everyone(*second(h, mc // 2)).wait_recv()
            turn(h, mc)
    @pl.loop(0, 4)
    def _(mc):
        for h in range(2):
            forward(h, mc)
        whole(1, sendz, recvz.at[mc]).wait_recv()
        products(mc, 0, high_ref, low_ref)

    low_rows = lax.broadcasted_iota(jnp.int32, (8, 128), 0) < 4

    def one_pair(refs, out_ref, half, pair):
        a = half * (refs[0].shape[0] // 2) + pair * 2
        both = tuple(jnp.concatenate([ref[a], ref[a + 1]], 1) for ref in refs)
        t = dot3((phase_ref[0], phase_ref[1]), both, ((1,), (0,)))
        gs = []
        for i in range(2):
            cosine, sine = t[:64, i * 128 : i * 128 + 128], t[64:, i * 128 : i * 128 + 128]
            odd = lane_block(sine.shape, 16) == 1
            gs.append(cosine + jnp.where(odd, -pltpu.roll(sine, 16, 1), pltpu.roll(sine, 112, 1)))
        row = pl.ds(pair * 8, 8)
        for t8 in range(8):
            a0, a1 = (g[t8 * 8 : t8 * 8 + 8] for g in gs)
            out_ref[0, half, t8, row, :] = jnp.where(low_rows, a0, pltpu.roll(a1, 4, 0))
            out_ref[1, half, t8, row, :] = jnp.where(low_rows, pltpu.roll(a0, 4, 0), a1)

    def to_mate(part, half):
        return remote(
            parts[part].at[1 - core, half], pairs[part].at[half],
            sendp.at[part, half], recvp.at[part, half], chan=mate,
        )

    def last(part):
        return sums[part], alls[part], sends.at[part], recvs.at[part]

    def spread(part, d, y, lo):
        peer_z, peer = (z + lo) % 2, owner(d, y, 0) // 2
        src, dst, send, recv = last(part)
        return remote(
            src.at[lo * 8 + peer], dst.at[z * 8 + place], send, recv,
            z=peer_z, chan=peer * 2 + core,
        )

    def add_and_send(part, half):
        to_mate(part, half).wait_recv()
        sums[part][half * 8 : half * 8 + 8] = parts[part][core, half] + pairs[part][half]

        for step in PLANE:
            if step[2] == half:
                spread(part, *step).start()

        if not half:
            alls[part][z * 8 + place] = sums[part][place]

    parts, pairs = (part_ref, part2_ref), (pair_ref, pair2_ref)
    sums, alls = (sum_ref, sum2_ref), (all_ref, all2_ref)
    for half in range(2):
        for pair in range(8):
            one_pair((high_ref, low_ref), part_ref, half, pair)
        to_mate(0, half).start()
    def late_products(mc):
        whole(1, sendf, recvf.at[mc]).wait_recv()
        products(mc, 1, high2_ref, low2_ref)

    @pl.loop(0, 1)
    def _(mc):
        late_products(mc)

    for half in range(2):
        add_and_send(0, half)

    @pl.loop(1, 4)
    def _(mc):
        late_products(mc)

    for half in range(2):
        for pair in range(2):
            one_pair((high2_ref, low2_ref), part2_ref, half, pair)
        to_mate(1, half).start()
    for half in range(2):
        add_and_send(1, half)

    for group in (first(1), second(0, 1), second(1, 0), second(1, 1), last(0)):
        everyone(*group).wait_send()
    whole(8, sendx, recvx.at[0, 0]).wait_send()
    whole(4, sendf, recvf.at[0]).wait_send()
    whole(4, sendz, recvz.at[0]).wait_send()
    for part in range(2):
        for half in range(2):
            to_mate(part, half).wait_send()
    everyone(*last(0)).wait_recv()
    for h in range(2):
        res_ref[h] = jnp.sum(all_ref[h * 8 : h * 8 + 8], axis=0)
    everyone(*last(1)).wait_recv()
    for h in range(2):
        late = jnp.sum(all2_ref[h * 8 : h * 8 + 8], axis=0)
        for i in range(4):
            there = pltpu.roll(late, lax.rem(far + 4 - i, 4) * 32, 1)
            for g in range(4):
                late_ref[h, g * 16 + i * 4 : g * 16 + i * 4 + 4] = there[g * 4 : g * 4 + 4]
    missing = lax.broadcasted_iota(jnp.int32, (64, 128), 1) // 32 == far
    lo, hi = (jnp.where(missing, late_ref[h], res_ref[h]) for h in range(2))
    odd = lane_block(lo.shape, 16) == 1
    res_ref[0] = jnp.where(odd, pltpu.roll(hi, 16, 1), lo)
    res_ref[1] = jnp.where(odd, hi, pltpu.roll(lo, 112, 1))
    for j in range(4):
        for c in range(2):
            out_ref[j, c] = res_ref[c, pl.ds(j, 16, stride=4), :]

    everyone(*last(1)).wait_send()


DMA = pltpu.SemaphoreType.DMA


def summed(rows):
    shapes = [(2, 2, 8), (2, 8), (16,), (16,)]
    return [pltpu.VMEM((*shape, rows, 128), F32) for shape in shapes]


def on_device(samples, bins, offsets):
    chunk = pltpu.VMEM((2, 16, 4, 8, 128), F32)
    pieces = pltpu.VMEM((2, 2, 16, 2, 8, 128), F32)
    sixteen = pltpu.VMEM((16, 64, 128), F32)
    given = [
        samples, bins.reshape(1, -1), offsets.reshape(1, -1),
        jnp.asarray(channel_table()), jnp.asarray(block_table()), jnp.asarray(twiddles()),
    ]
    return pl.pallas_call(
        kernel,
        out_shape=jax.ShapeDtypeStruct((4, 2, 16, 128), F32),
        in_specs=[HBM] * 6,
        out_specs=VMEM,
        scratch_shapes=[
            pltpu.VMEM((1, ALPHAS), jnp.int32),
            pltpu.VMEM((1, ALPHAS), jnp.int32),
            pltpu.VMEM((2, 16, 32, 128), F32),
            pltpu.VMEM((2, 256, 256), BF16),
            pltpu.VMEM((2, BLOCKS, BLOCKS // 2), BF16),
            pltpu.VMEM((2, BLOCKS // 2, 128), F32),
            pltpu.VMEM((512, 256), F32),
            chunk, chunk, pieces, pieces,
            pltpu.VMEM((4, 4, 16, 2, 8, 128), F32),
            pltpu.VMEM((4, 16, 2, 8, 128), F32),
            pltpu.VMEM((2, 128, 256), BF16),
            pltpu.VMEM((32, 256, 128), BF16),
            pltpu.VMEM((32, 256, 128), BF16),
            pltpu.VMEM((8, 256, 128), BF16),
            pltpu.VMEM((8, 256, 128), BF16),
            pltpu.VMEM((2, 32, 256, 256), BF16),
            *summed(64),
            *summed(16),
            pltpu.VMEM((2, 64, 128), F32),
            pltpu.VMEM((2, 64, 128), F32),
            DMA((6,)), DMA((2,)), DMA((2,)), DMA((2, 2)), DMA((2, 2)),
            DMA, DMA((2, 4)), DMA, DMA((4,)), DMA, DMA((4,)),
            DMA((2, 2)), DMA((2, 2)), DMA((2,)), DMA((2,)),
        ],
        compiler_params=pltpu.CompilerParams(
            vmem_limit_bytes=40 * 2**20, collective_id=0, has_side_effects=True
        ),
        name="coherence",
    )(*(pltpu.with_memory_space_constraint(v, pltpu.HBM) for v in given))


def solution(mesh):
    finer = Mesh(mesh.devices.reshape(4, 2, mesh.shape["chan"]), ("x", "z", "chan"))
    sensor = ("x", "z")
    return jax.shard_map(
        on_device,
        mesh=finer,
        in_specs=(P(None, sensor, "chan", None), P(), P()),
        out_specs=P("chan", None, sensor, None),
        check_vma=False,
    )
```
